32 devices in a mesh: dp: 8 (over y, x, core), branch: 4 (over z).
Axes of the slice: x: 2, y: 2, z: 4, core: 2. Of those that a mesh axis runs over, the one named last changes fastest.
Arguments:
- tokens: bfloat16 [8192, 2048], P(('dp', 'branch')), may hold values from -6 to 6
- doc_ids: int32 [8192], P('dp'), may hold values from 0 to 15, as said below
- real_rows: int32 [8192], P('dp'), may hold values from 0 to 1, as said below
- cotangent: bfloat16 [8192, 2048], P(('dp', 'branch')), may hold values from -6 to 6
- norm_gain: float32 [2048], P(('dp', 'branch')), may hold values from 0.5 to 1.5
- norm_shift: float32 [2048], P(('dp', 'branch')), may hold values from -2 to 2
- out_bias: float32 [2048], P(('dp', 'branch')), may hold values from -2 to 2
- w_qkv: float32 [3, 2048, 2048], P(None, 'dp', 'branch'), may hold values from -0.125 to 0.125
- b_qkv: float32 [3, 32, 64], P(None, 'branch', 'dp'), may hold values from -3 to 3
- w_out: float32 [2048, 2048], P('branch', 'dp'), may hold values from -0.75 to 0.75
- w_up: float32 [2048, 8192], P('dp', 'branch'), may hold values from -0.125 to 0.125
- b_up: float32 [64, 128], P('branch', 'dp'), may hold values from -3 to 3
- w_down: float32 [8192, 2048], P('branch', 'dp'), may hold values from -0.0625 to 0.0625
Outputs:
- block_out: bfloat16 [8192, 2048], P(('dp', 'branch'))
- tokens_grad: bfloat16 [8192, 2048], P(('dp', 'branch'))
- norm_gain_grad: float32 [2048], P(('dp', 'branch'))
- norm_shift_grad: float32 [2048], P(('dp', 'branch'))
- out_bias_grad: float32 [2048], P(('dp', 'branch'))
- w_qkv_grad: float32 [3, 2048, 2048], P(None, 'dp', 'branch')
- b_qkv_grad: float32 [3, 32, 64], P(None, 'branch', 'dp')
- w_out_grad: float32 [2048, 2048], P('branch', 'dp')
- w_up_grad: float32 [2048, 8192], P('dp', 'branch')
- b_up_grad: float32 [64, 128], P('branch', 'dp')
- w_down_grad: float32 [8192, 2048], P('branch', 'dp')
The draws below stay inside these ranges and needn't reach their ends.
Inputs may be any that keep to these rules, and one draw needn't show every extreme that they name: `doc_ids`: within each aligned block of 1024 slots the ids start at 0 and never fall; a sequence has 64 times a power of two slots, up to 1024; some sequence has exactly 1024; all padding slots of a block share the id 1024 // 64 - 1, which real slots of a block with padding never take; the last block ends in padding. `real_rows`: within each block, the slots of whole sequences come first and are 1; the rest of the block is 0; every block holds a sequence; the last block ends in padding.
All inputs are finite; a program needn't handle non-finite values.
Results may differ from the reference program's by a relative error of at most 0.014.
Values may be sent and summed in bfloat16 or wider, within the bound.
A program may use at most 192 MiB of HBM per device.

```python
import math
import jax
import jax.numpy as jnp
from jax import lax

D = 2048
HEADS = 32
HEAD_DIM = 64
ROT = 32
FF = 8192
UNIT_COLS = 128
TOK_DEV = 1024
MIN_LEN = 64
LEVELS = 5
LONGEST = 1024
TOKENS = 8192


def seq_layout(key):
    blocks_all = TOKENS // TOK_DEV
    most_seqs = TOK_DEV // MIN_LEN
    first_key, second_key = jax.random.split(jax.random.fold_in(key, 11))
    level_one = jax.random.randint(first_key, (blocks_all, most_seqs), 0, LEVELS, dtype=jnp.int32)
    level_two = jax.random.randint(second_key, (blocks_all, most_seqs), 0, LEVELS, dtype=jnp.int32)
    levels_min = jnp.minimum(level_one, level_two)
    lengths = MIN_LEN * jnp.left_shift(jnp.ones_like(levels_min), levels_min)
    lengths = lengths.at[0, 0].set(LONGEST)
    last_row = jnp.full((most_seqs,), LONGEST, dtype=jnp.int32).at[0].set(MIN_LEN)
    lengths = lengths.at[blocks_all - 1].set(last_row)
    seq_ends = jnp.cumsum(lengths, axis=1).astype(jnp.int32)
    row_index = jnp.arange(TOK_DEV, dtype=jnp.int32)
    doc_rows = jnp.sum((seq_ends[:, None, :] <= row_index[None, :, None]).astype(jnp.int32), axis=-1).astype(jnp.int32)
    doc_end = jnp.take_along_axis(seq_ends, doc_rows, axis=1)
    real_mask = (doc_end <= TOK_DEV).astype(jnp.int32)
    doc_rows = jnp.where(real_mask == 1, doc_rows, jnp.full_like(doc_rows, most_seqs - 1))
    return (doc_rows.reshape(TOKENS), real_mask.reshape(TOKENS))


def draw_doc_ids(key, part):
    return seq_layout(key)[0]


def draw_real_rows(key, part):
    return seq_layout(key)[1]


def with_spikes(entries, rng, source, target, blocks, factor):
    owner, partner = [(jnp.arange(entries.shape[axis_at]) // (entries.shape[axis_at] // blocks)).reshape([-1 if axis == axis_at else 1 for axis in range(entries.ndim)]) for axis_at in (source, target)]
    chosen = jax.random.permutation(rng, blocks)[partner]
    strong = (owner == chosen) | (owner == (partner + blocks // 2) % blocks)
    return jnp.where(strong, factor * entries, entries)


def block_levels(stream_key, extent, cuts, smallest, top_value):
    gain, own = 1.0, jax.random.fold_in(stream_key, 6)
    for position, parts in cuts:
        steps = jnp.exp(jax.random.uniform(jax.random.fold_in(own, position), (parts,), jnp.float32, smallest / len(cuts), top_value / len(cuts)))
        gain = gain * jnp.repeat(steps, extent[position] // parts).reshape([-1 if axis == position else 1 for axis in range(len(extent))])
    return gain


def normal_values(stream_key, extent, width, bound, cuts=(), kind=jnp.bfloat16):
    level = block_levels(stream_key, extent, cuts, -0.22, 0.18) if cuts else 1.0
    drawn = jax.random.normal(stream_key, extent, jnp.float32) * width * level
    return jnp.minimum(jnp.maximum(drawn, -bound), bound).astype(kind)


def gaussian_with(own_key, shape, width, reach, cuts, heavy, kind=jnp.bfloat16):
    result = width * jax.random.normal(own_key, shape, jnp.float32)
    if cuts:
        result = result * block_levels(own_key, shape, cuts, -0.22, 0.18)
    return jnp.clip(with_spikes(result, jax.random.fold_in(own_key, 3), *heavy), -reach, reach).astype(kind)


def setup_inputs(seed: int = 0) -> dict:
    keys = jax.random.split(jax.random.key(seed), 14)
    tokens = normal_values(keys[0], (TOKENS, D), 1.0, 6.0, ((0, 32),))
    doc_ids = draw_doc_ids(jax.random.fold_in(keys[13], 71), 0)
    real_rows = draw_real_rows(jax.random.fold_in(keys[13], 71), 0)
    cotangent = gaussian_with(keys[3], (TOKENS, D), 1.0, 6.0, ((0, 32),), (0, 1, 32, 2.75))
    norm_gain = jnp.clip(1.0 + 0.1 * jax.random.normal(keys[4], (D,), jnp.float32), 0.5, 1.5)
    norm_shift = normal_values(keys[5], (D,), 0.3, 2.0, ((0, 32),), jnp.float32)
    out_bias = normal_values(keys[6], (D,), 0.3, 2.0, ((0, 32),), jnp.float32)
    w_qkv = normal_values(keys[7], (3, D, D), D ** -0.5, 0.125, ((1, 8), (2, 4)), jnp.float32)
    b_qkv = normal_values(keys[8], (3, HEADS, HEAD_DIM), 0.5, 3.0, ((1, 4), (2, 8)), jnp.float32)
    w_out = normal_values(keys[9], (D, D), (D // 32) ** -0.5, 0.75, ((0, 4), (1, 8)), jnp.float32)
    w_up = normal_values(keys[10], (D, FF), D ** -0.5, 0.125, ((0, 8), (1, 4)), jnp.float32)
    b_up = normal_values(keys[11], (FF // UNIT_COLS, UNIT_COLS), 0.5, 3.0, ((0, 4), (1, 8)), jnp.float32)
    w_down = normal_values(keys[12], (FF, D), FF ** -0.5, 0.0625, ((0, 4), (1, 8)), jnp.float32)
    return {"tokens": tokens, "doc_ids": doc_ids, "real_rows": real_rows, "cotangent": cotangent, "norm_gain": norm_gain, "norm_shift": norm_shift, "out_bias": out_bias, "w_qkv": w_qkv, "b_qkv": b_qkv, "w_out": w_out, "w_up": w_up, "b_up": b_up, "w_down": w_down}


@jax.custom_vjp
def low(v):
    return lax.optimization_barrier(v.astype(jnp.bfloat16)).astype(jnp.float32)

@jax.custom_vjp
def low_back(v):
    return v

def low_keep(v):
    return (low(v), None)

def low_pass(kept, grad):
    return (grad,)

def back_keep(v):
    return (v, None)

def back_low(kept, grad):
    return (low(grad),)
low.defvjp(low_keep, low_pass)
low_back.defvjp(back_keep, back_low)
NORM_EPS = 1e-05
NEGATIVE = -1e+30
EXACT_PRECISION = lax.Precision.HIGHEST

def positions(doc_rows):
    row_count = doc_rows.shape[0]
    row_index = jnp.arange(row_count, dtype=jnp.int32)
    change = jnp.concatenate([jnp.ones((1,), dtype=bool), doc_rows[1:] != doc_rows[:-1]])
    begins = lax.cummax(jnp.where(change, row_index, jnp.zeros_like(row_index)), axis=0)
    return row_index - begins

def rotary_tables(doc_rows):
    places = positions(doc_rows).astype(jnp.float32)
    half_rot = ROT // 2
    frequency = 10000.0 ** (-2.0 * jnp.arange(half_rot, dtype=jnp.float32) / ROT)
    angles = places[:, None] * frequency[None, :]
    return (jnp.cos(angles), jnp.sin(angles))

def rotate(values, cosine, sine_tab):
    half_rot = ROT // 2
    first_half = values[..., :half_rot]
    second_half = values[..., half_rot:2 * half_rot]
    remain = values[..., 2 * half_rot:]
    return jnp.concatenate([first_half * cosine - second_half * sine_tab, second_half * cosine + first_half * sine_tab, remain], axis=-1)

def forward(xfloat, norm_gain, norm_shift, out_bias, w_qkv, b_qkv, w_out, w_up, b_up, w_down, doc_rows, real_float):
    mean_removed = xfloat - lax.optimization_barrier(jnp.mean(xfloat, axis=-1, keepdims=True))
    inverse_deviation = lax.rsqrt(lax.optimization_barrier(jnp.mean(mean_removed * mean_removed, axis=-1, keepdims=True)) + NORM_EPS)
    normed_input = low(mean_removed * inverse_deviation * low(norm_gain) + low(norm_shift))
    project = jnp.einsum('td,cde->cte', normed_input, low(w_qkv), precision=EXACT_PRECISION)
    project = low_back(project + low(b_qkv).reshape(3, 1, D))
    row_count = xfloat.shape[0]
    heads_view = project.reshape(3, row_count, HEADS, HEAD_DIM).transpose(0, 2, 1, 3)
    cosine, sine_tab = rotary_tables(doc_rows)
    queries = low(rotate(heads_view[0], cosine, sine_tab))
    keys_rot = low(rotate(heads_view[1], cosine, sine_tab))
    values_low = low(heads_view[2])
    row_index = jnp.arange(row_count, dtype=jnp.int32)
    allowed = (doc_rows[:, None] == doc_rows[None, :]) & (row_index[None, :] <= row_index[:, None])
    factor = 1.0 / math.sqrt(HEAD_DIM)
    scores = low_back(jnp.einsum('hqd,hkd->hqk', queries, keys_rot, precision=EXACT_PRECISION) * factor)
    masked = jnp.where(allowed[None], scores, NEGATIVE)
    probability = low(jax.nn.softmax(masked, axis=-1))
    attended = low(low_back(jnp.einsum('hqk,hkd->hqd', probability, values_low, precision=EXACT_PRECISION)))
    attended = attended.transpose(1, 0, 2).reshape(row_count, D)
    hidden_pre = low_back(jnp.dot(normed_input, low(w_up), precision=EXACT_PRECISION) + low(b_up).reshape(FF))
    activated = low(jax.nn.gelu(hidden_pre, approximate=True))
    branch_sum = jnp.dot(attended, low(w_out), precision=EXACT_PRECISION)
    branch_sum = branch_sum + jnp.dot(activated, low(w_down), precision=EXACT_PRECISION) + low(out_bias)
    return xfloat + real_float[:, None] * branch_sum

def reference(tokens, doc_ids, real_rows, cotangent, norm_gain, norm_shift, out_bias, w_qkv, b_qkv, w_out, w_up, b_up, w_down):
    groups = TOKENS // TOK_DEV
    parameters = (norm_gain, norm_shift, out_bias, w_qkv, b_qkv, w_out, w_up, b_up, w_down)
    inputs = (tokens.reshape(groups, TOK_DEV, D), doc_ids.reshape(groups, TOK_DEV), real_rows.reshape(groups, TOK_DEV), cotangent.reshape(groups, TOK_DEV, D))

    def one_group(totals, pieces):
        tok_rows, doc_rows, real_mask, cot_rows = pieces
        real_float = real_mask.astype(jnp.float32)

        def local_forward(xfloat, *weights_all):
            return forward(xfloat, *weights_all, doc_rows, real_float)
        output, pullback = jax.vjp(local_forward, tok_rows.astype(jnp.float32), *parameters)
        gradients = pullback(cot_rows.astype(jnp.float32))
        totals = tuple((running + addend for running, addend in zip(totals, gradients[1:])))
        return (totals, (output.astype(jnp.bfloat16), gradients[0].astype(jnp.bfloat16)))
    initial = tuple((jnp.zeros_like(member_arr) for member_arr in parameters))
    totals, outputs = lax.scan(one_group, initial, inputs)
    block_out = outputs[0].reshape(TOKENS, D)
    tokens_grad = outputs[1].reshape(TOKENS, D)
    return (block_out, tokens_grad, totals[0], totals[1], totals[2], totals[3], totals[4], totals[5], totals[6], totals[7], totals[8])
```

```python
import functools
import math

import jax
import jax.numpy as jnp
from jax import lax
from jax.experimental import pallas as pl
from jax.experimental.pallas import tpu as pltpu
from jax.sharding import PartitionSpec as P

HEAD_DIM = 64
ROT = 32
NORM_EPS = 1e-05
NEGATIVE = -1e30
BF = jnp.bfloat16
F32 = jnp.float32
MESH = pl.DeviceIdType.MESH
VMEM_LIMIT = 60 * 2**20
GATHER_VMEM = 32 * 2**20


def ring_place(group):
    row = group // 2
    return 2 * row + (group + row) % 2


def ring_group(place):
    row = place // 2
    return 2 * row + (place + row) % 2


def chunk_rows(group, half, rows):
    return pl.ds(pl.multiple_of((2 * group + half) * rows, rows), rows)


class Links:
    def __init__(self, dp_size, branch_size):
        self.groups = dp_size // 2
        self.branches = branch_size
        dp = lax.axis_index("dp")
        self.core = dp % 2
        self.other = 1 - self.core
        self.group = dp // 2
        self.place = ring_place(self.group)
        self.branch = lax.axis_index("branch")
        self.sibling = {"dp": 2 * self.group + self.other}
        right = ring_group((self.place + 1) % self.groups)
        left = ring_group((self.place + self.groups - 1) % self.groups)
        self.ring = ({"dp": 2 * right + self.core}, {"dp": 2 * left + self.core})
        self.has_up = self.branch < self.branches - 1
        self.has_down = self.branch > 0
        self.peers = [{"branch": (self.branch + k) % branch_size} for k in range(1, branch_size)]
        self.up = {"branch": self.branch + 1}
        self.down = {"branch": self.branch - 1}

    def meet(self):
        barrier = pltpu.get_barrier_semaphore()

        def greet(device):
            pl.semaphore_signal(barrier, 1, device_id=device, device_id_type=MESH)

        greet(self.sibling)
        greet(self.ring[0])
        greet(self.ring[1])
        for device in self.peers:
            greet(device)
        pl.semaphore_wait(barrier, 3 + len(self.peers))


def remote(src, dst, send, recv, device):
    return pltpu.make_async_remote_copy(
        src_ref=src, dst_ref=dst, send_sem=send, recv_sem=recv, device_id=device, device_id_type=MESH
    )


def gather_kernel(dp_size, branch_size, n_w, *refs):
    rows_refs = refs[:2]
    w_refs = refs[2 : 2 + n_w]
    full_refs = refs[2 + n_w : 4 + n_w]
    wf_refs = refs[4 + n_w : 4 + 2 * n_w]
    small_out = refs[4 + 2 * n_w]
    (z_send, z_recv, s_send, s_recv, l_sem, w_send, w_recv, ws_send, ws_recv, wl_sem, p_send, p_recv, p_local) = refs[
        5 + 2 * n_w :
    ]
    at = Links(dp_size, branch_size)
    at.meet()
    rows = rows_refs[0].shape[0]
    waits = []

    def piece(block, branch):
        start = (block * branch_size + branch) * rows
        return pl.ds(pl.multiple_of(start, rows), rows)

    for a in range(2):
        mine = piece(at.core, at.branch)
        for cond, way, device in ((at.has_up, 0, at.up), (at.has_down, 1, at.down)):
            copy = remote(
                rows_refs[a], full_refs[a].at[mine], z_send.at[a, way, 0], z_recv.at[a, at.branch], device
            )
            if a == 0:
                pl.when(cond)(copy.start)
            waits.append((cond, copy.wait_send))
        copy = remote(
            rows_refs[a], full_refs[a].at[mine], s_send.at[a, at.branch], s_recv.at[a, at.branch], at.sibling
        )
        copy.start()
        waits.append((None, copy.wait_send))
        own = pltpu.make_async_copy(rows_refs[a], full_refs[a].at[mine], l_sem.at[a])
        own.start()
        waits.append((None, own.wait))
    for w in range(n_w):
        here = chunk_rows(at.group, at.core, w_refs[w].shape[1])
        copy = remote(
            w_refs[w].at[at.other], wf_refs[w].at[here], ws_send.at[w], ws_recv.at[w], at.sibling
        )
        copy.start()
        waits.append((None, copy.wait_send))
        own = pltpu.make_async_copy(w_refs[w].at[at.core], wf_refs[w].at[here], wl_sem.at[w])
        own.start()

    def ring_copy(w, half, step):
        shift = step if half == 0 else -step
        source = ring_group((at.place - shift + at.groups) % at.groups)
        part = wf_refs[w].at[chunk_rows(source, half, w_refs[w].shape[1])]
        return remote(part, part, w_send.at[w, half, step], w_recv.at[w, half, step], at.ring[half])

    def ring_step(w, step):
        if step == 0:
            here = wf_refs[w].at[chunk_rows(at.group, at.core, w_refs[w].shape[1])]
            pltpu.make_async_copy(w_refs[w].at[at.core], here, wl_sem.at[w]).wait()
            there = wf_refs[w].at[chunk_rows(at.group, at.other, w_refs[w].shape[1])]
            remote(there, there, ws_send.at[w], ws_recv.at[w], at.sibling).wait_recv()
        for half in range(2):
            if step > 0:
                shift = step if half == 0 else -step
                source = ring_group((at.place - shift + at.groups) % at.groups)
                part = wf_refs[w].at[chunk_rows(source, half, w_refs[w].shape[1])]
                remote(
                    part, part, w_send.at[w, half, step - 1], w_recv.at[w, half, step - 1], at.ring[half]
                ).wait_recv()
            if step < at.groups - 1:
                copy = ring_copy(w, half, step)
                copy.start()
                waits.append((None, copy.wait_send))

    def line_step(a, step):
        for way in range(2):
            source = at.branch - step if way == 0 else at.branch + step
            inside = source >= 0 if way == 0 else source < branch_size
            part = full_refs[a].at[piece(at.core, jnp.clip(source, 0, branch_size - 1))]
            onward = at.branch < branch_size - 1 if way == 0 else at.branch > 0
            device = at.up if way == 0 else at.down
            source = jnp.clip(source, 0, branch_size - 1)
            arrived = remote(part, part, z_send.at[a, way, 0], z_recv.at[a, source], device)
            forward = remote(part, part, z_send.at[a, way, step], z_recv.at[a, source], device)
            across = remote(part, part, s_send.at[a, source], s_recv.at[a, source], at.sibling)

            @pl.when(inside)
            def _():
                arrived.wait_recv()
                pl.when(onward)(forward.start)
                across.start()

            def both(inside=inside, onward=onward, forward=forward, across=across):
                @pl.when(inside)
                def _():
                    pl.when(onward)(forward.wait_send)
                    across.wait_send()

            waits.append((None, both))

    def begin_second():
        mine = piece(at.core, at.branch)
        for cond, way, device in ((at.has_up, 0, at.up), (at.has_down, 1, at.down)):
            copy = remote(
                rows_refs[1], full_refs[1].at[mine], z_send.at[1, way, 0], z_recv.at[1, at.branch], device
            )
            pl.when(cond)(copy.start)

    for w in range(n_w):
        ring_step(w, 0)
    line_steps = [(0, s) for s in range(1, branch_size)] + [(1, s) for s in range(1, branch_size)]
    ring_steps = [(w, s) for s in range(1, at.groups) for w in range(n_w)]
    events = [((i + 1.0) / len(line_steps) * 137.0, 0, e) for i, e in enumerate(line_steps)]
    events += [((i + 1.0) / len(ring_steps) * 103.0, 1, e) for i, e in enumerate(ring_steps)]
    for _, kind, event in sorted(events):
        if kind == 0:
            line_step(*event)
            if event == (0, branch_size - 2 if branch_size > 2 else 1):
                begin_second()
        else:
            ring_step(*event)
    params = wf_refs[n_w - 1]
    own = pltpu.make_async_copy(params, small_out.at[at.branch], p_local)
    own.start()
    waits.append((None, own.wait))
    for k in range(1, branch_size):
        copy = remote(params, small_out.at[at.branch], p_send.at[k], p_recv.at[k], at.peers[k - 1])
        copy.start()
        waits.append((None, copy.wait_send))
    for k in range(1, branch_size):
        slot = small_out.at[(at.branch - k + branch_size) % branch_size]
        remote(slot, slot, p_send.at[k], p_recv.at[k], at.peers[k - 1]).wait_recv()
    for a in range(2):
        for branch in range(branch_size):
            part = full_refs[a].at[piece(at.other, branch)]
            remote(part, part, s_send.at[a, branch], s_recv.at[a, branch], at.sibling).wait_recv()
    for cond, wait in waits:
        if cond is None:
            wait()
        else:
            pl.when(cond)(wait)


def gather_all(dp_size, branch_size, arrays, weights):
    rows, width = arrays[0].shape
    n_w = len(weights)
    groups = dp_size // 2
    out_shape = [jax.ShapeDtypeStruct((2 * branch_size * rows, width), BF)] * 2
    out_shape += [jax.ShapeDtypeStruct((dp_size * w.shape[1], w.shape[2]), BF) for w in weights]
    out_shape += [jax.ShapeDtypeStruct((branch_size, dp_size * weights[-1].shape[1], weights[-1].shape[2]), BF)]
    dma = pltpu.SemaphoreType.DMA
    return pl.pallas_call(
        functools.partial(gather_kernel, dp_size, branch_size, n_w),
        out_shape=out_shape,
        in_specs=[pl.BlockSpec(memory_space=pl.ANY)] * (2 + n_w),
        out_specs=[pl.BlockSpec(memory_space=pl.ANY)] * (3 + n_w),
        scratch_shapes=[
            dma((2, 2, branch_size)),
            dma((2, branch_size)),
            dma((2, branch_size)),
            dma((2, branch_size)),
            dma((2,)),
            dma((n_w, 2, groups)),
            dma((n_w, 2, groups)),
            dma((n_w,)),
            dma((n_w,)),
            dma((n_w,)),
            dma((branch_size,)),
            dma((branch_size,)),
            dma,
        ],
        compiler_params=pltpu.CompilerParams(
            collective_id=0, has_side_effects=True, vmem_limit_bytes=GATHER_VMEM
        ),
        name="gather_all",
    )(*arrays, *weights)


def scatter_kernel(dp_size, branch_size, *refs):
    (h_ref, gm_ref, dqkv_ref, dz_ref, o_ref, u_ref, dh_ref, sums_ref) = refs[:8]
    g_refs = refs[8:12]
    tok_out, sum_out, sib_land = refs[12:15]
    slots = refs[15:19]
    firsts = refs[19:23]
    gots = refs[23:27]
    (own_buf, sib_buf, line_slot, w_send, w_recv, ws_send, ws_recv, z_send, z_recv, s_send, s_recv,
     l_sem, left_buf, x_sem, sum_slot, sum_first, sum_got, sum_peer, p_send, p_recv) = refs[27:]
    at = Links(dp_size, branch_size)
    at.meet()
    rows = own_buf.shape[0]
    toks = branch_size * rows
    w_rows = firsts[0].shape[1]
    block = left_buf.shape[3]
    lefts = (gm_ref, h_ref)
    rights = (u_ref, o_ref, dz_ref, dqkv_ref)
    last = at.groups - 1
    waits = []
    first_sent = {}

    sib_copy = remote(
        dh_ref.at[pl.ds(at.other * toks, toks)], sib_land, s_send, s_recv, at.sibling
    )
    sib_copy.start()

    def left_copy(a, half, step):
        shift = step + 1 if half == 0 else -step - 1
        dest = ring_group((at.place - shift + 2 * at.groups) % at.groups)
        start = (2 * dest + half) * w_rows if block == w_rows else dest * block
        start = pl.multiple_of(start, block)
        return pltpu.make_async_copy(lefts[a].at[:, pl.ds(start, block)], left_buf.at[a, half], x_sem.at[a, half])

    def ring_step(a, step):
        for half in range(2):
            left_copy(a, half, step).wait()
            for w in (2 * a, 2 * a + 1):
                total = lax.dot_general(
                    left_buf[a, half, :, pl.ds(half * (block - w_rows), w_rows)], rights[w][...], (((0,), (0,)), ((), ())), preferred_element_type=F32
                )
                if step > 0:
                    slot = slots[w].at[half, step - 1]
                    remote(
                        slot, slot, w_send.at[w, half, step - 1], w_recv.at[w, half, step - 1], at.ring[half]
                    ).wait_recv()
                    total = total + slot[...].astype(F32)
                if step < last:
                    out = firsts[w].at[half] if step == 0 else slots[w].at[half, step - 1]
                    out[...] = total.astype(BF)
                    copy = remote(
                        out, slots[w].at[half, step], w_send.at[w, half, step], w_recv.at[w, half, step], at.ring[half]
                    )
                    copy.start()
                    if step == 0:
                        first_sent[w, half] = copy
                    else:
                        waits.append(copy.wait_send)
                else:
                    out = firsts[w].at[half]
                    first_sent[w, half].wait_send()
                    copy = remote(out, gots[w], ws_send.at[w], ws_recv.at[w], at.sibling)

                    @pl.when(at.core == half)
                    def _():
                        g_refs[w][half] = total

                    @pl.when(at.core != half)
                    def _():
                        out[...] = total.astype(BF)
                        copy.start()

                    waits.append(lambda copy=copy, half=half: pl.when(at.core != half)(copy.wait_send))

            if step < last:
                left_copy(a, half, step + 1).start()

    n_w = 4

    def sum_step(step):
        for half in range(2):
            shift = step + 1 if half == 0 else -step - 1
            dest = ring_group((at.place - shift + 2 * at.groups) % at.groups)
            total = sums_ref[chunk_rows(dest, half, 8)]
            if step > 0:
                slot = sum_slot.at[half, step - 1]
                remote(
                    slot, slot, w_send.at[n_w, half, step - 1], w_recv.at[n_w, half, step - 1], at.ring[half]
                ).wait_recv()
                total = total + slot[...]
            out = sum_first.at[step, half]
            out[...] = total
            if step < last:
                copy = remote(
                    out, sum_slot.at[half, step], w_send.at[n_w, half, step], w_recv.at[n_w, half, step], at.ring[half]
                )
                copy.start()
                waits.append(copy.wait_send)
        if step == last:
            copy = remote(
                sum_first.at[last, at.other], sum_got, ws_send.at[n_w], ws_recv.at[n_w], at.sibling
            )
            copy.start()
            copy.wait()
            mine = sum_peer.at[0]
            mine[...] = sum_first[last, at.core] + sum_got[...]
            sum_out[at.core] = sum_first[last, at.core]
            sum_out[at.other] = sum_got[...]
            for k in range(1, branch_size):
                copy = remote(mine, sum_peer.at[k], p_send.at[k], p_recv.at[k], at.peers[k - 1])
                copy.start()
                waits.append(copy.wait_send)

    def sum_end():
        total = sum_peer[0]
        for k in range(1, branch_size):
            remote(sum_peer.at[0], sum_peer.at[k], p_send.at[k], p_recv.at[k], at.peers[k - 1]).wait_recv()
            total = total + sum_peer[k]
        sum_out[2] = total

    def load_own(k, d):
        own = pltpu.make_async_copy(dh_ref.at[pl.ds(at.core * toks + d * rows, rows)], own_buf, l_sem.at[0])
        sib = pltpu.make_async_copy(sib_land.at[pl.ds(d * rows, rows)], sib_buf, l_sem.at[1])
        own.start()
        sib.start()
        own.wait()
        sib.wait()

    def line_step(k):
        for way in range(2):
            d = branch_size - 1 - k if way == 0 else k
            going = at.branch < d if way == 0 else at.branch > d
            more = at.branch > 0 if way == 0 else at.branch < branch_size - 1
            device = at.up if way == 0 else at.down
            slot = line_slot.at[way, d - 1 + way]
            sent = remote(slot, slot, z_send.at[way, d], z_recv.at[way, d], device)

            @pl.when(going)
            def _():
                load_own(k, d)
                total = own_buf[...].astype(F32) + sib_buf[...].astype(F32)

                @pl.when(more)
                def _():
                    sent.wait_recv()
                    slot[...] = (total + slot[...].astype(F32)).astype(BF)

                @pl.when(jnp.logical_not(more))
                def _():
                    slot[...] = total.astype(BF)

                sent.start()

            waits.append(lambda going=going, sent=sent: pl.when(going)(sent.wait_send))

    def line_end():
        d = at.branch
        load_own(0, d)
        tok_out[...] = own_buf[...].astype(F32) + sib_buf[...].astype(F32)
        for way in range(2):
            more = at.branch > 0 if way == 0 else at.branch < branch_size - 1
            slot = line_slot.at[way, d - 1 + way]
            device = at.up if way == 0 else at.down

            @pl.when(more)
            def _():
                remote(slot, slot, z_send.at[way, d], z_recv.at[way, d], device).wait_recv()
                tok_out[...] += slot[...].astype(F32)

    for a in range(2):
        for half in range(2):
            left_copy(a, half, 0).start()
    sum_step(0)
    ring_step(0, 0)
    sib_copy.wait_recv()
    line_step(0)
    ring_step(1, 0)
    for k in range(1, branch_size - 1):
        line_step(k)
    events = []
    for s in range(1, at.groups):
        for a in range(2):
            ring_step(a, s)
        sum_step(s)
        if s == 2:
            line_end()
    if at.groups < 3:
        line_end()
    for w in range(n_w):
        remote(firsts[w].at[0], gots[w], ws_send.at[w], ws_recv.at[w], at.sibling).wait_recv()
        g_refs[w][at.other] = gots[w][...].astype(F32)
    sum_end()
    sib_copy.wait_send()
    for wait in waits:
        wait()


def scatter_all(dp_size, branch_size, h, gm, dqkv, dz, o, u, dh, sums):
    widths = [u.shape[1], o.shape[1], dz.shape[1], dqkv.shape[1]]
    width = h.shape[1]
    w_rows = width // dp_size
    groups = dp_size // 2
    toks = h.shape[0] // 2
    rows = toks // branch_size
    n_w = 4
    dma = pltpu.SemaphoreType.DMA
    vm = pl.BlockSpec(memory_space=pltpu.VMEM)
    hb = pl.BlockSpec(memory_space=pl.ANY)
    out_shape = [jax.ShapeDtypeStruct((2, w_rows, n), F32) for n in widths]
    out_shape += [jax.ShapeDtypeStruct((rows, width), F32), jax.ShapeDtypeStruct((3, 8, 128), F32)]
    out_shape += [jax.ShapeDtypeStruct((toks, width), BF)]
    out = pl.pallas_call(
        functools.partial(scatter_kernel, dp_size, branch_size),
        out_shape=out_shape,
        in_specs=[hb] * 2 + [vm] * 4 + [hb, vm],
        out_specs=[vm] * 6 + [hb],
        scratch_shapes=[pltpu.VMEM((2, groups - 1, w_rows, n), BF) for n in widths]
        + [pltpu.VMEM((2, w_rows, n), BF) for n in widths]
        + [pltpu.VMEM((w_rows, n), BF) for n in widths]
        + [
            pltpu.VMEM((rows, width), BF),
            pltpu.VMEM((rows, width), BF),
            pltpu.VMEM((2, branch_size - 1, rows, width), BF),
            dma((n_w + 1, 2, groups)),
            dma((n_w + 1, 2, groups)),
            dma((n_w + 1,)),
            dma((n_w + 1,)),
            dma((2, branch_size)),
            dma((2, branch_size)),
            dma(()),
            dma(()),
            dma((2,)),
            pltpu.VMEM((2, 2, 2 * toks, w_rows if w_rows % 128 == 0 else 2 * w_rows), BF),
            dma((2, 2)),
            pltpu.VMEM((2, groups - 1, 8, 128), F32),
            pltpu.VMEM((groups, 2, 8, 128), F32),
            pltpu.VMEM((8, 128), F32),
            pltpu.VMEM((branch_size, 8, 128), F32),
            dma((branch_size,)),
            dma((branch_size,)),
        ],
        compiler_params=pltpu.CompilerParams(
            collective_id=1, has_side_effects=True, vmem_limit_bytes=VMEM_LIMIT
        ),
        name="scatter_all",
    )(h, gm, dqkv, dz, o, u, dh, sums)
    return out[:6]


def turn(values, tables, sign):
    fixed, from_low, from_high = tables
    half = ROT // 2
    return (
        values * fixed
        + sign * (pltpu.roll(values, half, 1) * from_low + pltpu.roll(values, 2 * HEAD_DIM - half, 1) * from_high)
    )


def score_tile(keys, queries, begins, first, q_tile):
    scores = lax.dot_general(keys, queries, (((1,), (1,)), ((), ())), preferred_element_type=F32)
    key_at = lax.broadcasted_iota(jnp.int32, scores.shape, 0)
    query_at = first + lax.broadcasted_iota(jnp.int32, scores.shape, 1)
    allowed = jnp.logical_and(key_at >= begins, key_at <= query_at)
    return jnp.where(allowed, scores, NEGATIVE)


def attend_kernel(q_tile, q_ref, k_ref, v_ref, begin_ref, table_ref, qr_ref, kr_ref, vr_ref, o_ref, lse_ref):
    tables = tuple(table_ref[0, i] for i in range(3))
    qr_ref[...] = (turn(q_ref[...], tables, 1.0) * (HEAD_DIM**-0.5)).astype(BF)
    kr_ref[...] = turn(k_ref[...], tables, 1.0).astype(BF)
    vr_ref[...] = v_ref[...].astype(BF)
    toks = q_ref.shape[0]
    for first in range(0, toks, q_tile):
        span = first + q_tile
        begins = begin_ref[0, 0:1, first:span]
        outs = []
        for head in range(2):
            lanes = slice(head * HEAD_DIM, (head + 1) * HEAD_DIM)
            scores = score_tile(kr_ref[:span, lanes], qr_ref[first:span, lanes], begins, first, q_tile)
            top = jnp.max(scores, axis=0, keepdims=True)
            weights = jnp.exp(scores - top)
            total = jnp.sum(weights, axis=0, keepdims=True)
            lse_ref[0, 0, head : head + 1, first:span] = top + jnp.log(total)
            mixed = lax.dot_general(
                vr_ref[:span, lanes], weights.astype(BF), (((0,), (0,)), ((), ())), preferred_element_type=F32
            )
            outs.append(mixed / total)
        o_ref[first:span, :] = jnp.concatenate(outs, axis=0).T.astype(BF)


def attend_back_kernel(
    q_tile, qr_ref, kr_ref, vr_ref, o_ref, do_ref, lse_ref, begin_ref, table_ref, dq_ref, dk_ref, dv_ref, k_acc, v_acc
):
    tables = tuple(table_ref[0, i] for i in range(3))
    toks = qr_ref.shape[0]
    k_acc[...] = jnp.zeros_like(k_acc)
    v_acc[...] = jnp.zeros_like(v_acc)
    for first in range(0, toks, q_tile):
        span = first + q_tile
        begins = begin_ref[0, 0:1, first:span]
        both = (do_ref[first:span, :].astype(F32) * o_ref[first:span, :].astype(F32)).T
        turned = []
        for head in range(2):
            lanes = slice(head * HEAD_DIM, (head + 1) * HEAD_DIM)
            delta = jnp.sum(both[lanes], axis=0, keepdims=True)
            queries = qr_ref[first:span, lanes]
            grads = do_ref[first:span, lanes]
            keys = kr_ref[:span, lanes]
            scores = score_tile(keys, queries, begins, first, q_tile)
            prob = jnp.exp(scores - lse_ref[0, 0, head : head + 1, first:span])
            v_acc[head, :span, :] += jnp.dot(prob.astype(BF), grads, preferred_element_type=F32)
            dprob = lax.dot_general(
                vr_ref[:span, lanes], grads, (((1,), (1,)), ((), ())), preferred_element_type=F32
            )
            ds = (prob * (dprob - delta)).astype(BF)
            k_acc[head, :span, :] += jnp.dot(ds, queries, preferred_element_type=F32)
            turned.append(
                lax.dot_general(keys, ds, (((0,), (0,)), ((), ())), preferred_element_type=F32)
            )
        dq = jnp.concatenate(turned, axis=0).T * (HEAD_DIM**-0.5)
        dq_ref[first:span, :] = turn(dq, tuple(t[first:span] for t in tables), -1.0).astype(BF)
    dk = jnp.concatenate([k_acc[0], k_acc[1]], axis=1)
    dk_ref[...] = turn(dk, tables, -1.0).astype(BF)
    dv_ref[...] = jnp.concatenate([v_acc[0], v_acc[1]], axis=1).astype(BF)


def attention_specs(toks, pairs):
    wide = 2 * HEAD_DIM

    def cols(shift):
        return pl.BlockSpec((toks, wide), lambda i, j: (i, j + shift * pairs))

    begin = pl.BlockSpec((1, 8, toks), lambda i, j: (i, 0, 0))
    table = pl.BlockSpec((1, 3, toks, wide), lambda i, j: (i, 0, 0, 0))
    lse = pl.BlockSpec((1, 1, 2, toks), lambda i, j: (i, j, 0, 0))
    return cols, begin, table, lse


def attend(project, begins, tables):
    blocks, _, toks = begins.shape
    pairs = project.shape[1] // (6 * HEAD_DIM)
    cols, begin, table, lse = attention_specs(toks, pairs)
    narrow = jax.ShapeDtypeStruct((blocks * toks, pairs * 2 * HEAD_DIM), BF)
    return pl.pallas_call(
        functools.partial(attend_kernel, min(256, toks)),
        grid=(blocks, pairs),
        in_specs=[cols(0), cols(1), cols(2), begin, table],
        out_specs=[cols(0)] * 4 + [lse],
        out_shape=[narrow] * 4 + [jax.ShapeDtypeStruct((blocks, pairs, 2, toks), F32)],
        compiler_params=pltpu.CompilerParams(vmem_limit_bytes=GATHER_VMEM),
        name="attend",
    )(project, project, project, begins, tables)


def attend_back(queries, keys, values, o, do, lse_rows, begins, tables):
    blocks, _, toks = begins.shape
    pairs = queries.shape[1] // (2 * HEAD_DIM)
    cols, begin, table, lse = attention_specs(toks, pairs)
    narrow = jax.ShapeDtypeStruct(queries.shape, BF)
    acc = pltpu.VMEM((2, toks, HEAD_DIM), F32)
    return pl.pallas_call(
        functools.partial(attend_back_kernel, min(256, toks)),
        grid=(blocks, pairs),
        in_specs=[cols(0)] * 5 + [lse, begin, table],
        out_specs=[cols(0)] * 3,
        out_shape=[narrow] * 3,
        scratch_shapes=[acc, acc],
        compiler_params=pltpu.CompilerParams(vmem_limit_bytes=GATHER_VMEM),
        name="attend_back",
    )(queries, keys, values, o, do, lse_rows, begins, tables)


def rotary_tables(doc_rows):
    row_count = doc_rows.shape[0]
    row_index = jnp.arange(row_count, dtype=jnp.int32)
    same = doc_rows[:, None] == doc_rows[None, :]
    begins = jnp.min(jnp.where(same, row_index[:, None], row_count), axis=0)
    places = (row_index - begins).astype(F32)
    half = ROT // 2
    frequency = 10000.0 ** (-2.0 * jnp.arange(half, dtype=F32) / ROT)
    angles = places[:, None] * frequency[None, :]
    cosine, sine = jnp.cos(angles), jnp.sin(angles)
    none = jnp.zeros((row_count, HEAD_DIM - ROT), F32)
    blank = jnp.zeros_like(sine)
    fixed = jnp.concatenate([cosine, cosine, none + 1.0], axis=1)
    from_low = jnp.concatenate([blank, sine, none], axis=1)
    from_high = jnp.concatenate([-sine, blank, none], axis=1)
    tables = jnp.stack([jnp.tile(t, (1, 2)) for t in (fixed, from_low, from_high)])
    return jnp.broadcast_to(begins[None], (8, row_count)), tables


def contract_cols(left, right):
    return lax.dot_general(left, right, (((1,), (1,)), ((), ())), preferred_element_type=F32)


def gelu_tanh(values):
    return jax.nn.gelu(values, approximate=True)


def local(
    dp_size, branch_size, tokens, doc_ids, real_rows, cotangent, norm_gain, norm_shift, out_bias,
    w_qkv, b_qkv, w_out, w_up, b_up, w_down,
):
    dp = lax.axis_index("dp")
    branch = lax.axis_index("branch")
    core = dp % 2
    my_rows, width = tokens.shape
    toks = doc_ids.shape[0]
    w_rows = w_qkv.shape[1]
    cols = w_qkv.shape[2] // 2
    hid = w_up.shape[1] // 2
    heads = cols // HEAD_DIM

    my_real = lax.dynamic_slice_in_dim(real_rows, branch * my_rows, my_rows).astype(F32)
    masked_cot = (cotangent.astype(F32) * my_real[:, None]).astype(BF)
    qkv_l = w_qkv.astype(BF).reshape(3, w_rows, 2, cols).transpose(2, 1, 0, 3).reshape(2, w_rows, 3 * cols)
    up_l = w_up.astype(BF).reshape(w_rows, 2, hid).transpose(1, 0, 2)
    out_l = w_out.astype(BF).T.reshape(w_rows, 2, cols).transpose(1, 0, 2)
    down_l = w_down.astype(BF).T.reshape(w_rows, 2, hid).transpose(1, 0, 2)

    small = jnp.concatenate([v.reshape(-1) for v in (norm_gain, norm_shift, out_bias, b_qkv, b_up)]).astype(BF)
    small = jnp.pad(small, (0, -small.size % 128))
    small = jnp.broadcast_to(small[None, None], (2, 16, small.size))

    tok_all, gm, wqkv, wup, wot, wdt, _, params = gather_all(
        dp_size, branch_size, (tokens, masked_cot), (qkv_l, up_l, out_l, down_l, small)
    )
    params = params.reshape(branch_size, dp_size, 16, -1)[:, :, 0].astype(F32)
    sizes = [norm_gain.size, norm_shift.size, out_bias.size, b_qkv.size, b_up.size]
    stops = [sum(sizes[: i + 1]) for i in range(5)]
    gain, shift, bias_full = (
        params[:, :, stops[i] - sizes[i] : stops[i]].transpose(1, 0, 2).reshape(width) for i in range(3)
    )
    mine = lax.dynamic_index_in_dim(params, branch, 0, keepdims=False)
    qkv_b = mine[:, stops[2] : stops[3]].reshape((dp_size,) + b_qkv.shape).transpose(1, 2, 0, 3)
    qkv_b = qkv_b.reshape(3, 2, cols)
    qkv_b = lax.dynamic_index_in_dim(qkv_b, core, 1, keepdims=False).reshape(3 * cols)
    up_b = mine[:, stops[3] : stops[4]].reshape((dp_size,) + b_up.shape).transpose(1, 0, 2).reshape(2, hid)
    up_b = lax.dynamic_index_in_dim(up_b, core, 0, keepdims=False)
    swap = [(i, i + 1 - 2 * (i % 2)) for i in range(dp_size)]
    other_ids = lax.ppermute(doc_ids, "dp", swap)
    ids = jnp.where(core == 0, jnp.stack([doc_ids, other_ids]), jnp.stack([other_ids, doc_ids]))

    def normed(values):
        xfloat = values.astype(F32)
        removed = xfloat - jnp.mean(xfloat, axis=-1, keepdims=True)
        inverse = lax.rsqrt(jnp.mean(removed * removed, axis=-1, keepdims=True) + NORM_EPS)
        return removed * inverse, inverse

    xhat_all = normed(tok_all)[0]
    h = (xhat_all * gain + shift).astype(BF)
    project = jnp.dot(h, wqkv, preferred_element_type=F32) + qkv_b
    found = [rotary_tables(ids[i]) for i in range(2)]
    begins = jnp.stack([t[0] for t in found])
    tables = jnp.stack([t[1] for t in found])
    queries, keys, values, o, lse_rows = attend(project, begins, tables)
    hidden = jnp.dot(h, wup, preferred_element_type=F32) + up_b
    u = gelu_tanh(hidden).astype(BF)
    br = (contract_cols(o, wot) + contract_cols(u, wdt)).astype(BF).reshape(2, toks, width)
    give = lax.dynamic_index_in_dim(br, 1 - core, 0, keepdims=False)
    keep = lax.dynamic_index_in_dim(br, core, 0, keepdims=False)
    br = (keep.astype(F32) + lax.ppermute(give, "dp", swap).astype(F32)).astype(BF)
    summed = lax.psum_scatter(br, "branch", scatter_dimension=0, tiled=True).astype(F32)
    xfloat = tokens.astype(F32)

    dact = jnp.dot(gm, wdt, preferred_element_type=F32)
    dz = jax.vjp(gelu_tanh, hidden)[1](dact)[0].astype(BF)
    do = jnp.dot(gm, wot, preferred_element_type=F32).astype(BF)
    dqkv = jnp.concatenate(attend_back(queries, keys, values, o, do, lse_rows, begins, tables), axis=1)
    dh_part = contract_cols(dz, wup) + contract_cols(dqkv, wqkv)
    dh = dh_part.astype(BF)

    part = norm_gain.shape[0]
    vectors = jnp.stack(
        [jnp.sum(dh_part * xhat_all, axis=0), jnp.sum(dh_part, axis=0), jnp.sum(masked_cot, axis=0, dtype=F32)]
    )
    vectors = vectors.reshape(3, dp_size, branch_size * part).transpose(1, 0, 2).reshape(dp_size, -1)
    q_sum = jnp.sum(dqkv, axis=0, dtype=F32).reshape(3, heads, dp_size, -1).transpose(2, 0, 1, 3).reshape(dp_size, -1)
    u_sum = jnp.sum(dz, axis=0, dtype=F32).reshape(b_up.shape[0] // 2, dp_size, -1).transpose(1, 0, 2)
    u_sum = u_sum.reshape(dp_size, -1)
    sums = jnp.concatenate([vectors, q_sum, u_sum], axis=1)
    ends = (vectors.shape[1], vectors.shape[1] + q_sum.shape[1], sums.shape[1])
    sums = jnp.pad(sums, ((0, 0), (0, 1024 - sums.shape[1]))).reshape(8 * dp_size, 128)
    sums, summed = lax.optimization_barrier((sums, summed))

    g_down, g_out, g_up, g_qkv, dh_mine, total = scatter_all(dp_size, branch_size, h, gm, dqkv, dz, o, u, dh, sums)
    total = total.reshape(3, 1024)
    block_out = (xfloat + my_real[:, None] * (summed + bias_full)).astype(BF)
    xhat, inverse = normed(tokens)
    scaled = dh_mine * gain
    input_grad = inverse * (
        scaled
        - jnp.mean(scaled, axis=-1, keepdims=True)
        - xhat * jnp.mean(scaled * xhat, axis=-1, keepdims=True)
    )
    tokens_grad = (cotangent.astype(F32) + input_grad).astype(BF)

    gain_g, shift_g, bias_g = lax.dynamic_slice_in_dim(
        total[2, : ends[0]].reshape(3, branch_size * part), branch * part, part, axis=1
    )
    b_q = total[:2, ends[0] : ends[1]].reshape(2, 3, heads, -1).transpose(1, 0, 2, 3).reshape(b_qkv.shape)
    b_u = total[:2, ends[1] : ends[2]].reshape(b_up.shape)
    g_qkv = g_qkv.reshape(2, w_rows, 3, cols).transpose(2, 1, 0, 3).reshape(w_qkv.shape)
    g_up = g_up.transpose(1, 0, 2).reshape(w_up.shape)
    g_out = g_out.transpose(0, 2, 1).reshape(w_out.shape)
    g_down = g_down.transpose(0, 2, 1).reshape(w_down.shape)
    return (block_out, tokens_grad, gain_g, shift_g, bias_g, g_qkv, b_q, g_out, g_up, b_u, g_down)


def solution(mesh):
    in_specs = (
        P(("dp", "branch"), None),
        P("dp"),
        P("dp"),
        P(("dp", "branch"), None),
        P(("dp", "branch")),
        P(("dp", "branch")),
        P(("dp", "branch")),
        P(None, "dp", "branch"),
        P(None, "branch", "dp"),
        P("branch", "dp"),
        P("dp", "branch"),
        P("branch", "dp"),
        P("branch", "dp"),
    )
    out_specs = (
        P(("dp", "branch"), None),
        P(("dp", "branch"), None),
        P(("dp", "branch")),
        P(("dp", "branch")),
        P(("dp", "branch")),
        P(None, "dp", "branch"),
        P(None, "branch", "dp"),
        P("branch", "dp"),
        P("dp", "branch"),
        P("branch", "dp"),
        P("branch", "dp"),
    )
    body = functools.partial(local, mesh.shape["dp"], mesh.shape["branch"])
    return jax.shard_map(body, mesh=mesh, in_specs=in_specs, out_specs=out_specs, check_vma=False)
```

```python
import functools
import math

import jax
import jax.numpy as jnp
import numpy as np
from jax import lax
from jax.experimental import pallas as pl
from jax.experimental.pallas import tpu as pltpu
from jax.sharding import PartitionSpec as P

HEAD_DIM = 64
ROT = 32
NORM_EPS = 1e-05
NEGATIVE = -1e30
BF = jnp.bfloat16
F32 = jnp.float32
MESH = pl.DeviceIdType.MESH
VMEM_LIMIT = 48 * 2**20
ROW_TILE = 256
GATHER_VMEM = 32 * 2**20


def ring_place(group):
    row = group // 2
    return 2 * row + (group + row) % 2


def ring_group(place):
    row = place // 2
    return 2 * row + (place + row) % 2


def chunk_rows(group, half, rows):
    return pl.ds(pl.multiple_of((2 * group + half) * rows, rows), rows)


class Links:
    def __init__(self, dp_size, branch_size):
        self.groups = dp_size // 2
        self.branches = branch_size
        dp = lax.axis_index("dp")
        self.core = dp % 2
        self.other = 1 - self.core
        self.group = dp // 2
        self.place = ring_place(self.group)
        self.branch = lax.axis_index("branch")
        self.sibling = {"dp": 2 * self.group + self.other}
        right = ring_group((self.place + 1) % self.groups)
        left = ring_group((self.place + self.groups - 1) % self.groups)
        self.ring = ({"dp": 2 * right + self.core}, {"dp": 2 * left + self.core})
        self.has_up = self.branch < self.branches - 1
        self.has_down = self.branch > 0
        self.peers = [{"branch": (self.branch + k) % branch_size} for k in range(1, branch_size)]
        self.up = {"branch": self.branch + 1}
        self.down = {"branch": self.branch - 1}

    def meet(self):
        barrier = pltpu.get_barrier_semaphore()

        def greet(device):
            pl.semaphore_signal(barrier, 1, device_id=device, device_id_type=MESH)

        greet(self.sibling)
        greet(self.ring[0])
        greet(self.ring[1])
        for device in self.peers:
            greet(device)
        pl.semaphore_wait(barrier, 3 + len(self.peers))


def remote(src, dst, send, recv, device):
    return pltpu.make_async_remote_copy(
        src_ref=src, dst_ref=dst, send_sem=send, recv_sem=recv, device_id=device, device_id_type=MESH
    )


def gather_kernel(dp_size, branch_size, n_w, *refs):
    rows_ref = refs[0]
    w_refs = refs[1 : 1 + n_w]
    full_ref = refs[1 + n_w]
    wf_refs = refs[2 + n_w : 2 + 2 * n_w]
    small_out = refs[2 + 2 * n_w]
    (z_send, z_recv, s_send, s_recv, l_sem, w_send, w_recv, ws_send, ws_recv, wl_sem, p_send, p_recv, p_local) = refs[
        3 + 2 * n_w :
    ]
    at = Links(dp_size, branch_size)
    at.meet()
    rows = rows_ref.shape[0]
    waits = []

    def piece(block, branch):
        start = (block * branch_size + branch) * rows
        return full_ref.at[pl.ds(pl.multiple_of(start, rows), rows)]

    for cond, way, device in ((at.has_up, 0, at.up), (at.has_down, 1, at.down)):
        copy = remote(rows_ref, piece(0, at.branch), z_send.at[way, 0], z_recv.at[at.branch], device)
        pl.when(cond)(copy.start)
        waits.append((cond, copy.wait_send))
    copy = remote(rows_ref, piece(1, at.branch), s_send.at[at.branch], s_recv.at[at.branch], at.sibling)
    copy.start()
    waits.append((None, copy.wait_send))
    own = pltpu.make_async_copy(rows_ref, piece(0, at.branch), l_sem)
    own.start()
    waits.append((None, own.wait))
    for w in range(n_w):
        here = chunk_rows(at.group, at.core, w_refs[w].shape[1])
        copy = remote(
            w_refs[w].at[at.other], wf_refs[w].at[here], ws_send.at[w], ws_recv.at[w], at.sibling
        )
        copy.start()
        waits.append((None, copy.wait_send))
        own = pltpu.make_async_copy(w_refs[w].at[at.core], wf_refs[w].at[here], wl_sem.at[w])
        own.start()

    def ring_copy(w, half, step):
        shift = step if half == 0 else -step
        source = ring_group((at.place - shift + at.groups) % at.groups)
        part = wf_refs[w].at[chunk_rows(source, half, w_refs[w].shape[1])]
        return remote(part, part, w_send.at[w, half, step], w_recv.at[w, half, step], at.ring[half])

    def ring_step(w, step):
        if step == 0:
            here = wf_refs[w].at[chunk_rows(at.group, at.core, w_refs[w].shape[1])]
            pltpu.make_async_copy(w_refs[w].at[at.core], here, wl_sem.at[w]).wait()
            there = wf_refs[w].at[chunk_rows(at.group, at.other, w_refs[w].shape[1])]
            remote(there, there, ws_send.at[w], ws_recv.at[w], at.sibling).wait_recv()
        for half in range(2):
            if step > 0:
                shift = step if half == 0 else -step
                source = ring_group((at.place - shift + at.groups) % at.groups)
                part = wf_refs[w].at[chunk_rows(source, half, w_refs[w].shape[1])]
                remote(
                    part, part, w_send.at[w, half, step - 1], w_recv.at[w, half, step - 1], at.ring[half]
                ).wait_recv()
            if step < at.groups - 1:
                copy = ring_copy(w, half, step)
                copy.start()
                waits.append((None, copy.wait_send))

    def line_step(step):
        for way in range(2):
            source = at.branch - step if way == 0 else at.branch + step
            inside = source >= 0 if way == 0 else source < branch_size
            onward = at.has_up if way == 0 else at.has_down
            device = at.up if way == 0 else at.down
            source = jnp.clip(source, 0, branch_size - 1)
            part = piece(0, source)
            forward = remote(part, part, z_send.at[way, step], z_recv.at[source], device)
            across = remote(part, piece(1, source), s_send.at[source], s_recv.at[source], at.sibling)

            @pl.when(inside)
            def _():
                forward.wait_recv()
                pl.when(onward)(forward.start)
                across.start()

            def both(inside=inside, onward=onward, forward=forward, across=across):
                @pl.when(inside)
                def _():
                    pl.when(onward)(forward.wait_send)
                    across.wait_send()

            waits.append((None, both))

    for w in range(n_w):
        ring_step(w, 0)
    line_steps = list(range(1, branch_size))
    ring_steps = [(w, s) for s in range(1, at.groups) for w in range(n_w)]
    events = [(23.0 * e, 0, e) for e in line_steps]
    events += [((i + 1.0) / len(ring_steps) * 103.0, 1, e) for i, e in enumerate(ring_steps)]
    for _, kind, event in sorted(events, key=lambda e: e[:2]):
        if kind == 0:
            line_step(event)
        else:
            ring_step(*event)
    params = wf_refs[n_w - 1]
    own = pltpu.make_async_copy(params, small_out.at[at.branch], p_local)
    own.start()
    waits.append((None, own.wait))
    for k in range(1, branch_size):
        copy = remote(params, small_out.at[at.branch], p_send.at[k], p_recv.at[k], at.peers[k - 1])
        copy.start()
        waits.append((None, copy.wait_send))
    for k in range(1, branch_size):
        slot = small_out.at[(at.branch - k + branch_size) % branch_size]
        remote(slot, slot, p_send.at[k], p_recv.at[k], at.peers[k - 1]).wait_recv()
    for branch in range(branch_size):
        part = piece(1, branch)
        remote(part, part, s_send.at[branch], s_recv.at[branch], at.sibling).wait_recv()
    for cond, wait in waits:
        if cond is None:
            wait()
        else:
            pl.when(cond)(wait)


def gather_all(dp_size, branch_size, array, weights):
    rows, width = array.shape
    n_w = len(weights)
    groups = dp_size // 2
    out_shape = [jax.ShapeDtypeStruct((2 * branch_size * rows, width), BF)]
    out_shape += [jax.ShapeDtypeStruct((dp_size * w.shape[1], w.shape[2]), BF) for w in weights]
    out_shape += [jax.ShapeDtypeStruct((branch_size, dp_size * weights[-1].shape[1], weights[-1].shape[2]), BF)]
    dma = pltpu.SemaphoreType.DMA
    return pl.pallas_call(
        functools.partial(gather_kernel, dp_size, branch_size, n_w),
        out_shape=out_shape,
        in_specs=[pl.BlockSpec(memory_space=pl.ANY)] * (1 + n_w),
        out_specs=[pl.BlockSpec(memory_space=pl.ANY)] * (2 + n_w),
        scratch_shapes=[
            dma((2, branch_size)),
            dma((branch_size,)),
            dma((branch_size,)),
            dma((branch_size,)),
            dma,
            dma((n_w, 2, groups)),
            dma((n_w, 2, groups)),
            dma((n_w,)),
            dma((n_w,)),
            dma((n_w,)),
            dma((branch_size,)),
            dma((branch_size,)),
            dma,
        ],
        compiler_params=pltpu.CompilerParams(
            collective_id=0, has_side_effects=True, vmem_limit_bytes=GATHER_VMEM
        ),
        cost_estimate=pl.CostEstimate(
            flops=100 * 4 * rows * width * width, bytes_accessed=2 * rows * width, transcendentals=0
        ),
        name="gather_all",
    )(array, *weights)


def scatter_kernel(dp_size, branch_size, *refs):
    n_w = 4
    (h_ref, gm_ref, other_ref, dqkv_ref, dz_ref, o_ref, u_ref, dh_ref, sums_ref) = refs[:9]
    g_refs = refs[9:13]
    tok_out, sum_out, sib_land = refs[13:16]
    slots = refs[16:20]
    got_refs = refs[20:24]
    outs = refs[24:28]
    ins = refs[28:32]
    (own_buf, sib_buf, line_slot, w_send, w_recv, ws_send, ws_recv, z_send, z_recv, s_send, s_recv,
     l_sem, left_buf, x_sem, i_sem, sum_slot, sum_first, sum_got, sum_peer, p_send, p_recv) = refs[32:]
    at = Links(dp_size, branch_size)
    at.meet()
    rows = own_buf.shape[0]
    toks = branch_size * rows
    w_rows = outs[2].shape[2]
    cols = dqkv_ref.shape[2]
    block = left_buf.shape[3]
    lefts = ((gm_ref, other_ref), (h_ref,))
    rights = (u_ref, o_ref, dz_ref, dqkv_ref)
    last = at.groups - 1
    waits = []
    sent = {}

    sib_copy = remote(dh_ref.at[pl.ds(toks, toks)], sib_land, s_send, s_recv, at.sibling)
    sib_copy.start()

    def ring_dest(half, step):
        shift = step + 1 if half == 0 else -step - 1
        return ring_group((at.place - shift + 2 * at.groups) % at.groups)

    def left_copy(a, half, step):
        dest = ring_dest(half, step)
        start = (2 * dest + half) * w_rows if block == w_rows else dest * block
        start = pl.multiple_of(start, block)
        size = left_buf.shape[2] // len(lefts[a])
        return [
            pltpu.make_async_copy(
                ref.at[:, pl.ds(start, block)], left_buf.at[a, half, pl.ds(i * size, size)], x_sem.at[a, half, i]
            )
            for i, ref in enumerate(lefts[a])
        ]

    def product(a, half, w):
        left = left_buf[a, half, :, pl.ds(half * (block - w_rows), w_rows)]

        def dot(right, flip=False):
            pair = (right, left) if flip else (left, right)
            return lax.dot_general(*pair, (((0,), (0,)), ((), ())), preferred_element_type=F32)

        if w < 3:
            return dot(rights[w][...], w < 2)
        return jnp.concatenate([dot(rights[w][c]) for c in range(3)], axis=1)

    def finish(w, values, core):
        if w < 2:
            size = values.shape[0]
            g_refs[w][pl.ds(pl.multiple_of(core * size, size), size), :] = values
        elif w == 2:
            size = values.shape[1]
            g_refs[w][:, pl.ds(pl.multiple_of(core * size, size), size)] = values
        else:
            for c in range(3):
                g_refs[w][c, :, pl.ds(pl.multiple_of(core * cols, cols), cols)] = values[:, c * cols : (c + 1) * cols]

    def ring_piece(a, half, i, step):
        w = 2 * a + i
        if i == 0:
            for load in left_copy(a, half, step):
                load.wait()
        total = product(a, half, w)
        if step > 0:
            slot = slots[w].at[half, step - 1]
            remote(
                slot, slot, w_send.at[w, half, step - 1], w_recv.at[w, half, step - 1], at.ring[half]
            ).wait_recv()
            load = pltpu.make_async_copy(slot, ins[w], i_sem)
            load.start()
            load.wait()
            total = total + ins[w][...].astype(F32)
        if step > 1:
            sent.pop((w, half, step - 2)).wait_send()
        out = outs[w].at[step % 2, half]
        if step < last:
            out[...] = total.astype(BF)
            copy = remote(
                out, slots[w].at[half, step], w_send.at[w, half, step], w_recv.at[w, half, step], at.ring[half]
            )
            copy.start()
            sent[w, half, step] = copy
        else:
            copy = remote(out, got_refs[w], ws_send.at[w], ws_recv.at[w], at.sibling)

            @pl.when(at.core == half)
            def _():
                finish(w, total, at.core)

            @pl.when(at.core != half)
            def _():
                out[...] = total.astype(BF)
                copy.start()

            waits.append(lambda copy=copy, half=half: pl.when(at.core != half)(copy.wait_send))
        if i == 1 and step < last:
            for load in left_copy(a, half, step + 1):
                load.start()

    def sum_step(step):
        for half in range(2):
            total = sums_ref[chunk_rows(ring_dest(half, step), half, 8)]
            if step > 0:
                slot = sum_slot.at[half, step - 1]
                remote(
                    slot, slot, w_send.at[n_w, half, step - 1], w_recv.at[n_w, half, step - 1], at.ring[half]
                ).wait_recv()
                total = total + slot[...]
            out = sum_first.at[step, half]
            out[...] = total
            if step < last:
                copy = remote(
                    out, sum_slot.at[half, step], w_send.at[n_w, half, step], w_recv.at[n_w, half, step], at.ring[half]
                )
                copy.start()
                waits.append(copy.wait_send)
        if step == last:
            copy = remote(sum_first.at[last, at.other], sum_got, ws_send.at[n_w], ws_recv.at[n_w], at.sibling)
            copy.start()
            copy.wait()
            mine = sum_peer.at[0]
            mine[...] = sum_first[last, at.core] + sum_got[...]
            sum_out[at.core] = sum_first[last, at.core]
            sum_out[at.other] = sum_got[...]
            for k in range(1, branch_size):
                copy = remote(mine, sum_peer.at[k], p_send.at[k], p_recv.at[k], at.peers[k - 1])
                copy.start()
                waits.append(copy.wait_send)

    def sum_end():
        total = sum_peer[0]
        for k in range(1, branch_size):
            remote(sum_peer.at[0], sum_peer.at[k], p_send.at[k], p_recv.at[k], at.peers[k - 1]).wait_recv()
            total = total + sum_peer[k]
        sum_out[2] = total

    def load_own(d):
        own = pltpu.make_async_copy(dh_ref.at[pl.ds(d * rows, rows)], own_buf, l_sem.at[0])
        sib = pltpu.make_async_copy(sib_land.at[pl.ds(d * rows, rows)], sib_buf, l_sem.at[1])
        own.start()
        sib.start()
        own.wait()
        sib.wait()

    def line_step(slot_time):
        far = branch_size - 1 - slot_time
        for way in range(2):
            d = at.branch + far if way == 0 else at.branch - far
            going = d < branch_size if way == 0 else d >= 0
            more = at.has_down if way == 0 else at.has_up
            device = at.up if way == 0 else at.down
            slot = line_slot.at[way, d - 1 + way]
            passing = remote(slot, slot, z_send.at[way, d], z_recv.at[way, d], device)

            @pl.when(going)
            def _():
                load_own(d)
                total = own_buf[...].astype(F32) + sib_buf[...].astype(F32)

                @pl.when(more)
                def _():
                    passing.wait_recv()
                    slot[...] = (total + slot[...].astype(F32)).astype(BF)

                @pl.when(jnp.logical_not(more))
                def _():
                    slot[...] = total.astype(BF)

                passing.start()

            waits.append(lambda going=going, passing=passing: pl.when(going)(passing.wait_send))

    def line_end():
        d = at.branch
        load_own(d)
        for way in range(2):
            more = at.has_down if way == 0 else at.has_up
            slot = line_slot.at[way, d - 1 + way]
            device = at.up if way == 0 else at.down

            @pl.when(more)
            def _():
                remote(slot, slot, z_send.at[way, d], z_recv.at[way, d], device).wait_recv()

        below, above = (
            jnp.where(at.has_down, line_slot[0, jnp.maximum(d - 1, 0)].astype(F32), 0.0),
            jnp.where(at.has_up, line_slot[1, jnp.minimum(d, branch_size - 2)].astype(F32), 0.0),
        )
        tok_out[...] = (own_buf[...].astype(F32) + sib_buf[...].astype(F32) + below + above).astype(BF)

    for a in range(2):
        for half in range(2):
            for load in left_copy(a, half, 0):
                load.start()
    sum_step(0)
    pieces = [(a, half, i) for a in range(2) for half in range(2) for i in range(2)]
    size = [rights[2 * a + i].shape[-1] * (1 + a * i * 2) for a, half, i in pieces]
    due = [sum(size[: i + 1]) / sum(size) for i in range(len(pieces))]
    period = 34.0
    events = [(period * (s - 1 + f) + 4.0, 1, (*p, s)) for s in range(1, at.groups) for p, f in zip(pieces, due)]
    events += [(2.0 * i, 1, (*p, 0)) for i, p in enumerate(pieces)]
    events += [(9.0 + 24.0 * k, 0, k) for k in range(branch_size)]
    events += [(10.0 + 12.0 * s, 2, s) for s in range(1, at.groups)]
    events += [(18.0 + 12.0 * at.groups, 3, 0)]
    for _, kind, event in sorted(events, key=lambda e: e[:2]):
        if kind == 0 and event == 0:
            sib_copy.wait_recv()
        if kind == 0 and event == branch_size - 1:
            line_end()
        elif kind == 0:
            line_step(event)
        elif kind == 1:
            ring_piece(*event)
        elif kind == 2:
            sum_step(event)
        else:
            sum_end()
    for w in range(n_w):
        remote(outs[w].at[0, 0], got_refs[w], ws_send.at[w], ws_recv.at[w], at.sibling).wait_recv()
        finish(w, got_refs[w][...].astype(F32), at.other)
    sib_copy.wait_send()
    for copy in sent.values():
        copy.wait_send()
    for wait in waits:
        wait()


def scatter_all(dp_size, branch_size, h, gm, gm_other, dqkv, dz, o, u, dh, sums):
    widths = [u.shape[1], o.shape[1], dz.shape[1], 3 * dqkv.shape[2]]
    width = h.shape[1]
    w_rows = width // dp_size
    groups = dp_size // 2
    toks = h.shape[0] // 2
    rows = toks // branch_size
    n_w = 4
    dma = pltpu.SemaphoreType.DMA
    vm = pl.BlockSpec(memory_space=pltpu.VMEM)
    hb = pl.BlockSpec(memory_space=pl.ANY)
    shapes = [(widths[0], w_rows), (widths[1], w_rows), (w_rows, widths[2]), (w_rows, widths[3])]
    out_shape = [
        jax.ShapeDtypeStruct((2 * widths[0], w_rows), F32),
        jax.ShapeDtypeStruct((2 * widths[1], w_rows), F32),
        jax.ShapeDtypeStruct((w_rows, 2 * widths[2]), F32),
        jax.ShapeDtypeStruct((3, w_rows, 2 * dqkv.shape[2]), F32),
    ]
    out_shape += [jax.ShapeDtypeStruct((rows, width), BF), jax.ShapeDtypeStruct((3, 8, 128), F32)]
    out_shape += [jax.ShapeDtypeStruct((toks, width), BF)]
    out_shape += [jax.ShapeDtypeStruct((2, groups - 1) + shape, BF) for shape in shapes]
    out = pl.pallas_call(
        functools.partial(scatter_kernel, dp_size, branch_size),
        out_shape=out_shape,
        in_specs=[hb] * 3 + [vm] * 4 + [hb, vm],
        out_specs=[vm] * 6 + [hb] * 5,
        scratch_shapes=[pltpu.VMEM(shape, BF) for shape in shapes]
        + [pltpu.VMEM((2, 2) + shape, BF) for shape in shapes]
        + [pltpu.VMEM(shape, BF) for shape in shapes]
        + [
            pltpu.VMEM((rows, width), BF),
            pltpu.VMEM((rows, width), BF),
            pltpu.VMEM((2, branch_size - 1, rows, width), BF),
            dma((n_w + 1, 2, groups)),
            dma((n_w + 1, 2, groups)),
            dma((n_w + 1,)),
            dma((n_w + 1,)),
            dma((2, branch_size)),
            dma((2, branch_size)),
            dma(()),
            dma(()),
            dma((2,)),
            pltpu.VMEM((2, 2, 2 * toks, w_rows if w_rows % 128 == 0 else 2 * w_rows), BF),
            dma((2, 2, 2)),
            dma(()),
            pltpu.VMEM((2, groups - 1, 8, 128), F32),
            pltpu.VMEM((groups, 2, 8, 128), F32),
            pltpu.VMEM((8, 128), F32),
            pltpu.VMEM((branch_size, 8, 128), F32),
            dma((branch_size,)),
            dma((branch_size,)),
        ],
        compiler_params=pltpu.CompilerParams(
            collective_id=1, has_side_effects=True, vmem_limit_bytes=VMEM_LIMIT
        ),
        cost_estimate=pl.CostEstimate(
            flops=4 * toks * width * sum(widths), bytes_accessed=2 * toks * width, transcendentals=0
        ),
        name="scatter_all",
    )(h, gm, gm_other, dqkv, dz, o, u, dh, sums)
    return out[:4], out[4], out[5]


def turn(values, tables, sign):
    fixed, from_low, from_high = tables
    half = ROT // 2
    return (
        values * fixed
        + sign * (pltpu.roll(values, half, 1) * from_low + pltpu.roll(values, 2 * HEAD_DIM - half, 1) * from_high)
    )


def score_tile(keys, queries, begins, first, q_tile):
    scores = lax.dot_general(keys, queries, (((1,), (1,)), ((), ())), preferred_element_type=F32)
    key_at = lax.broadcasted_iota(jnp.int32, scores.shape, 0)
    query_at = first + lax.broadcasted_iota(jnp.int32, scores.shape, 1)
    allowed = jnp.logical_and(key_at >= begins, key_at <= query_at)
    return jnp.where(allowed, scores, NEGATIVE)


def attend_kernel(q_tile, q_ref, k_ref, v_ref, begin_ref, fixed_ref, low_ref, high_ref, qr_ref, kr_ref, vr_ref, o_ref, lse_ref):
    tables = (fixed_ref[0], low_ref[0], high_ref[0])
    qr_ref[...] = (turn(q_ref[...], tables, 1.0) * (HEAD_DIM**-0.5)).astype(BF)
    kr_ref[...] = turn(k_ref[...], tables, 1.0).astype(BF)
    vr_ref[...] = v_ref[...].astype(BF)
    toks = q_ref.shape[0]
    for first in range(0, toks, q_tile):
        span = first + q_tile
        begins = begin_ref[0, 0:1, first:span]
        outs = []
        for head in range(2):
            lanes = slice(head * HEAD_DIM, (head + 1) * HEAD_DIM)
            scores = score_tile(kr_ref[:span, lanes], qr_ref[first:span, lanes], begins, first, q_tile)
            top = jnp.max(scores, axis=0, keepdims=True)
            weights = jnp.exp(scores - top)
            total = jnp.sum(weights, axis=0, keepdims=True)
            lse_ref[0, 0, head : head + 1, first:span] = top + jnp.log(total)
            mixed = lax.dot_general(
                vr_ref[:span, lanes], weights.astype(BF), (((0,), (0,)), ((), ())), preferred_element_type=F32
            )
            outs.append(mixed / total)
        o_ref[first:span, :] = jnp.concatenate(outs, axis=0).T.astype(BF)


def attend_back_kernel(
    q_tile, qr_ref, kr_ref, vr_ref, o_ref, do_ref, lse_ref, begin_ref, fixed_ref, low_ref, high_ref, grad_ref, k_acc, v_acc
):
    tables = (fixed_ref[0], low_ref[0], high_ref[0])
    toks = qr_ref.shape[0]
    k_acc[...] = jnp.zeros_like(k_acc)
    v_acc[...] = jnp.zeros_like(v_acc)
    for first in range(0, toks, q_tile):
        span = first + q_tile
        begins = begin_ref[0, 0:1, first:span]
        both = (do_ref[first:span, :].astype(F32) * o_ref[first:span, :].astype(F32)).T
        turned = []
        for head in range(2):
            lanes = slice(head * HEAD_DIM, (head + 1) * HEAD_DIM)
            delta = jnp.sum(both[lanes], axis=0, keepdims=True)
            queries = qr_ref[first:span, lanes]
            grads = do_ref[first:span, lanes]
            keys = kr_ref[:span, lanes]
            scores = score_tile(keys, queries, begins, first, q_tile)
            prob = jnp.exp(scores - lse_ref[0, 0, head : head + 1, first:span])
            v_acc[head, :span, :] += jnp.dot(prob.astype(BF), grads, preferred_element_type=F32)
            dprob = lax.dot_general(
                vr_ref[:span, lanes], grads, (((1,), (1,)), ((), ())), preferred_element_type=F32
            )
            ds = (prob * (dprob - delta)).astype(BF)
            k_acc[head, :span, :] += jnp.dot(ds, queries, preferred_element_type=F32)
            turned.append(
                lax.dot_general(keys, ds, (((0,), (0,)), ((), ())), preferred_element_type=F32)
            )
        dq = jnp.concatenate(turned, axis=0).T * (HEAD_DIM**-0.5)
        grad_ref[0, first:span, :] = turn(dq, tuple(t[first:span] for t in tables), -1.0).astype(BF)
    dk = jnp.concatenate([k_acc[0], k_acc[1]], axis=1)
    grad_ref[1] = turn(dk, tables, -1.0).astype(BF)
    grad_ref[2] = jnp.concatenate([v_acc[0], v_acc[1]], axis=1).astype(BF)


def attention_specs(toks, pairs):
    wide = 2 * HEAD_DIM

    def cols(shift):
        return pl.BlockSpec((toks, wide), lambda i, j: (i, j + shift * pairs))

    begin = pl.BlockSpec((1, 8, toks), lambda i, j: (i, 0, 0))
    table = pl.BlockSpec((1, toks, wide), lambda i, j: (i, 0, 0))
    lse = pl.BlockSpec((1, 1, 2, toks), lambda i, j: (i, j, 0, 0))
    return cols, begin, table, lse


def attend(project, begins, tables):
    blocks, _, toks = begins.shape
    pairs = project.shape[1] // (6 * HEAD_DIM)
    cols, begin, table, lse = attention_specs(toks, pairs)
    narrow = jax.ShapeDtypeStruct((blocks * toks, pairs * 2 * HEAD_DIM), BF)
    return pl.pallas_call(
        functools.partial(attend_kernel, min(256, toks)),
        grid=(blocks, pairs),
        in_specs=[cols(0), cols(1), cols(2), begin] + [table] * 3,
        out_specs=[cols(0)] * 4 + [lse],
        out_shape=[narrow] * 4 + [jax.ShapeDtypeStruct((blocks, pairs, 2, toks), F32)],
        compiler_params=pltpu.CompilerParams(vmem_limit_bytes=GATHER_VMEM),
        name="attend",
    )(project, project, project, begins, *tables)


def attend_back(queries, keys, values, o, do, lse_rows, begins, tables):
    blocks, _, toks = begins.shape
    pairs = queries.shape[1] // (2 * HEAD_DIM)
    cols, begin, table, lse = attention_specs(toks, pairs)
    acc = pltpu.VMEM((2, toks, HEAD_DIM), F32)
    return pl.pallas_call(
        functools.partial(attend_back_kernel, min(256, toks)),
        grid=(blocks, pairs),
        in_specs=[cols(0)] * 5 + [lse, begin] + [table] * 3,
        out_specs=pl.BlockSpec((3, toks, 2 * HEAD_DIM), lambda i, j: (0, i, j)),
        out_shape=jax.ShapeDtypeStruct((3,) + queries.shape, BF),
        scratch_shapes=[acc, acc],
        compiler_params=pltpu.CompilerParams(vmem_limit_bytes=GATHER_VMEM),
        name="attend_back",
    )(queries, keys, values, o, do, lse_rows, begins, *tables)


def rotary_tables(doc_rows):
    row_count = doc_rows.shape[0]
    row_index = jnp.arange(row_count, dtype=jnp.int32)
    same = doc_rows[:, None] == doc_rows[None, :]
    begins = jnp.min(jnp.where(same, row_index[:, None], row_count), axis=0)
    places = (row_index - begins).astype(F32)
    half = ROT // 2
    lane = np.arange(2 * HEAD_DIM) % HEAD_DIM
    turning = lane < ROT
    frequency = np.where(turning, 10000.0 ** (-2.0 * (lane % half) / ROT), 0.0).astype(np.float32)
    angles = places[:, None] * frequency[None, :]
    sine = jnp.sin(angles)
    from_low = sine * np.where(turning & (lane >= half), 1.0, 0.0).astype(np.float32)
    from_high = sine * np.where(lane < half, -1.0, 0.0).astype(np.float32)
    return jnp.broadcast_to(begins[None], (8, row_count)), (jnp.cos(angles), from_low, from_high)


def dot_nt(left, right):
    return lax.dot_general(left, right, (((1,), (1,)), ((), ())), preferred_element_type=F32)


def standardized(rows):
    xfloat = rows.astype(F32)
    removed = xfloat - jnp.mean(xfloat, axis=-1, keepdims=True)
    inverse = lax.rsqrt(jnp.mean(removed * removed, axis=-1, keepdims=True) + NORM_EPS)
    return removed * inverse, inverse


def enter_kernel(tok_ref, gain_ref, shift_ref, wq_ref, qb_ref, wu_ref, ub_ref, h_ref, project_ref, u_ref, slope_ref):
    h = (standardized(tok_ref[...])[0] * gain_ref[0:1] + shift_ref[0:1]).astype(BF)
    h_ref[...] = h
    project_ref[...] = jnp.dot(h, wq_ref[...], preferred_element_type=F32) + qb_ref[0:1]
    z = jnp.dot(h, wu_ref[...], preferred_element_type=F32) + ub_ref[0:1]
    scale, cubic = math.sqrt(2.0 / math.pi), 0.044715
    square = z * z
    bent = jnp.tanh(scale * z * (1.0 + cubic * square))
    half = 0.5 * (1.0 + bent)
    u_ref[...] = (z * half).astype(BF)
    slope = half + 0.5 * z * (1.0 - bent * bent) * (scale * (1.0 + 3.0 * cubic * square))
    slope_ref[...] = slope.astype(BF)


def branch_kernel(o_ref, u_ref, wo_ref, wd_ref, br_ref):
    br_ref[...] = (dot_nt(o_ref[...], wo_ref[...]) + dot_nt(u_ref[...], wd_ref[...])).astype(BF)


def grad_kernel(gm_ref, other_ref, slope_ref, wo_ref, wd_ref, do_ref, dz_ref, sum_ref):
    step = pl.program_id(0)

    @pl.when(step == 0)
    def _():
        sum_ref[...] = jnp.zeros_like(sum_ref)

    def use(rows_ref):
        gm = rows_ref[...]
        do_ref[...] = jnp.dot(gm, wo_ref[...], preferred_element_type=F32).astype(BF)
        dz = jnp.dot(gm, wd_ref[...], preferred_element_type=F32) * slope_ref[...].astype(F32)
        dz = dz.astype(BF)
        dz_ref[...] = dz
        sum_ref[0:1] += jnp.sum(dz.astype(F32), axis=0, keepdims=True)

    own = step < pl.num_programs(0) // 2
    pl.when(own)(lambda: use(gm_ref))
    pl.when(jnp.logical_not(own))(lambda: use(other_ref))


def leave_kernel(tok_ref, grad_ref, dz_ref, wq_ref, wu_ref, dh_ref, sum_ref, q_sum_ref):
    @pl.when(pl.program_id(0) == 0)
    def _():
        sum_ref[...] = jnp.zeros_like(sum_ref)
        q_sum_ref[...] = jnp.zeros_like(q_sum_ref)

    cols = grad_ref.shape[2]
    grads = jnp.concatenate([grad_ref[c] for c in range(3)], axis=1)
    dh = dot_nt(dz_ref[...], wu_ref[...]) + dot_nt(grads, wq_ref[...])
    dh_ref[...] = dh.astype(BF)
    xhat = standardized(tok_ref[...])[0]
    sum_ref[0:1] += jnp.sum(dh * xhat, axis=0, keepdims=True)
    sum_ref[1:2] += jnp.sum(dh, axis=0, keepdims=True)
    q_sum_ref[0:1] += jnp.sum(grads.astype(F32), axis=0, keepdims=True)


def row_call(kernel, name, tiles, tiled, whole, outs, sums):
    tile = ROW_TILE

    def spec(width):
        return pl.BlockSpec((tile, width), lambda i: (i, 0))

    in_specs = [s if s is not None else spec(x.shape[1]) for x, s in tiled]
    in_specs += [pl.BlockSpec(x.shape, lambda i: (0, 0)) for x in whole]
    flops = 2 * tiles * tile * sum(x.size for x in whole)
    traffic = 2 * sum(x.size for x in whole) + 2 * sum(x.size for x, _ in tiled) + 4 * tiles * tile * sum(w for w, _ in outs)
    return pl.pallas_call(
        kernel,
        grid=(tiles,),
        in_specs=in_specs,
        out_specs=[spec(w) for w, _ in outs] + [pl.BlockSpec((8, w), lambda i: (0, 0)) for w in sums],
        out_shape=[jax.ShapeDtypeStruct((tiles * tile, w), t) for w, t in outs]
        + [jax.ShapeDtypeStruct((8, w), F32) for w in sums],
        compiler_params=pltpu.CompilerParams(vmem_limit_bytes=VMEM_LIMIT),
        cost_estimate=pl.CostEstimate(flops=flops, bytes_accessed=traffic, transcendentals=0),
        name=name,
    )(*[x for x, _ in tiled], *whole)


def local(
    dp_size, branch_size, tokens, doc_ids, real_rows, cotangent, norm_gain, norm_shift, out_bias,
    w_qkv, b_qkv, w_out, w_up, b_up, w_down,
):
    dp = lax.axis_index("dp")
    branch = lax.axis_index("branch")
    core = dp % 2
    my_rows, width = tokens.shape
    toks = doc_ids.shape[0]
    w_rows = w_qkv.shape[1]
    cols = w_qkv.shape[2] // 2
    hid = w_up.shape[1] // 2
    heads = cols // HEAD_DIM

    my_real = lax.dynamic_slice_in_dim(real_rows, branch * my_rows, my_rows).astype(F32)
    masked_cot = (cotangent.astype(F32) * my_real[:, None]).astype(BF)
    qkv_l = w_qkv.astype(BF).reshape(3, w_rows, 2, cols).transpose(2, 1, 0, 3).reshape(2, w_rows, 3 * cols)
    up_l = w_up.astype(BF).reshape(w_rows, 2, hid).transpose(1, 0, 2)
    out_l = w_out.astype(BF).T.reshape(w_rows, 2, cols).transpose(1, 0, 2)
    down_l = w_down.astype(BF).T.reshape(w_rows, 2, hid).transpose(1, 0, 2)

    small = jnp.concatenate([v.reshape(-1) for v in (norm_gain, norm_shift, out_bias, b_qkv, b_up)]).astype(BF)
    small = jnp.pad(small, (0, -small.size % 128))
    small = jnp.broadcast_to(small[None, None], (2, 16, small.size))

    tok_all, wqkv, wup, wot, wdt, _, params = gather_all(
        dp_size, branch_size, tokens, (qkv_l, up_l, out_l, down_l, small)
    )
    swap = [(i, i + 1 - 2 * (i % 2)) for i in range(dp_size)]
    late_cot, tok_all = lax.optimization_barrier((masked_cot, tok_all))
    gm_own = lax.all_gather(late_cot, "branch", axis=0, tiled=True)
    params = params.reshape(branch_size, dp_size, 16, -1)[:, :, 0].astype(F32)
    sizes = [norm_gain.size, norm_shift.size, out_bias.size, b_qkv.size, b_up.size]
    stops = [sum(sizes[: i + 1]) for i in range(5)]
    gain, shift, bias_full = (
        params[:, :, stops[i] - sizes[i] : stops[i]].transpose(1, 0, 2).reshape(width) for i in range(3)
    )
    mine = lax.dynamic_index_in_dim(params, branch, 0, keepdims=False)
    qkv_b = mine[:, stops[2] : stops[3]].reshape((dp_size,) + b_qkv.shape).transpose(1, 2, 0, 3)
    qkv_b = qkv_b.reshape(3, 2, cols)
    qkv_b = lax.dynamic_index_in_dim(qkv_b, core, 1, keepdims=False).reshape(3 * cols)
    up_b = mine[:, stops[3] : stops[4]].reshape((dp_size,) + b_up.shape).transpose(1, 0, 2).reshape(2, hid)
    up_b = lax.dynamic_index_in_dim(up_b, core, 0, keepdims=False)
    ids = jnp.stack([doc_ids, lax.ppermute(doc_ids, "dp", swap)])

    def row(values):
        return jnp.broadcast_to(values[None], (8, values.size))

    tiles = 2 * toks // ROW_TILE
    h, project, u, slope = row_call(
        enter_kernel, "enter", tiles, [(tok_all, None)], [row(gain), row(shift), wqkv, row(qkv_b), wup, row(up_b)],
        [(width, BF), (3 * cols, F32), (hid, BF), (hid, BF)], [],
    )
    found = [rotary_tables(ids[i]) for i in range(2)]
    begins = jnp.stack([t[0] for t in found])
    tables = [jnp.stack([t[1][i] for t in found]) for i in range(3)]
    queries, keys, values, o, lse_rows = attend(project, begins, tables)
    gm_own, _ = lax.optimization_barrier((gm_own, o))
    gm_other = lax.ppermute(gm_own, "dp", swap)
    half_tiles = tiles // 2

    def branch_out(first):
        def later(width):
            return pl.BlockSpec((ROW_TILE, width), lambda i: (i + first, 0))

        return row_call(
            branch_kernel, "branch_out", half_tiles, [(o, later(cols)), (u, later(hid))], [wot, wdt], [(width, BF)], []
        )[0]

    given = lax.ppermute(branch_out(half_tiles), "dp", swap)
    br = (branch_out(0).astype(F32) + given.astype(F32)).astype(BF)
    xfloat = tokens.astype(F32)

    near = pl.BlockSpec((ROW_TILE, width), lambda i: (jnp.minimum(i, half_tiles - 1), 0))
    far = pl.BlockSpec((ROW_TILE, width), lambda i: (jnp.maximum(i - half_tiles, 0), 0))
    do, dz, up_sums = row_call(
        grad_kernel, "branch_grad", tiles, [(gm_own, near), (gm_other, far), (slope, None)], [wot, wdt],
        [(cols, BF), (hid, BF)], [hid],
    )
    do, br = lax.optimization_barrier((do, br))
    summed = lax.psum_scatter(br, "branch", scatter_dimension=0, tiled=True).astype(F32)
    dqkv = attend_back(queries, keys, values, o, do, lse_rows, begins, tables)
    three = pl.BlockSpec((3, ROW_TILE, cols), lambda i: (0, i, 0))
    dh, token_sums, q_sums = row_call(
        leave_kernel, "leave", tiles, [(tok_all, None), (dqkv, three), (dz, None)], [wqkv, wup],
        [(width, BF)], [width, 3 * cols],
    )

    part = norm_gain.shape[0]
    vectors = jnp.stack(
        [token_sums[0], token_sums[1], jnp.sum(masked_cot, axis=0, dtype=F32)]
    )
    vectors = vectors.reshape(3, dp_size, branch_size * part).transpose(1, 0, 2).reshape(dp_size, -1)
    q_sum = q_sums[0].reshape(3, heads, dp_size, -1).transpose(2, 0, 1, 3).reshape(dp_size, -1)
    u_sum = up_sums[0].reshape(b_up.shape[0] // 2, dp_size, -1).transpose(1, 0, 2)
    u_sum = u_sum.reshape(dp_size, -1)
    sums = jnp.concatenate([vectors, q_sum, u_sum], axis=1)
    ends = (vectors.shape[1], vectors.shape[1] + q_sum.shape[1], sums.shape[1])
    sums = jnp.pad(sums, ((0, 0), (0, 1024 - sums.shape[1]))).reshape(8 * dp_size, 128)

    (g_down, g_out, g_up, g_qkv), dh_mine, total = scatter_all(
        dp_size, branch_size, h, gm_own, gm_other, dqkv, dz, o, u, dh, sums
    )
    dh_mine = dh_mine.astype(F32)
    total = total.reshape(3, 1024)
    block_out = (xfloat + my_real[:, None] * (summed + bias_full)).astype(BF)
    xhat, inverse = standardized(tokens)
    scaled = dh_mine * gain
    input_grad = inverse * (
        scaled
        - jnp.mean(scaled, axis=-1, keepdims=True)
        - xhat * jnp.mean(scaled * xhat, axis=-1, keepdims=True)
    )
    tokens_grad = (cotangent.astype(F32) + input_grad).astype(BF)

    gain_g, shift_g, bias_g = lax.dynamic_slice_in_dim(
        total[2, : ends[0]].reshape(3, branch_size * part), branch * part, part, axis=1
    )
    b_q = total[:2, ends[0] : ends[1]].reshape(2, 3, heads, -1).transpose(1, 0, 2, 3).reshape(b_qkv.shape)
    b_u = total[:2, ends[1] : ends[2]].reshape(b_up.shape)
    return (block_out, tokens_grad, gain_g, shift_g, bias_g, g_qkv, b_q, g_out, g_up, b_u, g_down)


def solution(mesh):
    in_specs = (
        P(("dp", "branch"), None),
        P("dp"),
        P("dp"),
        P(("dp", "branch"), None),
        P(("dp", "branch")),
        P(("dp", "branch")),
        P(("dp", "branch")),
        P(None, "dp", "branch"),
        P(None, "branch", "dp"),
        P("branch", "dp"),
        P("dp", "branch"),
        P("branch", "dp"),
        P("branch", "dp"),
    )
    out_specs = (
        P(("dp", "branch"), None),
        P(("dp", "branch"), None),
        P(("dp", "branch")),
        P(("dp", "branch")),
        P(("dp", "branch")),
        P(None, "dp", "branch"),
        P(None, "branch", "dp"),
        P("branch", "dp"),
        P("dp", "branch"),
        P("branch", "dp"),
        P("branch", "dp"),
    )
    body = functools.partial(local, mesh.shape["dp"], mesh.shape["branch"])
    return jax.shard_map(body, mesh=mesh, in_specs=in_specs, out_specs=out_specs, check_vma=False)
```

```python
import functools
import math

import jax
import jax.numpy as jnp
import numpy as np
from jax import lax
from jax.experimental import pallas as pl
from jax.experimental.pallas import tpu as pltpu
from jax.sharding import PartitionSpec as P

HEAD_DIM = 64
ROT = 32
NORM_EPS = 1e-05
NEGATIVE = -1e30
BF = jnp.bfloat16
F32 = jnp.float32
MESH = pl.DeviceIdType.MESH
VMEM_LIMIT = 48 * 2**20
ROW_TILE = 512
ENTER_VMEM = 48 * 2**20
FIRST_HOP = 2
GATHER_VMEM = 48 * 2**20


def ring_place(group):
    row = group // 2
    return 2 * row + (group + row) % 2


def ring_group(place):
    row = place // 2
    return 2 * row + (place + row) % 2


def chunk_rows(group, half, rows):
    return pl.ds(pl.multiple_of((2 * group + half) * rows, rows), rows)


class Links:
    def __init__(self, dp_size, branch_size):
        self.groups = dp_size // 2
        self.branches = branch_size
        dp = lax.axis_index("dp")
        self.core = dp % 2
        self.other = 1 - self.core
        self.group = dp // 2
        self.place = ring_place(self.group)
        self.branch = lax.axis_index("branch")
        self.sibling = {"dp": 2 * self.group + self.other}
        right = ring_group((self.place + 1) % self.groups)
        left = ring_group((self.place + self.groups - 1) % self.groups)
        self.ring = ({"dp": 2 * right + self.core}, {"dp": 2 * left + self.core})
        self.has_up = self.branch < self.branches - 1
        self.has_down = self.branch > 0
        self.peers = [{"branch": (self.branch + k) % branch_size} for k in range(1, branch_size)]
        self.up = {"branch": self.branch + 1}
        self.down = {"branch": self.branch - 1}

    def meet(self):
        barrier = pltpu.get_barrier_semaphore()

        def greet(device):
            pl.semaphore_signal(barrier, 1, device_id=device, device_id_type=MESH)

        greet(self.sibling)
        greet(self.ring[0])
        greet(self.ring[1])
        for device in self.peers:
            greet(device)
        pl.semaphore_wait(barrier, 3 + len(self.peers))


def remote(src, dst, send, recv, device):
    return pltpu.make_async_remote_copy(
        src_ref=src, dst_ref=dst, send_sem=send, recv_sem=recv, device_id=device, device_id_type=MESH
    )


class WeightRing:
    def __init__(self, at, parts, fulls, sems):
        self.at, self.parts, self.fulls = at, parts, fulls
        self.send, self.recv, self.near_send, self.near_recv, self.local = sems

    def rows(self, w, group, half):
        return self.fulls[w].at[chunk_rows(group, half, self.parts[w].shape[1])]

    def near(self, w):
        at = self.at
        here = self.rows(w, at.group, at.core)
        return remote(self.parts[w].at[at.other], here, self.near_send.at[w], self.near_recv.at[w], at.sibling)

    def own(self, w):
        at = self.at
        return pltpu.make_async_copy(self.parts[w].at[at.core], self.rows(w, at.group, at.core), self.local.at[w])

    def hop(self, w, half, step):
        at = self.at
        shift = step if half == 0 else -step
        part = self.rows(w, ring_group((at.place - shift + at.groups) % at.groups), half)
        return remote(part, part, self.send.at[w, half, step], self.recv.at[w, half, step], at.ring[half])

    def share(self):
        for w in range(len(self.parts)):
            self.near(w).start()
            self.own(w).start()

    def shared(self):
        for w in range(len(self.parts)):
            self.own(w).wait()
            there = self.rows(w, self.at.group, self.at.other)
            remote(there, there, self.near_send.at[w], self.near_recv.at[w], self.at.sibling).wait_recv()

    def step(self, w, step):
        at = self.at
        for half in range(2):
            if step > 0:
                shift = step if half == 0 else -step
                part = self.rows(w, ring_group((at.place - shift + at.groups) % at.groups), half)
                sems = self.send.at[w, half, step - 1], self.recv.at[w, half, step - 1]
                remote(part, part, *sems, at.ring[half]).wait_recv()
            if step < at.groups - 1:
                self.hop(w, half, step).start()

    def drain(self):
        for w in range(len(self.parts)):
            self.near(w).wait_send()
            for half in range(2):
                for step in range(self.at.groups - 1):
                    self.hop(w, half, step).wait_send()


def gather_kernel(dp_size, branch_size, n_w, *refs):
    rows_ref = refs[0]
    w_refs = refs[1 : 1 + n_w]
    full_ref = refs[1 + n_w]
    wf_refs = refs[2 + n_w : 2 + 2 * n_w]
    small_out = refs[2 + 2 * n_w]
    (z_send, z_recv, s_send, s_recv, l_sem, w_send, w_recv, ws_send, ws_recv, wl_sem, p_send, p_recv, p_local) = refs[
        3 + 2 * n_w :
    ]
    at = Links(dp_size, branch_size)
    at.meet()
    rows = rows_ref.shape[0]
    waits = []

    def piece(block, branch):
        start = (block * branch_size + branch) * rows
        return full_ref.at[pl.ds(pl.multiple_of(start, rows), rows)]

    for cond, way, device in ((at.has_up, 0, at.up), (at.has_down, 1, at.down)):
        copy = remote(rows_ref, piece(0, at.branch), z_send.at[way, 0], z_recv.at[at.branch], device)
        pl.when(cond)(copy.start)
        waits.append((cond, copy.wait_send))
    copy = remote(rows_ref, piece(1, at.branch), s_send.at[at.branch], s_recv.at[at.branch], at.sibling)
    copy.start()
    waits.append((None, copy.wait_send))
    own = pltpu.make_async_copy(rows_ref, piece(0, at.branch), l_sem)
    own.start()
    waits.append((None, own.wait))
    ring = WeightRing(at, w_refs, wf_refs, (w_send, w_recv, ws_send, ws_recv, wl_sem))
    ring.share()
    ring.shared()
    for w in range(n_w):
        ring.step(w, 0)

    def line_step(step):
        for way in range(2):
            source = at.branch - step if way == 0 else at.branch + step
            inside = source >= 0 if way == 0 else source < branch_size
            onward = at.has_up if way == 0 else at.has_down
            device = at.up if way == 0 else at.down
            source = jnp.clip(source, 0, branch_size - 1)
            part = piece(0, source)
            forward = remote(part, part, z_send.at[way, step], z_recv.at[source], device)
            across = remote(part, piece(1, source), s_send.at[source], s_recv.at[source], at.sibling)

            @pl.when(inside)
            def _():
                forward.wait_recv()
                pl.when(onward)(forward.start)
                across.start()

            def both(inside=inside, onward=onward, forward=forward, across=across):
                @pl.when(inside)
                def _():
                    pl.when(onward)(forward.wait_send)
                    across.wait_send()

            waits.append((None, both))

    line_steps = list(range(1, branch_size))
    ring_steps = [(w, s) for s in range(1, at.groups) for w in range(n_w)]
    events = [(23.0 * e, 0, e) for e in line_steps]
    events += [((i + 1.0) / len(ring_steps) * 69.0, 1, e) for i, e in enumerate(ring_steps)]
    for _, kind, event in sorted(events, key=lambda e: e[:2]):
        if kind == 0:
            line_step(event)
        else:
            ring.step(*event)
    params = wf_refs[n_w - 1]
    own = pltpu.make_async_copy(params, small_out.at[at.branch], p_local)
    own.start()
    waits.append((None, own.wait))
    for k in range(1, branch_size):
        copy = remote(params, small_out.at[at.branch], p_send.at[k], p_recv.at[k], at.peers[k - 1])
        copy.start()
        waits.append((None, copy.wait_send))
    for k in range(1, branch_size):
        slot = small_out.at[(at.branch - k + branch_size) % branch_size]
        remote(slot, slot, p_send.at[k], p_recv.at[k], at.peers[k - 1]).wait_recv()
    for branch in range(branch_size):
        part = piece(1, branch)
        remote(part, part, s_send.at[branch], s_recv.at[branch], at.sibling).wait_recv()
    ring.drain()
    for cond, wait in waits:
        if cond is None:
            wait()
        else:
            pl.when(cond)(wait)


def gather_all(dp_size, branch_size, array, weights):
    rows, width = array.shape
    n_w = len(weights)
    groups = dp_size // 2
    out_shape = [jax.ShapeDtypeStruct((2 * branch_size * rows, width), BF)]
    out_shape += [jax.ShapeDtypeStruct((dp_size * w.shape[1], w.shape[2]), BF) for w in weights]
    out_shape += [jax.ShapeDtypeStruct((branch_size, dp_size * weights[-1].shape[1], weights[-1].shape[2]), BF)]
    dma = pltpu.SemaphoreType.DMA
    return pl.pallas_call(
        functools.partial(gather_kernel, dp_size, branch_size, n_w),
        out_shape=out_shape,
        in_specs=[pl.BlockSpec(memory_space=pltpu.HBM)] * (1 + n_w),
        out_specs=[pl.BlockSpec(memory_space=pltpu.HBM)] * (2 + n_w),
        scratch_shapes=[
            dma((2, branch_size)),
            dma((branch_size,)),
            dma((branch_size,)),
            dma((branch_size,)),
            dma,
            dma((n_w, 2, groups)),
            dma((n_w, 2, groups)),
            dma((n_w,)),
            dma((n_w,)),
            dma((n_w,)),
            dma((branch_size,)),
            dma((branch_size,)),
            dma,
        ],
        compiler_params=pltpu.CompilerParams(
            collective_id=0, has_side_effects=True, vmem_limit_bytes=GATHER_VMEM
        ),
        cost_estimate=pl.CostEstimate(
            flops=100 * 4 * rows * width * width, bytes_accessed=2 * rows * width, transcendentals=0
        ),
        name="gather_all",
    )(array, *weights)


def scatter_kernel(dp_size, branch_size, *refs):
    n_w = 4
    (h_ref, gm_ref, other_ref, dqkv_ref, dz_ref, o_ref, u_ref, dh_ref, sums_ref) = refs[:9]
    g_refs = refs[9:13]
    tok_out, sum_out, sib_land = refs[13:16]
    slots = refs[16:20]
    got_refs = refs[20:24]
    outs = refs[24:28]
    ins = refs[28:32]
    (own_buf, sib_buf, line_slot, w_send, w_recv, ws_send, ws_recv, z_send, z_recv, s_send, s_recv,
     l_sem, left_buf, x_sem, i_sem, sum_slot, sum_first, sum_got, sum_peer, p_send, p_recv) = refs[32:]
    at = Links(dp_size, branch_size)
    at.meet()
    rows = own_buf.shape[0]
    toks = branch_size * rows
    w_rows = outs[2].shape[2]
    cols = dqkv_ref.shape[2]
    block = left_buf.shape[3]
    lefts = ((gm_ref, other_ref), (h_ref,))
    rights = (u_ref, o_ref, dz_ref, dqkv_ref)
    last = at.groups - 1
    waits = []
    sent = {}

    sib_copy = remote(dh_ref.at[pl.ds(toks, toks)], sib_land, s_send, s_recv, at.sibling)
    sib_copy.start()

    def ring_dest(half, step):
        shift = step + 1 if half == 0 else -step - 1
        return ring_group((at.place - shift + 2 * at.groups) % at.groups)

    def left_copy(a, half, step):
        dest = ring_dest(half, step)
        start = (2 * dest + half) * w_rows if block == w_rows else dest * block
        start = pl.multiple_of(start, block)
        size = left_buf.shape[2] // len(lefts[a])
        return [
            pltpu.make_async_copy(
                ref.at[:, pl.ds(start, block)], left_buf.at[a, half, pl.ds(i * size, size)], x_sem.at[a, half, i]
            )
            for i, ref in enumerate(lefts[a])
        ]

    def product(a, half, w):
        left = left_buf[a, half, :, pl.ds(half * (block - w_rows), w_rows)]

        def dot(right, flip=False):
            pair = (right, left) if flip else (left, right)
            return lax.dot_general(*pair, (((0,), (0,)), ((), ())), preferred_element_type=F32)

        if w < 3:
            return dot(rights[w][...], w < 2)
        return jnp.concatenate([dot(rights[w][c]) for c in range(3)], axis=1)

    def finish(w, values, core):
        if w < 2:
            size = values.shape[0]
            g_refs[w][pl.ds(pl.multiple_of(core * size, size), size), :] = values
        elif w == 2:
            size = values.shape[1]
            g_refs[w][:, pl.ds(pl.multiple_of(core * size, size), size)] = values
        else:
            for c in range(3):
                g_refs[w][c, :, pl.ds(pl.multiple_of(core * cols, cols), cols)] = values[:, c * cols : (c + 1) * cols]

    def ring_piece(a, half, i, step):
        w = 2 * a + i
        if i == 0:
            for load in left_copy(a, half, step):
                load.wait()
        total = product(a, half, w)
        if step > 0:
            slot = slots[w].at[half, step - 1]
            remote(
                slot, slot, w_send.at[w, half, step - 1], w_recv.at[w, half, step - 1], at.ring[half]
            ).wait_recv()
            load = pltpu.make_async_copy(slot, ins[w], i_sem)
            load.start()
            load.wait()
            total = total + ins[w][...].astype(F32)
        if step > 1:
            sent.pop((w, half, step - 2)).wait_send()
        out = outs[w].at[step % 2, half]
        if step < last:
            out[...] = total.astype(BF)
            copy = remote(
                out, slots[w].at[half, step], w_send.at[w, half, step], w_recv.at[w, half, step], at.ring[half]
            )
            copy.start()
            sent[w, half, step] = copy
        else:
            copy = remote(out, got_refs[w], ws_send.at[w], ws_recv.at[w], at.sibling)

            @pl.when(at.core == half)
            def _():
                finish(w, total, at.core)

            @pl.when(at.core != half)
            def _():
                out[...] = total.astype(BF)
                copy.start()

            waits.append(lambda copy=copy, half=half: pl.when(at.core != half)(copy.wait_send))
        if i == 1 and step < last:
            for load in left_copy(a, half, step + 1):
                load.start()

    def sum_step(step):
        for half in range(2):
            total = sums_ref[chunk_rows(ring_dest(half, step), half, 8)]
            if step > 0:
                slot = sum_slot.at[half, step - 1]
                remote(
                    slot, slot, w_send.at[n_w, half, step - 1], w_recv.at[n_w, half, step - 1], at.ring[half]
                ).wait_recv()
                total = total + slot[...]
            out = sum_first.at[step, half]
            out[...] = total
            if step < last:
                copy = remote(
                    out, sum_slot.at[half, step], w_send.at[n_w, half, step], w_recv.at[n_w, half, step], at.ring[half]
                )
                copy.start()
                waits.append(copy.wait_send)
        if step == last:
            copy = remote(sum_first.at[last, at.other], sum_got, ws_send.at[n_w], ws_recv.at[n_w], at.sibling)
            copy.start()
            copy.wait()
            mine = sum_peer.at[0]
            mine[...] = sum_first[last, at.core] + sum_got[...]
            sum_out[at.core] = sum_first[last, at.core]
            sum_out[at.other] = sum_got[...]
            for k in range(1, branch_size):
                copy = remote(mine, sum_peer.at[k], p_send.at[k], p_recv.at[k], at.peers[k - 1])
                copy.start()
                waits.append(copy.wait_send)

    def sum_end():
        total = sum_peer[0]
        for k in range(1, branch_size):
            remote(sum_peer.at[0], sum_peer.at[k], p_send.at[k], p_recv.at[k], at.peers[k - 1]).wait_recv()
            total = total + sum_peer[k]
        sum_out[2] = total

    def load_own(d):
        own = pltpu.make_async_copy(dh_ref.at[pl.ds(d * rows, rows)], own_buf, l_sem.at[0])
        sib = pltpu.make_async_copy(sib_land.at[pl.ds(d * rows, rows)], sib_buf, l_sem.at[1])
        own.start()
        sib.start()
        own.wait()
        sib.wait()

    def line_step(slot_time):
        far = branch_size - 1 - slot_time
        for way in range(2):
            d = at.branch + far if way == 0 else at.branch - far
            going = d < branch_size if way == 0 else d >= 0
            more = at.has_down if way == 0 else at.has_up
            device = at.up if way == 0 else at.down
            slot = line_slot.at[way, d - 1 + way]
            passing = remote(slot, slot, z_send.at[way, d], z_recv.at[way, d], device)

            @pl.when(going)
            def _():
                load_own(d)
                total = own_buf[...].astype(F32) + sib_buf[...].astype(F32)

                @pl.when(more)
                def _():
                    passing.wait_recv()
                    slot[...] = (total + slot[...].astype(F32)).astype(BF)

                @pl.when(jnp.logical_not(more))
                def _():
                    slot[...] = total.astype(BF)

                passing.start()

            waits.append(lambda going=going, passing=passing: pl.when(going)(passing.wait_send))

    def line_end():
        d = at.branch
        load_own(d)
        for way in range(2):
            more = at.has_down if way == 0 else at.has_up
            slot = line_slot.at[way, d - 1 + way]
            device = at.up if way == 0 else at.down

            @pl.when(more)
            def _():
                remote(slot, slot, z_send.at[way, d], z_recv.at[way, d], device).wait_recv()

        below, above = (
            jnp.where(at.has_down, line_slot[0, jnp.maximum(d - 1, 0)].astype(F32), 0.0),
            jnp.where(at.has_up, line_slot[1, jnp.minimum(d, branch_size - 2)].astype(F32), 0.0),
        )
        tok_out[...] = (own_buf[...].astype(F32) + sib_buf[...].astype(F32) + below + above).astype(BF)

    for a in range(2):
        for half in range(2):
            for load in left_copy(a, half, 0):
                load.start()
    sum_step(0)
    pieces = [(a, half, i) for a in range(2) for half in range(2) for i in range(2)]
    size = [rights[2 * a + i].shape[-1] * (1 + a * i * 2) for a, half, i in pieces]
    due = [sum(size[: i + 1]) / sum(size) for i in range(len(pieces))]
    period = 34.0
    events = [(period * (s - 1 + f) + 4.0, 1, (*p, s)) for s in range(1, at.groups) for p, f in zip(pieces, due)]
    events += [(2.0 * i, 1, (*p, 0)) for i, p in enumerate(pieces)]
    events += [(9.0 + 24.0 * k, 0, k) for k in range(branch_size)]
    events += [(10.0 + 12.0 * s, 2, s) for s in range(1, at.groups)]
    events += [(18.0 + 12.0 * at.groups, 3, 0)]
    for _, kind, event in sorted(events, key=lambda e: e[:2]):
        if kind == 0 and event == 0:
            sib_copy.wait_recv()
        if kind == 0 and event == branch_size - 1:
            line_end()
        elif kind == 0:
            line_step(event)
        elif kind == 1:
            ring_piece(*event)
        elif kind == 2:
            sum_step(event)
        else:
            sum_end()
    for w in range(n_w):
        remote(outs[w].at[0, 0], got_refs[w], ws_send.at[w], ws_recv.at[w], at.sibling).wait_recv()
        finish(w, got_refs[w][...].astype(F32), at.other)
    sib_copy.wait_send()
    for copy in sent.values():
        copy.wait_send()
    for wait in waits:
        wait()


def scatter_all(dp_size, branch_size, h, gm, gm_other, dqkv, dz, o, u, dh, sums):
    widths = [u.shape[1], o.shape[1], dz.shape[1], 3 * dqkv.shape[2]]
    width = h.shape[1]
    w_rows = width // dp_size
    groups = dp_size // 2
    toks = h.shape[0] // 2
    rows = toks // branch_size
    n_w = 4
    dma = pltpu.SemaphoreType.DMA
    vm = pl.BlockSpec(memory_space=pltpu.VMEM)
    hb = pl.BlockSpec(memory_space=pltpu.HBM)
    shapes = [(widths[0], w_rows), (widths[1], w_rows), (w_rows, widths[2]), (w_rows, widths[3])]
    out_shape = [
        jax.ShapeDtypeStruct((2 * widths[0], w_rows), F32),
        jax.ShapeDtypeStruct((2 * widths[1], w_rows), F32),
        jax.ShapeDtypeStruct((w_rows, 2 * widths[2]), F32),
        jax.ShapeDtypeStruct((3, w_rows, 2 * dqkv.shape[2]), F32),
    ]
    out_shape += [jax.ShapeDtypeStruct((rows, width), BF), jax.ShapeDtypeStruct((3, 8, 128), F32)]
    out_shape += [jax.ShapeDtypeStruct((toks, width), BF)]
    out_shape += [jax.ShapeDtypeStruct((2, groups - 1) + shape, BF) for shape in shapes]
    out = pl.pallas_call(
        functools.partial(scatter_kernel, dp_size, branch_size),
        out_shape=out_shape,
        in_specs=[hb] * 3 + [vm] * 4 + [hb, vm],
        out_specs=[vm] * 6 + [hb] * 5,
        scratch_shapes=[pltpu.VMEM(shape, BF) for shape in shapes]
        + [pltpu.VMEM((2, 2) + shape, BF) for shape in shapes]
        + [pltpu.VMEM(shape, BF) for shape in shapes]
        + [
            pltpu.VMEM((rows, width), BF),
            pltpu.VMEM((rows, width), BF),
            pltpu.VMEM((2, branch_size - 1, rows, width), BF),
            dma((n_w + 1, 2, groups)),
            dma((n_w + 1, 2, groups)),
            dma((n_w + 1,)),
            dma((n_w + 1,)),
            dma((2, branch_size)),
            dma((2, branch_size)),
            dma(()),
            dma(()),
            dma((2,)),
            pltpu.VMEM((2, 2, 2 * toks, w_rows if w_rows % 128 == 0 else 2 * w_rows), BF),
            dma((2, 2, 2)),
            dma(()),
            pltpu.VMEM((2, groups - 1, 8, 128), F32),
            pltpu.VMEM((groups, 2, 8, 128), F32),
            pltpu.VMEM((8, 128), F32),
            pltpu.VMEM((branch_size, 8, 128), F32),
            dma((branch_size,)),
            dma((branch_size,)),
        ],
        compiler_params=pltpu.CompilerParams(
            collective_id=1, has_side_effects=True, vmem_limit_bytes=VMEM_LIMIT
        ),
        cost_estimate=pl.CostEstimate(
            flops=4 * toks * width * sum(widths), bytes_accessed=2 * toks * width, transcendentals=0
        ),
        name="scatter_all",
    )(h, gm, gm_other, dqkv, dz, o, u, dh, sums)
    return out[:4], out[4], out[5]


def turn(values, tables, sign):
    fixed, from_low, from_high = tables
    half = ROT // 2
    return (
        values * fixed
        + sign * (pltpu.roll(values, half, 1) * from_low + pltpu.roll(values, 2 * HEAD_DIM - half, 1) * from_high)
    )


def score_tile(keys, queries, begins, first, q_tile):
    scores = lax.dot_general(keys, queries, (((1,), (1,)), ((), ())), preferred_element_type=F32)
    key_at = lax.broadcasted_iota(jnp.int32, scores.shape, 0)
    query_at = first + lax.broadcasted_iota(jnp.int32, scores.shape, 1)
    allowed = jnp.logical_and(key_at >= begins, key_at <= query_at)
    return jnp.where(allowed, scores, NEGATIVE)


def attend_kernel(q_tile, q_ref, k_ref, v_ref, begin_ref, fixed_ref, low_ref, high_ref, qr_ref, kr_ref, vr_ref, o_ref, lse_ref):
    tables = (fixed_ref[0], low_ref[0], high_ref[0])
    qr_ref[...] = (turn(q_ref[...], tables, 1.0) * (HEAD_DIM**-0.5)).astype(BF)
    kr_ref[...] = turn(k_ref[...], tables, 1.0).astype(BF)
    vr_ref[...] = v_ref[...].astype(BF)
    toks = q_ref.shape[0]
    for first in range(0, toks, q_tile):
        span = first + q_tile
        begins = begin_ref[0, 0:1, first:span]
        outs = []
        for head in range(2):
            lanes = slice(head * HEAD_DIM, (head + 1) * HEAD_DIM)
            scores = score_tile(kr_ref[:span, lanes], qr_ref[first:span, lanes], begins, first, q_tile)
            top = jnp.max(scores, axis=0, keepdims=True)
            weights = jnp.exp(scores - top)
            total = jnp.sum(weights, axis=0, keepdims=True)
            lse_ref[0, 0, head : head + 1, first:span] = top + jnp.log(total)
            mixed = lax.dot_general(
                vr_ref[:span, lanes], weights.astype(BF), (((0,), (0,)), ((), ())), preferred_element_type=F32
            )
            outs.append(mixed / total)
        o_ref[first:span, :] = jnp.concatenate(outs, axis=0).T.astype(BF)


def attend_back_kernel(
    q_tile, qr_ref, kr_ref, vr_ref, o_ref, do_ref, lse_ref, begin_ref, fixed_ref, low_ref, high_ref, grad_ref, k_acc, v_acc
):
    tables = (fixed_ref[0], low_ref[0], high_ref[0])
    toks = qr_ref.shape[0]
    k_acc[...] = jnp.zeros_like(k_acc)
    v_acc[...] = jnp.zeros_like(v_acc)
    for first in range(0, toks, q_tile):
        span = first + q_tile
        begins = begin_ref[0, 0:1, first:span]
        both = (do_ref[first:span, :].astype(F32) * o_ref[first:span, :].astype(F32)).T
        turned = []
        for head in range(2):
            lanes = slice(head * HEAD_DIM, (head + 1) * HEAD_DIM)
            delta = jnp.sum(both[lanes], axis=0, keepdims=True)
            queries = qr_ref[first:span, lanes]
            grads = do_ref[first:span, lanes]
            keys = kr_ref[:span, lanes]
            scores = score_tile(keys, queries, begins, first, q_tile)
            prob = jnp.exp(scores - lse_ref[0, 0, head : head + 1, first:span])
            v_acc[head, :span, :] += jnp.dot(prob.astype(BF), grads, preferred_element_type=F32)
            dprob = lax.dot_general(
                vr_ref[:span, lanes], grads, (((1,), (1,)), ((), ())), preferred_element_type=F32
            )
            ds = (prob * (dprob - delta)).astype(BF)
            k_acc[head, :span, :] += jnp.dot(ds, queries, preferred_element_type=F32)
            turned.append(
                lax.dot_general(keys, ds, (((0,), (0,)), ((), ())), preferred_element_type=F32)
            )
        dq = jnp.concatenate(turned, axis=0).T * (HEAD_DIM**-0.5)
        grad_ref[0, first:span, :] = turn(dq, tuple(t[first:span] for t in tables), -1.0).astype(BF)
    dk = jnp.concatenate([k_acc[0], k_acc[1]], axis=1)
    grad_ref[1] = turn(dk, tables, -1.0).astype(BF)
    grad_ref[2] = jnp.concatenate([v_acc[0], v_acc[1]], axis=1).astype(BF)


def attention_specs(toks, pairs):
    wide = 2 * HEAD_DIM

    def cols(shift):
        return pl.BlockSpec((toks, wide), lambda i, j: (i, j + shift * pairs))

    begin = pl.BlockSpec((1, 8, toks), lambda i, j: (i, 0, 0))
    table = pl.BlockSpec((1, toks, wide), lambda i, j: (i, 0, 0))
    lse = pl.BlockSpec((1, 1, 2, toks), lambda i, j: (i, j, 0, 0))
    return cols, begin, table, lse


def attend(project, begins, tables):
    blocks, _, toks = begins.shape
    pairs = project.shape[1] // (6 * HEAD_DIM)
    cols, begin, table, lse = attention_specs(toks, pairs)
    narrow = jax.ShapeDtypeStruct((blocks * toks, pairs * 2 * HEAD_DIM), BF)
    return pl.pallas_call(
        functools.partial(attend_kernel, min(256, toks)),
        grid=(blocks, pairs),
        in_specs=[cols(0), cols(1), cols(2), begin] + [table] * 3,
        out_specs=[cols(0)] * 4 + [lse],
        out_shape=[narrow] * 4 + [jax.ShapeDtypeStruct((blocks, pairs, 2, toks), F32)],
        compiler_params=pltpu.CompilerParams(vmem_limit_bytes=60 * 2**20),
        name="attend",
    )(project, project, project, begins, *tables)


def attend_back(queries, keys, values, o, do, lse_rows, begins, tables):
    blocks, _, toks = begins.shape
    pairs = queries.shape[1] // (2 * HEAD_DIM)
    cols, begin, table, lse = attention_specs(toks, pairs)
    acc = pltpu.VMEM((2, toks, HEAD_DIM), F32)
    return pl.pallas_call(
        functools.partial(attend_back_kernel, min(256, toks)),
        grid=(blocks, pairs),
        in_specs=[cols(0)] * 5 + [lse, begin] + [table] * 3,
        out_specs=pl.BlockSpec((3, toks, 2 * HEAD_DIM), lambda i, j: (0, i, j)),
        out_shape=jax.ShapeDtypeStruct((3,) + queries.shape, BF),
        scratch_shapes=[acc, acc],
        compiler_params=pltpu.CompilerParams(vmem_limit_bytes=60 * 2**20),
        name="attend_back",
    )(queries, keys, values, o, do, lse_rows, begins, *tables)


def rotary_tables(doc_rows):
    row_count = doc_rows.shape[0]
    row_index = jnp.arange(row_count, dtype=jnp.int32)
    same = doc_rows[:, None] == doc_rows[None, :]
    begins = jnp.min(jnp.where(same, row_index[:, None], row_count), axis=0)
    places = (row_index - begins).astype(F32)
    half = ROT // 2
    lane = np.arange(2 * HEAD_DIM) % HEAD_DIM
    turning = lane < ROT
    frequency = np.where(turning, 10000.0 ** (-2.0 * (lane % half) / ROT), 0.0).astype(np.float32)
    angles = places[:, None] * frequency[None, :]
    sine = jnp.sin(angles)
    from_low = sine * np.where(turning & (lane >= half), 1.0, 0.0).astype(np.float32)
    from_high = sine * np.where(lane < half, -1.0, 0.0).astype(np.float32)
    return jnp.broadcast_to(begins[None], (8, row_count)), (jnp.cos(angles), from_low, from_high)


def dot_nt(left, right):
    return lax.dot_general(left, right, (((1,), (1,)), ((), ())), preferred_element_type=F32)


def standardized(rows):
    xfloat = rows.astype(F32)
    removed = xfloat - jnp.mean(xfloat, axis=-1, keepdims=True)
    inverse = lax.rsqrt(jnp.mean(removed * removed, axis=-1, keepdims=True) + NORM_EPS)
    return removed * inverse, inverse


def enter_kernel(
    dp_size, branch_size, tok_ref, gain_ref, shift_ref, wq_ref, qb_ref, wu_ref, ub_ref, part_ref,
    h_ref, project_ref, u_ref, slope_ref, full_ref, *sems,
):
    tile_at, tiles = pl.program_id(0), pl.num_programs(0)
    at = Links(dp_size, branch_size)
    ring = WeightRing(at, [part_ref], [full_ref], sems)

    @pl.when(tile_at == 0)
    def _():
        at.meet()
        ring.share()
        ring.shared()
        ring.step(0, 0)

    pl.when(tile_at == FIRST_HOP)(lambda: ring.step(0, 1))

    h = (standardized(tok_ref[...])[0] * gain_ref[0:1] + shift_ref[0:1]).astype(BF)
    h_ref[...] = h
    project_ref[...] = jnp.dot(h, wq_ref[...], preferred_element_type=F32) + qb_ref[0:1]
    z = jnp.dot(h, wu_ref[...], preferred_element_type=F32) + ub_ref[0:1]
    scale, cubic = math.sqrt(2.0 / math.pi), 0.044715
    square = z * z
    bent = jnp.tanh(scale * z * (1.0 + cubic * square))
    half = 0.5 * (1.0 + bent)
    u_ref[...] = (z * half).astype(BF)
    slope = half + 0.5 * z * (1.0 - bent * bent) * (scale * (1.0 + 3.0 * cubic * square))
    slope_ref[...] = slope.astype(BF)

    @pl.when(tile_at == tiles - 1)
    def _():
        for step in range(2, at.groups):
            ring.step(0, step)
        ring.drain()


def enter(dp_size, branch_size, tok_all, gain, shift, wqkv, qkv_b, wup, up_b, part):
    total, width = tok_all.shape
    groups = dp_size // 2
    tile = ROW_TILE
    dma = pltpu.SemaphoreType.DMA

    def spec(width):
        return pl.BlockSpec((tile, width), lambda i: (i, 0))

    whole = (gain, shift, wqkv, qkv_b, wup, up_b)
    outs = [(width, BF), (wqkv.shape[1], F32), (wup.shape[1], BF), (wup.shape[1], BF)]
    far = pl.BlockSpec(memory_space=pltpu.HBM)
    return pl.pallas_call(
        functools.partial(enter_kernel, dp_size, branch_size),
        grid=(total // tile,),
        in_specs=[spec(width)] + [pl.BlockSpec(x.shape, lambda i: (0, 0)) for x in whole] + [far],
        out_specs=[spec(w) for w, _ in outs] + [far],
        out_shape=[jax.ShapeDtypeStruct((total, w), t) for w, t in outs]
        + [jax.ShapeDtypeStruct((dp_size * part.shape[1], part.shape[2]), BF)],
        scratch_shapes=[dma((1, 2, groups)), dma((1, 2, groups)), dma((1,)), dma((1,)), dma((1,))],
        compiler_params=pltpu.CompilerParams(
            collective_id=2, has_side_effects=True, vmem_limit_bytes=ENTER_VMEM
        ),
        cost_estimate=pl.CostEstimate(
            flops=2 * total * (wqkv.size + wup.size), bytes_accessed=2 * total * width, transcendentals=0
        ),
        name="enter",
    )(tok_all, *whole, part)


def branch_kernel(o_ref, u_ref, *refs):
    more, (wo_ref, wd_ref, br_ref) = refs[:-3], refs[-3:]
    total = dot_nt(o_ref[...], wo_ref[...]) + dot_nt(u_ref[...], wd_ref[...])
    for ref in more:
        total = total + ref[...].astype(F32)
    br_ref[...] = total.astype(BF)


def grad_kernel(gm_ref, other_ref, slope_ref, wo_ref, wd_ref, do_ref, dz_ref, sum_ref):
    step = pl.program_id(0)

    @pl.when(step == 0)
    def _():
        sum_ref[...] = jnp.zeros_like(sum_ref)

    def use(rows_ref):
        gm = rows_ref[...]
        do_ref[...] = jnp.dot(gm, wo_ref[...], preferred_element_type=F32).astype(BF)
        dz = jnp.dot(gm, wd_ref[...], preferred_element_type=F32) * slope_ref[...].astype(F32)
        dz = dz.astype(BF)
        dz_ref[...] = dz
        sum_ref[0:1] += jnp.sum(dz.astype(F32), axis=0, keepdims=True)

    own = step < pl.num_programs(0) // 2
    pl.when(own)(lambda: use(gm_ref))
    pl.when(jnp.logical_not(own))(lambda: use(other_ref))


def leave_kernel(tok_ref, grad_ref, dz_ref, wq_ref, wu_ref, dh_ref, sum_ref, q_sum_ref):
    @pl.when(pl.program_id(0) == 0)
    def _():
        sum_ref[...] = jnp.zeros_like(sum_ref)
        q_sum_ref[...] = jnp.zeros_like(q_sum_ref)

    cols = grad_ref.shape[2]
    grads = jnp.concatenate([grad_ref[c] for c in range(3)], axis=1)
    dh = dot_nt(dz_ref[...], wu_ref[...]) + dot_nt(grads, wq_ref[...])
    dh_ref[...] = dh.astype(BF)
    xhat = standardized(tok_ref[...])[0]
    sum_ref[0:1] += jnp.sum(dh * xhat, axis=0, keepdims=True)
    sum_ref[1:2] += jnp.sum(dh, axis=0, keepdims=True)
    q_sum_ref[0:1] += jnp.sum(grads.astype(F32), axis=0, keepdims=True)


def row_call(kernel, name, tiles, tiled, whole, outs, sums):
    tile = ROW_TILE

    def spec(width):
        return pl.BlockSpec((tile, width), lambda i: (i, 0))

    in_specs = [s if s is not None else spec(x.shape[1]) for x, s in tiled]
    in_specs += [pl.BlockSpec(x.shape, lambda i: (0, 0)) for x in whole]
    flops = 2 * tiles * tile * sum(x.size for x in whole)
    traffic = 2 * sum(x.size for x in whole) + 2 * sum(x.size for x, _ in tiled) + 4 * tiles * tile * sum(w for w, _ in outs)
    return pl.pallas_call(
        kernel,
        grid=(tiles,),
        in_specs=in_specs,
        out_specs=[spec(w) for w, _ in outs] + [pl.BlockSpec((8, w), lambda i: (0, 0)) for w in sums],
        out_shape=[jax.ShapeDtypeStruct((tiles * tile, w), t) for w, t in outs]
        + [jax.ShapeDtypeStruct((8, w), F32) for w in sums],
        compiler_params=pltpu.CompilerParams(vmem_limit_bytes=60 * 2**20),
        cost_estimate=pl.CostEstimate(flops=flops, bytes_accessed=traffic, transcendentals=0),
        name=name,
    )(*[x for x, _ in tiled], *whole)


def local(
    dp_size, branch_size, tokens, doc_ids, real_rows, cotangent, norm_gain, norm_shift, out_bias,
    w_qkv, b_qkv, w_out, w_up, b_up, w_down,
):
    dp = lax.axis_index("dp")
    branch = lax.axis_index("branch")
    core = dp % 2
    my_rows, width = tokens.shape
    toks = doc_ids.shape[0]
    w_rows = w_qkv.shape[1]
    cols = w_qkv.shape[2] // 2
    hid = w_up.shape[1] // 2
    heads = cols // HEAD_DIM

    my_real = lax.dynamic_slice_in_dim(real_rows, branch * my_rows, my_rows).astype(F32)
    masked_cot = (cotangent.astype(F32) * my_real[:, None]).astype(BF)
    qkv_l = w_qkv.astype(BF).reshape(3, w_rows, 2, cols).transpose(2, 1, 0, 3).reshape(2, w_rows, 3 * cols)
    up_l = w_up.astype(BF).reshape(w_rows, 2, hid).transpose(1, 0, 2)
    out_l = w_out.astype(BF).T.reshape(w_rows, 2, cols).transpose(1, 0, 2)
    down_l = w_down.astype(BF).T.reshape(w_rows, 2, hid).transpose(1, 0, 2)

    small = jnp.concatenate([v.reshape(-1) for v in (norm_gain, norm_shift, out_bias, b_qkv, b_up)]).astype(BF)
    small = jnp.pad(small, (0, -small.size % 128))
    small = jnp.broadcast_to(small[None, None], (2, 16, small.size))

    tok_all, wqkv, wup, wot, _, params = gather_all(
        dp_size, branch_size, tokens, (qkv_l, up_l, out_l, small)
    )
    swap = [(i, i + 1 - 2 * (i % 2)) for i in range(dp_size)]
    late_cot, tok_all = lax.optimization_barrier((masked_cot, tok_all))
    gm_own = lax.all_gather(late_cot, "branch", axis=0, tiled=True)
    params = params.reshape(branch_size, dp_size, 16, -1)[:, :, 0].astype(F32)
    sizes = [norm_gain.size, norm_shift.size, out_bias.size, b_qkv.size, b_up.size]
    stops = [sum(sizes[: i + 1]) for i in range(5)]
    gain, shift, bias_full = (
        params[:, :, stops[i] - sizes[i] : stops[i]].transpose(1, 0, 2).reshape(width) for i in range(3)
    )
    mine = lax.dynamic_index_in_dim(params, branch, 0, keepdims=False)
    qkv_b = mine[:, stops[2] : stops[3]].reshape((dp_size,) + b_qkv.shape).transpose(1, 2, 0, 3)
    qkv_b = qkv_b.reshape(3, 2, cols)
    qkv_b = lax.dynamic_index_in_dim(qkv_b, core, 1, keepdims=False).reshape(3 * cols)
    up_b = mine[:, stops[3] : stops[4]].reshape((dp_size,) + b_up.shape).transpose(1, 0, 2).reshape(2, hid)
    up_b = lax.dynamic_index_in_dim(up_b, core, 0, keepdims=False)
    ids = jnp.stack([doc_ids, lax.ppermute(doc_ids, "dp", swap)])

    def row(values):
        return jnp.broadcast_to(values[None], (8, values.size))

    tiles = 2 * toks // ROW_TILE
    h, project, u, slope, wdt = enter(
        dp_size, branch_size, tok_all, row(gain), row(shift), wqkv, row(qkv_b), wup, row(up_b), down_l
    )
    found = [rotary_tables(ids[i]) for i in range(2)]
    begins = jnp.stack([t[0] for t in found])
    tables = [jnp.stack([t[1][i] for t in found]) for i in range(3)]
    queries, keys, values, o, lse_rows = attend(project, begins, tables)
    gm_own, _ = lax.optimization_barrier((gm_own, o))
    gm_other = lax.ppermute(gm_own, "dp", swap)
    half_tiles = tiles // 2

    def branch_out(first, *more):
        def later(width):
            return pl.BlockSpec((ROW_TILE, width), lambda i: (i + first, 0))

        tiled = [(o, later(cols)), (u, later(hid))] + [(x, None) for x in more]
        return row_call(branch_kernel, "branch_out", half_tiles, tiled, [wot, wdt], [(width, BF)], [])[0]

    given = lax.ppermute(branch_out(half_tiles), "dp", swap)
    xfloat = tokens.astype(F32)

    near = pl.BlockSpec((ROW_TILE, width), lambda i: (jnp.minimum(i, half_tiles - 1), 0))
    far = pl.BlockSpec((ROW_TILE, width), lambda i: (jnp.maximum(i - half_tiles, 0), 0))
    do, dz, up_sums = row_call(
        grad_kernel, "branch_grad", tiles, [(gm_own, near), (gm_other, far), (slope, None)], [wot, wdt],
        [(cols, BF), (hid, BF)], [hid],
    )
    do, given = lax.optimization_barrier((do, given))
    br = branch_out(0, given)
    do, br = lax.optimization_barrier((do, br))
    summed = lax.psum_scatter(br, "branch", scatter_dimension=0, tiled=True).astype(F32)
    dqkv = attend_back(queries, keys, values, o, do, lse_rows, begins, tables)
    three = pl.BlockSpec((3, ROW_TILE, cols), lambda i: (0, i, 0))
    dh, token_sums, q_sums = row_call(
        leave_kernel, "leave", tiles, [(tok_all, None), (dqkv, three), (dz, None)], [wqkv, wup],
        [(width, BF)], [width, 3 * cols],
    )

    part = norm_gain.shape[0]
    vectors = jnp.stack(
        [token_sums[0], token_sums[1], jnp.sum(masked_cot, axis=0, dtype=F32)]
    )
    vectors = vectors.reshape(3, dp_size, branch_size * part).transpose(1, 0, 2).reshape(dp_size, -1)
    q_sum = q_sums[0].reshape(3, heads, dp_size, -1).transpose(2, 0, 1, 3).reshape(dp_size, -1)
    u_sum = up_sums[0].reshape(b_up.shape[0] // 2, dp_size, -1).transpose(1, 0, 2)
    u_sum = u_sum.reshape(dp_size, -1)
    sums = jnp.concatenate([vectors, q_sum, u_sum], axis=1)
    ends = (vectors.shape[1], vectors.shape[1] + q_sum.shape[1], sums.shape[1])
    sums = jnp.pad(sums, ((0, 0), (0, 1024 - sums.shape[1]))).reshape(8 * dp_size, 128)

    (g_down, g_out, g_up, g_qkv), dh_mine, total = scatter_all(
        dp_size, branch_size, h, gm_own, gm_other, dqkv, dz, o, u, dh, sums
    )
    dh_mine = dh_mine.astype(F32)
    total = total.reshape(3, 1024)
    block_out = (xfloat + my_real[:, None] * (summed + bias_full)).astype(BF)
    xhat, inverse = standardized(tokens)
    scaled = dh_mine * gain
    input_grad = inverse * (
        scaled
        - jnp.mean(scaled, axis=-1, keepdims=True)
        - xhat * jnp.mean(scaled * xhat, axis=-1, keepdims=True)
    )
    tokens_grad = (cotangent.astype(F32) + input_grad).astype(BF)

    gain_g, shift_g, bias_g = lax.dynamic_slice_in_dim(
        total[2, : ends[0]].reshape(3, branch_size * part), branch * part, part, axis=1
    )
    b_q = total[:2, ends[0] : ends[1]].reshape(2, 3, heads, -1).transpose(1, 0, 2, 3).reshape(b_qkv.shape)
    b_u = total[:2, ends[1] : ends[2]].reshape(b_up.shape)
    return (block_out, tokens_grad, gain_g, shift_g, bias_g, g_qkv, b_q, g_out, g_up, b_u, g_down)


def solution(mesh):
    in_specs = (
        P(("dp", "branch"), None),
        P("dp"),
        P("dp"),
        P(("dp", "branch"), None),
        P(("dp", "branch")),
        P(("dp", "branch")),
        P(("dp", "branch")),
        P(None, "dp", "branch"),
        P(None, "branch", "dp"),
        P("branch", "dp"),
        P("dp", "branch"),
        P("branch", "dp"),
        P("branch", "dp"),
    )
    out_specs = (
        P(("dp", "branch"), None),
        P(("dp", "branch"), None),
        P(("dp", "branch")),
        P(("dp", "branch")),
        P(("dp", "branch")),
        P(None, "dp", "branch"),
        P(None, "branch", "dp"),
        P("branch", "dp"),
        P("dp", "branch"),
        P("branch", "dp"),
        P("branch", "dp"),
    )
    body = functools.partial(local, mesh.shape["dp"], mesh.shape["branch"])
    return jax.shard_map(body, mesh=mesh, in_specs=in_specs, out_specs=out_specs, check_vma=False)
```

```python
import functools
import math

import jax
import jax.numpy as jnp
import numpy as np
from jax import lax
from jax.experimental import pallas as pl
from jax.experimental.pallas import tpu as pltpu
from jax.sharding import PartitionSpec as P

HEAD_DIM = 64
ROT = 32
NORM_EPS = 1e-05
NEGATIVE = -1e30
BF = jnp.bfloat16
F32 = jnp.float32
MESH = pl.DeviceIdType.MESH
VMEM_LIMIT = 48 * 2**20
ROW_TILE = 512
ENTER_VMEM = 48 * 2**20
FIRST_HOP = 2
GATHER_VMEM = 48 * 2**20


def ring_place(group):
    row = group // 2
    return 2 * row + (group + row) % 2


def ring_group(place):
    row = place // 2
    return 2 * row + (place + row) % 2


def chunk_rows(group, half, rows):
    return pl.ds(pl.multiple_of((2 * group + half) * rows, rows), rows)


class Links:
    def __init__(self, dp_size, branch_size):
        self.groups = dp_size // 2
        self.branches = branch_size
        dp = lax.axis_index("dp")
        self.core = dp % 2
        self.other = 1 - self.core
        self.group = dp // 2
        self.place = ring_place(self.group)
        self.branch = lax.axis_index("branch")
        self.sibling = {"dp": 2 * self.group + self.other}
        right = ring_group((self.place + 1) % self.groups)
        left = ring_group((self.place + self.groups - 1) % self.groups)
        self.ring = ({"dp": 2 * right + self.core}, {"dp": 2 * left + self.core})
        self.has_up = self.branch < self.branches - 1
        self.has_down = self.branch > 0
        self.peers = [{"branch": (self.branch + k) % branch_size} for k in range(1, branch_size)]
        self.up = {"branch": self.branch + 1}
        self.down = {"branch": self.branch - 1}

    def meet(self):
        barrier = pltpu.get_barrier_semaphore()

        def greet(device):
            pl.semaphore_signal(barrier, 1, device_id=device, device_id_type=MESH)

        greet(self.sibling)
        greet(self.ring[0])
        greet(self.ring[1])
        for device in self.peers:
            greet(device)
        pl.semaphore_wait(barrier, 3 + len(self.peers))


def remote(src, dst, send, recv, device):
    return pltpu.make_async_remote_copy(
        src_ref=src, dst_ref=dst, send_sem=send, recv_sem=recv, device_id=device, device_id_type=MESH
    )


class WeightRing:
    def __init__(self, at, parts, fulls, sems):
        self.at, self.parts, self.fulls = at, parts, fulls
        self.send, self.recv, self.near_send, self.near_recv, self.local = sems

    def rows(self, w, group, half):
        return self.fulls[w].at[chunk_rows(group, half, self.parts[w].shape[1])]

    def near(self, w):
        at = self.at
        here = self.rows(w, at.group, at.core)
        return remote(self.parts[w].at[at.other], here, self.near_send.at[w], self.near_recv.at[w], at.sibling)

    def own(self, w):
        at = self.at
        return pltpu.make_async_copy(self.parts[w].at[at.core], self.rows(w, at.group, at.core), self.local.at[w])

    def hop(self, w, half, step):
        at = self.at
        shift = step if half == 0 else -step
        part = self.rows(w, ring_group((at.place - shift + at.groups) % at.groups), half)
        return remote(part, part, self.send.at[w, half, step], self.recv.at[w, half, step], at.ring[half])

    def share(self):
        for w in range(len(self.parts)):
            self.near(w).start()
            self.own(w).start()

    def shared(self):
        for w in range(len(self.parts)):
            self.own(w).wait()
            there = self.rows(w, self.at.group, self.at.other)
            remote(there, there, self.near_send.at[w], self.near_recv.at[w], self.at.sibling).wait_recv()

    def step(self, w, step):
        at = self.at
        for half in range(2):
            if step > 0:
                shift = step if half == 0 else -step
                part = self.rows(w, ring_group((at.place - shift + at.groups) % at.groups), half)
                sems = self.send.at[w, half, step - 1], self.recv.at[w, half, step - 1]
                remote(part, part, *sems, at.ring[half]).wait_recv()
            if step < at.groups - 1:
                self.hop(w, half, step).start()

    def drain(self):
        for w in range(len(self.parts)):
            self.near(w).wait_send()
            for half in range(2):
                for step in range(self.at.groups - 1):
                    self.hop(w, half, step).wait_send()


def gather_kernel(dp_size, branch_size, n_w, *refs):
    rows_ref = refs[0]
    w_refs = refs[1 : 1 + n_w]
    full_ref = refs[1 + n_w]
    wf_refs = refs[2 + n_w : 2 + 2 * n_w]
    small_out = refs[2 + 2 * n_w]
    (z_send, z_recv, s_send, s_recv, l_sem, w_send, w_recv, ws_send, ws_recv, wl_sem, p_send, p_recv, p_local) = refs[
        3 + 2 * n_w :
    ]
    at = Links(dp_size, branch_size)
    at.meet()
    rows = rows_ref.shape[0]
    waits = []

    def piece(block, branch):
        start = (block * branch_size + branch) * rows
        return full_ref.at[pl.ds(pl.multiple_of(start, rows), rows)]

    for cond, way, device in ((at.has_up, 0, at.up), (at.has_down, 1, at.down)):
        copy = remote(rows_ref, piece(0, at.branch), z_send.at[way, 0], z_recv.at[at.branch], device)
        pl.when(cond)(copy.start)
        waits.append((cond, copy.wait_send))
    copy = remote(rows_ref, piece(1, at.branch), s_send.at[at.branch], s_recv.at[at.branch], at.sibling)
    copy.start()
    waits.append((None, copy.wait_send))
    own = pltpu.make_async_copy(rows_ref, piece(0, at.branch), l_sem)
    own.start()
    waits.append((None, own.wait))
    ring = WeightRing(at, w_refs, wf_refs, (w_send, w_recv, ws_send, ws_recv, wl_sem))
    ring.share()
    ring.shared()
    for w in range(n_w):
        ring.step(w, 0)

    def line_step(step):
        for way in range(2):
            source = at.branch - step if way == 0 else at.branch + step
            inside = source >= 0 if way == 0 else source < branch_size
            onward = at.has_up if way == 0 else at.has_down
            device = at.up if way == 0 else at.down
            source = jnp.clip(source, 0, branch_size - 1)
            part = piece(0, source)
            forward = remote(part, part, z_send.at[way, step], z_recv.at[source], device)
            across = remote(part, piece(1, source), s_send.at[source], s_recv.at[source], at.sibling)

            @pl.when(inside)
            def _():
                forward.wait_recv()
                pl.when(onward)(forward.start)
                across.start()

            def both(inside=inside, onward=onward, forward=forward, across=across):
                @pl.when(inside)
                def _():
                    pl.when(onward)(forward.wait_send)
                    across.wait_send()

            waits.append((None, both))

    def spread():
        params = wf_refs[n_w - 1]
        own = pltpu.make_async_copy(params, small_out.at[at.branch], p_local)
        own.start()
        waits.append((None, own.wait))
        for k in range(1, branch_size):
            copy = remote(params, small_out.at[at.branch], p_send.at[k], p_recv.at[k], at.peers[k - 1])
            copy.start()
            waits.append((None, copy.wait_send))

    line_steps = list(range(1, branch_size))
    ring_steps = [(w, s) for s in range(1, at.groups) for w in range(n_w)]
    events = [(2.0 + 23.3 * e, 0, e) for e in line_steps]
    size = [w_refs[w].shape[1] * w_refs[w].shape[2] for w in range(n_w)]
    period = 34.0 * sum(size) / (256 * 3072)
    due = [sum(size[: w + 1]) / sum(size) for w in range(n_w)]
    due[-1] = 4.0 * size[-1] / sum(size)
    events += [(5.0 + period * (s - 1 + due[w]), 1, (w, s)) for w, s in ring_steps]
    for _, kind, event in sorted(events, key=lambda e: e[:2]):
        if kind == 0:
            line_step(event)
        else:
            ring.step(*event)
            if event == (n_w - 1, at.groups - 1):
                spread()
    for k in range(1, branch_size):
        slot = small_out.at[(at.branch - k + branch_size) % branch_size]
        remote(slot, slot, p_send.at[k], p_recv.at[k], at.peers[k - 1]).wait_recv()
    for branch in range(branch_size):
        part = piece(1, branch)
        remote(part, part, s_send.at[branch], s_recv.at[branch], at.sibling).wait_recv()
    ring.drain()
    for cond, wait in waits:
        if cond is None:
            wait()
        else:
            pl.when(cond)(wait)


def gather_all(dp_size, branch_size, array, weights):
    rows, width = array.shape
    n_w = len(weights)
    groups = dp_size // 2
    out_shape = [jax.ShapeDtypeStruct((2 * branch_size * rows, width), BF)]
    out_shape += [jax.ShapeDtypeStruct((dp_size * w.shape[1], w.shape[2]), BF) for w in weights]
    out_shape += [jax.ShapeDtypeStruct((branch_size, dp_size * weights[-1].shape[1], weights[-1].shape[2]), BF)]
    dma = pltpu.SemaphoreType.DMA
    return pl.pallas_call(
        functools.partial(gather_kernel, dp_size, branch_size, n_w),
        out_shape=out_shape,
        in_specs=[pl.BlockSpec(memory_space=pltpu.HBM)] * (1 + n_w),
        out_specs=[pl.BlockSpec(memory_space=pltpu.HBM)] * (2 + n_w),
        scratch_shapes=[
            dma((2, branch_size)),
            dma((branch_size,)),
            dma((branch_size,)),
            dma((branch_size,)),
            dma,
            dma((n_w, 2, groups)),
            dma((n_w, 2, groups)),
            dma((n_w,)),
            dma((n_w,)),
            dma((n_w,)),
            dma((branch_size,)),
            dma((branch_size,)),
            dma,
        ],
        compiler_params=pltpu.CompilerParams(
            collective_id=0, has_side_effects=True, vmem_limit_bytes=GATHER_VMEM
        ),
        cost_estimate=pl.CostEstimate(
            flops=100 * 4 * rows * width * width, bytes_accessed=2 * rows * width, transcendentals=0
        ),
        name="gather_all",
    )(array, *weights)


def scatter_kernel(dp_size, branch_size, *refs):
    n_w = 4
    (h_ref, gm_ref, other_ref, dqkv_ref, dz_ref, o_ref, u_ref, dh_ref, sums_ref) = refs[:9]
    g_refs = refs[9:13]
    tok_out, sum_out, sib_land = refs[13:16]
    slots = refs[16:20]
    got_refs = refs[20:24]
    outs = refs[24:28]
    ins = refs[28:32]
    (own_buf, sib_buf, line_slot, w_send, w_recv, ws_send, ws_recv, z_send, z_recv, s_send, s_recv,
     l_sem, left_buf, x_sem, i_sem, sum_slot, sum_first, sum_got, sum_peer, p_send, p_recv) = refs[32:]
    at = Links(dp_size, branch_size)
    at.meet()
    rows = own_buf.shape[0]
    toks = branch_size * rows
    w_rows = outs[2].shape[2]
    cols = dqkv_ref.shape[2]
    block = left_buf.shape[3]
    lefts = ((gm_ref, other_ref), (h_ref,))
    rights = (u_ref, o_ref, dz_ref, dqkv_ref)
    last = at.groups - 1
    waits = []
    sent = {}

    sib_copy = remote(dh_ref.at[pl.ds(toks, toks)], sib_land, s_send, s_recv, at.sibling)
    sib_copy.start()

    def ring_dest(half, step):
        shift = step + 1 if half == 0 else -step - 1
        return ring_group((at.place - shift + 2 * at.groups) % at.groups)

    def left_copy(a, half, step):
        dest = ring_dest(half, step)
        start = (2 * dest + half) * w_rows if block == w_rows else dest * block
        start = pl.multiple_of(start, block)
        size = left_buf.shape[2] // len(lefts[a])
        return [
            pltpu.make_async_copy(
                ref.at[:, pl.ds(start, block)], left_buf.at[a, half, pl.ds(i * size, size)], x_sem.at[a, half, i]
            )
            for i, ref in enumerate(lefts[a])
        ]

    def product(a, half, w):
        left = left_buf[a, half, :, pl.ds(half * (block - w_rows), w_rows)]

        def dot(right, flip=False):
            pair = (right, left) if flip else (left, right)
            return lax.dot_general(*pair, (((0,), (0,)), ((), ())), preferred_element_type=F32)

        if w < 3:
            return dot(rights[w][...], w < 2)
        return jnp.concatenate([dot(rights[w][c]) for c in range(3)], axis=1)

    def finish(w, values, core):
        if w < 2:
            size = values.shape[0]
            g_refs[w][pl.ds(pl.multiple_of(core * size, size), size), :] = values
        elif w == 2:
            size = values.shape[1]
            g_refs[w][:, pl.ds(pl.multiple_of(core * size, size), size)] = values
        else:
            for c in range(3):
                g_refs[w][c, :, pl.ds(pl.multiple_of(core * cols, cols), cols)] = values[:, c * cols : (c + 1) * cols]

    def ring_piece(a, half, i, step):
        w = 2 * a + i
        if i == 0:
            for load in left_copy(a, half, step):
                load.wait()
        total = product(a, half, w)
        if step > 0:
            slot = slots[w].at[half, step - 1]
            remote(
                slot, slot, w_send.at[w, half, step - 1], w_recv.at[w, half, step - 1], at.ring[half]
            ).wait_recv()
            load = pltpu.make_async_copy(slot, ins[w], i_sem)
            load.start()
            load.wait()
            total = total + ins[w][...].astype(F32)
        if step > 1:
            sent.pop((w, half, step - 2)).wait_send()
        out = outs[w].at[step % 2, half]
        if step < last:
            out[...] = total.astype(BF)
            copy = remote(
                out, slots[w].at[half, step], w_send.at[w, half, step], w_recv.at[w, half, step], at.ring[half]
            )
            copy.start()
            sent[w, half, step] = copy
        else:
            copy = remote(out, got_refs[w], ws_send.at[w], ws_recv.at[w], at.sibling)

            @pl.when(at.core == half)
            def _():
                finish(w, total, at.core)

            @pl.when(at.core != half)
            def _():
                out[...] = total.astype(BF)
                copy.start()

            waits.append(lambda copy=copy, half=half: pl.when(at.core != half)(copy.wait_send))
        if i == 1 and step < last:
            for load in left_copy(a, half, step + 1):
                load.start()

    def sum_step(step):
        for half in range(2):
            total = sums_ref[chunk_rows(ring_dest(half, step), half, 8)]
            if step > 0:
                slot = sum_slot.at[half, step - 1]
                remote(
                    slot, slot, w_send.at[n_w, half, step - 1], w_recv.at[n_w, half, step - 1], at.ring[half]
                ).wait_recv()
                total = total + slot[...]
            out = sum_first.at[step, half]
            out[...] = total
            if step < last:
                copy = remote(
                    out, sum_slot.at[half, step], w_send.at[n_w, half, step], w_recv.at[n_w, half, step], at.ring[half]
                )
                copy.start()
                waits.append(copy.wait_send)
        if step == last:
            copy = remote(sum_first.at[last, at.other], sum_got, ws_send.at[n_w], ws_recv.at[n_w], at.sibling)
            copy.start()
            copy.wait()
            mine = sum_peer.at[0]
            mine[...] = sum_first[last, at.core] + sum_got[...]
            sum_out[at.core] = sum_first[last, at.core]
            sum_out[at.other] = sum_got[...]
            for k in range(1, branch_size):
                copy = remote(mine, sum_peer.at[k], p_send.at[k], p_recv.at[k], at.peers[k - 1])
                copy.start()
                waits.append(copy.wait_send)

    def sum_end():
        total = sum_peer[0]
        for k in range(1, branch_size):
            remote(sum_peer.at[0], sum_peer.at[k], p_send.at[k], p_recv.at[k], at.peers[k - 1]).wait_recv()
            total = total + sum_peer[k]
        sum_out[2] = total

    def load_own(d):
        own = pltpu.make_async_copy(dh_ref.at[pl.ds(d * rows, rows)], own_buf, l_sem.at[0])
        sib = pltpu.make_async_copy(sib_land.at[pl.ds(d * rows, rows)], sib_buf, l_sem.at[1])
        own.start()
        sib.start()
        own.wait()
        sib.wait()

    def line_step(slot_time):
        far = branch_size - 1 - slot_time
        for way in range(2):
            d = at.branch + far if way == 0 else at.branch - far
            going = d < branch_size if way == 0 else d >= 0
            more = at.has_down if way == 0 else at.has_up
            device = at.up if way == 0 else at.down
            slot = line_slot.at[way, d - 1 + way]
            passing = remote(slot, slot, z_send.at[way, d], z_recv.at[way, d], device)

            @pl.when(going)
            def _():
                load_own(d)
                total = own_buf[...].astype(F32) + sib_buf[...].astype(F32)

                @pl.when(more)
                def _():
                    passing.wait_recv()
                    slot[...] = (total + slot[...].astype(F32)).astype(BF)

                @pl.when(jnp.logical_not(more))
                def _():
                    slot[...] = total.astype(BF)

                passing.start()

            waits.append(lambda going=going, passing=passing: pl.when(going)(passing.wait_send))

    def line_end():
        d = at.branch
        load_own(d)
        for way in range(2):
            more = at.has_down if way == 0 else at.has_up
            slot = line_slot.at[way, d - 1 + way]
            device = at.up if way == 0 else at.down

            @pl.when(more)
            def _():
                remote(slot, slot, z_send.at[way, d], z_recv.at[way, d], device).wait_recv()

        below, above = (
            jnp.where(at.has_down, line_slot[0, jnp.maximum(d - 1, 0)].astype(F32), 0.0),
            jnp.where(at.has_up, line_slot[1, jnp.minimum(d, branch_size - 2)].astype(F32), 0.0),
        )
        tok_out[...] = (own_buf[...].astype(F32) + sib_buf[...].astype(F32) + below + above).astype(BF)

    for a in range(2):
        for half in range(2):
            for load in left_copy(a, half, 0):
                load.start()
    sum_step(0)
    pieces = [(a, half, i) for a in range(2) for half in range(2) for i in range(2)]
    size = [rights[2 * a + i].shape[-1] * (1 + a * i * 2) for a, half, i in pieces]
    due = [sum(size[: i + 1]) / sum(size) for i in range(len(pieces))]
    period = 34.0
    events = [(period * (s - 1 + f) + 4.0, 1, (*p, s)) for s in range(1, at.groups) for p, f in zip(pieces, due)]
    events += [(2.0 * i, 1, (*p, 0)) for i, p in enumerate(pieces)]
    events += [(9.0 + 24.0 * k, 0, k) for k in range(branch_size)]
    events += [(10.0 + 12.0 * s, 2, s) for s in range(1, at.groups)]
    events += [(18.0 + 12.0 * at.groups, 3, 0)]
    for _, kind, event in sorted(events, key=lambda e: e[:2]):
        if kind == 0 and event == 0:
            sib_copy.wait_recv()
        if kind == 0 and event == branch_size - 1:
            line_end()
        elif kind == 0:
            line_step(event)
        elif kind == 1:
            ring_piece(*event)
        elif kind == 2:
            sum_step(event)
        else:
            sum_end()
    for w in range(n_w):
        remote(outs[w].at[0, 0], got_refs[w], ws_send.at[w], ws_recv.at[w], at.sibling).wait_recv()
        finish(w, got_refs[w][...].astype(F32), at.other)
    sib_copy.wait_send()
    for copy in sent.values():
        copy.wait_send()
    for wait in waits:
        wait()


def scatter_all(dp_size, branch_size, h, gm, gm_other, dqkv, dz, o, u, dh, sums):
    widths = [u.shape[1], o.shape[1], dz.shape[1], 3 * dqkv.shape[2]]
    width = h.shape[1]
    w_rows = width // dp_size
    groups = dp_size // 2
    toks = h.shape[0] // 2
    rows = toks // branch_size
    n_w = 4
    dma = pltpu.SemaphoreType.DMA
    vm = pl.BlockSpec(memory_space=pltpu.VMEM)
    hb = pl.BlockSpec(memory_space=pltpu.HBM)
    shapes = [(widths[0], w_rows), (widths[1], w_rows), (w_rows, widths[2]), (w_rows, widths[3])]
    out_shape = [
        jax.ShapeDtypeStruct((2 * widths[0], w_rows), F32),
        jax.ShapeDtypeStruct((2 * widths[1], w_rows), F32),
        jax.ShapeDtypeStruct((w_rows, 2 * widths[2]), F32),
        jax.ShapeDtypeStruct((3, w_rows, 2 * dqkv.shape[2]), F32),
    ]
    out_shape += [jax.ShapeDtypeStruct((rows, width), BF), jax.ShapeDtypeStruct((3, 8, 128), F32)]
    out_shape += [jax.ShapeDtypeStruct((toks, width), BF)]
    out_shape += [jax.ShapeDtypeStruct((2, groups - 1) + shape, BF) for shape in shapes]
    out = pl.pallas_call(
        functools.partial(scatter_kernel, dp_size, branch_size),
        out_shape=out_shape,
        in_specs=[hb] * 3 + [vm] * 4 + [hb, vm],
        out_specs=[vm] * 6 + [hb] * 5,
        scratch_shapes=[pltpu.VMEM(shape, BF) for shape in shapes]
        + [pltpu.VMEM((2, 2) + shape, BF) for shape in shapes]
        + [pltpu.VMEM(shape, BF) for shape in shapes]
        + [
            pltpu.VMEM((rows, width), BF),
            pltpu.VMEM((rows, width), BF),
            pltpu.VMEM((2, branch_size - 1, rows, width), BF),
            dma((n_w + 1, 2, groups)),
            dma((n_w + 1, 2, groups)),
            dma((n_w + 1,)),
            dma((n_w + 1,)),
            dma((2, branch_size)),
            dma((2, branch_size)),
            dma(()),
            dma(()),
            dma((2,)),
            pltpu.VMEM((2, 2, 2 * toks, w_rows if w_rows % 128 == 0 else 2 * w_rows), BF),
            dma((2, 2, 2)),
            dma(()),
            pltpu.VMEM((2, groups - 1, 8, 128), F32),
            pltpu.VMEM((groups, 2, 8, 128), F32),
            pltpu.VMEM((8, 128), F32),
            pltpu.VMEM((branch_size, 8, 128), F32),
            dma((branch_size,)),
            dma((branch_size,)),
        ],
        compiler_params=pltpu.CompilerParams(
            collective_id=1, has_side_effects=True, vmem_limit_bytes=VMEM_LIMIT
        ),
        cost_estimate=pl.CostEstimate(
            flops=4 * toks * width * sum(widths), bytes_accessed=2 * toks * width, transcendentals=0
        ),
        name="scatter_all",
    )(h, gm, gm_other, dqkv, dz, o, u, dh, sums)
    return out[:4], out[4], out[5]


def turn(values, tables, sign):
    fixed, from_low, from_high = tables
    half = ROT // 2
    return (
        values * fixed
        + sign * (pltpu.roll(values, half, 1) * from_low + pltpu.roll(values, 2 * HEAD_DIM - half, 1) * from_high)
    )


def score_tile(keys, queries, begins, first, q_tile):
    scores = lax.dot_general(keys, queries, (((1,), (1,)), ((), ())), preferred_element_type=F32)
    key_at = lax.broadcasted_iota(jnp.int32, scores.shape, 0)
    query_at = first + lax.broadcasted_iota(jnp.int32, scores.shape, 1)
    allowed = jnp.logical_and(key_at >= begins, key_at <= query_at)
    return jnp.where(allowed, scores, NEGATIVE)


def attend_kernel(q_tile, q_ref, k_ref, v_ref, begin_ref, fixed_ref, low_ref, high_ref, qr_ref, kr_ref, vr_ref, o_ref, lse_ref):
    tables = (fixed_ref[0], low_ref[0], high_ref[0])
    qr_ref[...] = (turn(q_ref[...], tables, 1.0) * (HEAD_DIM**-0.5)).astype(BF)
    kr_ref[...] = turn(k_ref[...], tables, 1.0).astype(BF)
    vr_ref[...] = v_ref[...].astype(BF)
    toks = q_ref.shape[0]
    for first in range(0, toks, q_tile):
        span = first + q_tile
        begins = begin_ref[0, 0:1, first:span]
        outs = []
        for head in range(2):
            lanes = slice(head * HEAD_DIM, (head + 1) * HEAD_DIM)
            scores = score_tile(kr_ref[:span, lanes], qr_ref[first:span, lanes], begins, first, q_tile)
            top = jnp.max(scores, axis=0, keepdims=True)
            weights = jnp.exp(scores - top)
            total = jnp.sum(weights, axis=0, keepdims=True)
            lse_ref[0, 0, head : head + 1, first:span] = top + jnp.log(total)
            mixed = lax.dot_general(
                vr_ref[:span, lanes], weights.astype(BF), (((0,), (0,)), ((), ())), preferred_element_type=F32
            )
            outs.append(mixed / total)
        o_ref[first:span, :] = jnp.concatenate(outs, axis=0).T.astype(BF)


def attend_back_kernel(
    q_tile, qr_ref, kr_ref, vr_ref, o_ref, do_ref, lse_ref, begin_ref, fixed_ref, low_ref, high_ref, grad_ref, k_acc, v_acc
):
    tables = (fixed_ref[0], low_ref[0], high_ref[0])
    toks = qr_ref.shape[0]
    k_acc[...] = jnp.zeros_like(k_acc)
    v_acc[...] = jnp.zeros_like(v_acc)
    for first in range(0, toks, q_tile):
        span = first + q_tile
        begins = begin_ref[0, 0:1, first:span]
        both = (do_ref[first:span, :].astype(F32) * o_ref[first:span, :].astype(F32)).T
        turned = []
        for head in range(2):
            lanes = slice(head * HEAD_DIM, (head + 1) * HEAD_DIM)
            delta = jnp.sum(both[lanes], axis=0, keepdims=True)
            queries = qr_ref[first:span, lanes]
            grads = do_ref[first:span, lanes]
            keys = kr_ref[:span, lanes]
            scores = score_tile(keys, queries, begins, first, q_tile)
            prob = jnp.exp(scores - lse_ref[0, 0, head : head + 1, first:span])
            v_acc[head, :span, :] += jnp.dot(prob.astype(BF), grads, preferred_element_type=F32)
            dprob = lax.dot_general(
                vr_ref[:span, lanes], grads, (((1,), (1,)), ((), ())), preferred_element_type=F32
            )
            ds = (prob * (dprob - delta)).astype(BF)
            k_acc[head, :span, :] += jnp.dot(ds, queries, preferred_element_type=F32)
            turned.append(
                lax.dot_general(keys, ds, (((0,), (0,)), ((), ())), preferred_element_type=F32)
            )
        dq = jnp.concatenate(turned, axis=0).T * (HEAD_DIM**-0.5)
        grad_ref[0, first:span, :] = turn(dq, tuple(t[first:span] for t in tables), -1.0).astype(BF)
    dk = jnp.concatenate([k_acc[0], k_acc[1]], axis=1)
    grad_ref[1] = turn(dk, tables, -1.0).astype(BF)
    grad_ref[2] = jnp.concatenate([v_acc[0], v_acc[1]], axis=1).astype(BF)


def attention_specs(toks, pairs):
    wide = 2 * HEAD_DIM

    def cols(shift):
        return pl.BlockSpec((toks, wide), lambda i, j: (i, j + shift * pairs))

    begin = pl.BlockSpec((1, 8, toks), lambda i, j: (i, 0, 0))
    table = pl.BlockSpec((1, toks, wide), lambda i, j: (i, 0, 0))
    lse = pl.BlockSpec((1, 1, 2, toks), lambda i, j: (i, j, 0, 0))
    return cols, begin, table, lse


def attend(project, begins, tables):
    blocks, _, toks = begins.shape
    pairs = project.shape[1] // (6 * HEAD_DIM)
    cols, begin, table, lse = attention_specs(toks, pairs)
    narrow = jax.ShapeDtypeStruct((blocks * toks, pairs * 2 * HEAD_DIM), BF)
    return pl.pallas_call(
        functools.partial(attend_kernel, min(256, toks)),
        grid=(blocks, pairs),
        in_specs=[cols(0), cols(1), cols(2), begin] + [table] * 3,
        out_specs=[cols(0)] * 4 + [lse],
        out_shape=[narrow] * 4 + [jax.ShapeDtypeStruct((blocks, pairs, 2, toks), F32)],
        compiler_params=pltpu.CompilerParams(vmem_limit_bytes=60 * 2**20),
        name="attend",
    )(project, project, project, begins, *tables)


def attend_back(queries, keys, values, o, do, lse_rows, begins, tables):
    blocks, _, toks = begins.shape
    pairs = queries.shape[1] // (2 * HEAD_DIM)
    cols, begin, table, lse = attention_specs(toks, pairs)
    acc = pltpu.VMEM((2, toks, HEAD_DIM), F32)
    return pl.pallas_call(
        functools.partial(attend_back_kernel, min(256, toks)),
        grid=(blocks, pairs),
        in_specs=[cols(0)] * 5 + [lse, begin] + [table] * 3,
        out_specs=pl.BlockSpec((3, toks, 2 * HEAD_DIM), lambda i, j: (0, i, j)),
        out_shape=jax.ShapeDtypeStruct((3,) + queries.shape, BF),
        scratch_shapes=[acc, acc],
        compiler_params=pltpu.CompilerParams(vmem_limit_bytes=60 * 2**20),
        name="attend_back",
    )(queries, keys, values, o, do, lse_rows, begins, *tables)


def rotary_tables(doc_rows):
    row_count = doc_rows.shape[0]
    row_index = jnp.arange(row_count, dtype=jnp.int32)
    same = doc_rows[:, None] == doc_rows[None, :]
    begins = jnp.min(jnp.where(same, row_index[:, None], row_count), axis=0)
    places = (row_index - begins).astype(F32)
    half = ROT // 2
    lane = np.arange(2 * HEAD_DIM) % HEAD_DIM
    turning = lane < ROT
    frequency = np.where(turning, 10000.0 ** (-2.0 * (lane % half) / ROT), 0.0).astype(np.float32)
    angles = places[:, None] * frequency[None, :]
    sine = jnp.sin(angles)
    from_low = sine * np.where(turning & (lane >= half), 1.0, 0.0).astype(np.float32)
    from_high = sine * np.where(lane < half, -1.0, 0.0).astype(np.float32)
    return jnp.broadcast_to(begins[None], (8, row_count)), (jnp.cos(angles), from_low, from_high)


def dot_nt(left, right):
    return lax.dot_general(left, right, (((1,), (1,)), ((), ())), preferred_element_type=F32)


def standardized(rows):
    xfloat = rows.astype(F32)
    removed = xfloat - jnp.mean(xfloat, axis=-1, keepdims=True)
    inverse = lax.rsqrt(jnp.mean(removed * removed, axis=-1, keepdims=True) + NORM_EPS)
    return removed * inverse, inverse


def enter_kernel(
    dp_size, branch_size, tok_ref, gain_ref, shift_ref, wq_ref, qb_ref, wu_ref, ub_ref, part_ref,
    h_ref, project_ref, u_ref, slope_ref, full_ref, *sems,
):
    tile_at, tiles = pl.program_id(0), pl.num_programs(0)
    at = Links(dp_size, branch_size)
    ring = WeightRing(at, [part_ref], [full_ref], sems)

    @pl.when(tile_at == 0)
    def _():
        at.meet()
        ring.share()
        ring.shared()
        ring.step(0, 0)

    pl.when(tile_at == FIRST_HOP)(lambda: ring.step(0, 1))

    h = (standardized(tok_ref[...])[0] * gain_ref[0:1] + shift_ref[0:1]).astype(BF)
    h_ref[...] = h
    project_ref[...] = jnp.dot(h, wq_ref[...], preferred_element_type=F32) + qb_ref[0:1]
    z = jnp.dot(h, wu_ref[...], preferred_element_type=F32) + ub_ref[0:1]
    scale, cubic = math.sqrt(2.0 / math.pi), 0.044715
    square = z * z
    bent = jnp.tanh(scale * z * (1.0 + cubic * square))
    half = 0.5 * (1.0 + bent)
    u_ref[...] = (z * half).astype(BF)
    slope = half + 0.5 * z * (1.0 - bent * bent) * (scale * (1.0 + 3.0 * cubic * square))
    slope_ref[...] = slope.astype(BF)

    @pl.when(tile_at == tiles - 1)
    def _():
        for step in range(2, at.groups):
            ring.step(0, step)
        ring.drain()


def enter(dp_size, branch_size, tok_all, gain, shift, wqkv, qkv_b, wup, up_b, part):
    total, width = tok_all.shape
    groups = dp_size // 2
    tile = ROW_TILE
    dma = pltpu.SemaphoreType.DMA

    def spec(width):
        return pl.BlockSpec((tile, width), lambda i: (i, 0))

    whole = (gain, shift, wqkv, qkv_b, wup, up_b)
    outs = [(width, BF), (wqkv.shape[1], F32), (wup.shape[1], BF), (wup.shape[1], BF)]
    far = pl.BlockSpec(memory_space=pltpu.HBM)
    return pl.pallas_call(
        functools.partial(enter_kernel, dp_size, branch_size),
        grid=(total // tile,),
        in_specs=[spec(width)] + [pl.BlockSpec(x.shape, lambda i: (0, 0)) for x in whole] + [far],
        out_specs=[spec(w) for w, _ in outs] + [far],
        out_shape=[jax.ShapeDtypeStruct((total, w), t) for w, t in outs]
        + [jax.ShapeDtypeStruct((dp_size * part.shape[1], part.shape[2]), BF)],
        scratch_shapes=[dma((1, 2, groups)), dma((1, 2, groups)), dma((1,)), dma((1,)), dma((1,))],
        compiler_params=pltpu.CompilerParams(
            collective_id=2, has_side_effects=True, vmem_limit_bytes=ENTER_VMEM
        ),
        cost_estimate=pl.CostEstimate(
            flops=2 * total * (wqkv.size + wup.size), bytes_accessed=2 * total * width, transcendentals=0
        ),
        name="enter",
    )(tok_all, *whole, part)


def branch_kernel(o_ref, u_ref, *refs):
    more, (wo_ref, wd_ref, br_ref) = refs[:-3], refs[-3:]
    total = dot_nt(o_ref[...], wo_ref[...]) + dot_nt(u_ref[...], wd_ref[...])
    for ref in more:
        total = total + ref[...].astype(F32)
    br_ref[...] = total.astype(BF)


def grad_kernel(gm_ref, other_ref, slope_ref, wo_ref, wd_ref, do_ref, dz_ref, sum_ref):
    step = pl.program_id(0)

    @pl.when(step == 0)
    def _():
        sum_ref[...] = jnp.zeros_like(sum_ref)

    def use(rows_ref):
        gm = rows_ref[...]
        do_ref[...] = jnp.dot(gm, wo_ref[...], preferred_element_type=F32).astype(BF)
        dz = jnp.dot(gm, wd_ref[...], preferred_element_type=F32) * slope_ref[...].astype(F32)
        dz = dz.astype(BF)
        dz_ref[...] = dz
        sum_ref[0:1] += jnp.sum(dz.astype(F32), axis=0, keepdims=True)

    own = step < pl.num_programs(0) // 2
    pl.when(own)(lambda: use(gm_ref))
    pl.when(jnp.logical_not(own))(lambda: use(other_ref))


def leave_kernel(tok_ref, grad_ref, dz_ref, wq_ref, wu_ref, dh_ref, sum_ref, q_sum_ref):
    @pl.when(pl.program_id(0) == 0)
    def _():
        sum_ref[...] = jnp.zeros_like(sum_ref)
        q_sum_ref[...] = jnp.zeros_like(q_sum_ref)

    cols = grad_ref.shape[2]
    grads = jnp.concatenate([grad_ref[c] for c in range(3)], axis=1)
    dh = dot_nt(dz_ref[...], wu_ref[...]) + dot_nt(grads, wq_ref[...])
    dh_ref[...] = dh.astype(BF)
    xhat = standardized(tok_ref[...])[0]
    sum_ref[0:1] += jnp.sum(dh * xhat, axis=0, keepdims=True)
    sum_ref[1:2] += jnp.sum(dh, axis=0, keepdims=True)
    q_sum_ref[0:1] += jnp.sum(grads.astype(F32), axis=0, keepdims=True)


def row_call(kernel, name, tiles, tiled, whole, outs, sums):
    tile = ROW_TILE

    def spec(width):
        return pl.BlockSpec((tile, width), lambda i: (i, 0))

    in_specs = [s if s is not None else spec(x.shape[1]) for x, s in tiled]
    in_specs += [pl.BlockSpec(x.shape, lambda i: (0, 0)) for x in whole]
    flops = 2 * tiles * tile * sum(x.size for x in whole)
    traffic = 2 * sum(x.size for x in whole) + 2 * sum(x.size for x, _ in tiled) + 4 * tiles * tile * sum(w for w, _ in outs)
    return pl.pallas_call(
        kernel,
        grid=(tiles,),
        in_specs=in_specs,
        out_specs=[spec(w) for w, _ in outs] + [pl.BlockSpec((8, w), lambda i: (0, 0)) for w in sums],
        out_shape=[jax.ShapeDtypeStruct((tiles * tile, w), t) for w, t in outs]
        + [jax.ShapeDtypeStruct((8, w), F32) for w in sums],
        compiler_params=pltpu.CompilerParams(vmem_limit_bytes=60 * 2**20),
        cost_estimate=pl.CostEstimate(flops=flops, bytes_accessed=traffic, transcendentals=0),
        name=name,
    )(*[x for x, _ in tiled], *whole)


def local(
    dp_size, branch_size, tokens, doc_ids, real_rows, cotangent, norm_gain, norm_shift, out_bias,
    w_qkv, b_qkv, w_out, w_up, b_up, w_down,
):
    dp = lax.axis_index("dp")
    branch = lax.axis_index("branch")
    core = dp % 2
    my_rows, width = tokens.shape
    toks = doc_ids.shape[0]
    w_rows = w_qkv.shape[1]
    cols = w_qkv.shape[2] // 2
    hid = w_up.shape[1] // 2
    heads = cols // HEAD_DIM

    my_real = lax.dynamic_slice_in_dim(real_rows, branch * my_rows, my_rows).astype(F32)
    masked_cot = (cotangent.astype(F32) * my_real[:, None]).astype(BF)
    qkv_l = w_qkv.astype(BF).reshape(3, w_rows, 2, cols).transpose(2, 1, 0, 3).reshape(2, w_rows, 3 * cols)
    up_l = w_up.astype(BF).reshape(w_rows, 2, hid).transpose(1, 0, 2)
    out_l = w_out.astype(BF).T.reshape(w_rows, 2, cols).transpose(1, 0, 2)
    down_l = w_down.astype(BF).T.reshape(w_rows, 2, hid).transpose(1, 0, 2)

    small = jnp.concatenate([v.reshape(-1) for v in (norm_gain, norm_shift, out_bias, b_qkv, b_up)]).astype(BF)
    small = jnp.pad(small, (0, -small.size % 128))
    small = jnp.broadcast_to(small[None, None], (2, 16, small.size))

    tok_all, wqkv, wup, wot, _, params = gather_all(
        dp_size, branch_size, tokens, (qkv_l, up_l, out_l, small)
    )
    swap = [(i, i + 1 - 2 * (i % 2)) for i in range(dp_size)]
    late_cot, tok_all = lax.optimization_barrier((masked_cot, tok_all))
    gm_own = lax.all_gather(late_cot, "branch", axis=0, tiled=True)
    params = params.reshape(branch_size, dp_size, 16, -1)[:, :, 0].astype(F32)
    sizes = [norm_gain.size, norm_shift.size, out_bias.size, b_qkv.size, b_up.size]
    stops = [sum(sizes[: i + 1]) for i in range(5)]
    gain, shift, bias_full = (
        params[:, :, stops[i] - sizes[i] : stops[i]].transpose(1, 0, 2).reshape(width) for i in range(3)
    )
    mine = lax.dynamic_index_in_dim(params, branch, 0, keepdims=False)
    qkv_b = mine[:, stops[2] : stops[3]].reshape((dp_size,) + b_qkv.shape).transpose(1, 2, 0, 3)
    qkv_b = qkv_b.reshape(3, 2, cols)
    qkv_b = lax.dynamic_index_in_dim(qkv_b, core, 1, keepdims=False).reshape(3 * cols)
    up_b = mine[:, stops[3] : stops[4]].reshape((dp_size,) + b_up.shape).transpose(1, 0, 2).reshape(2, hid)
    up_b = lax.dynamic_index_in_dim(up_b, core, 0, keepdims=False)
    ids = jnp.stack([doc_ids, lax.ppermute(doc_ids, "dp", swap)])

    def row(values):
        return jnp.broadcast_to(values[None], (8, values.size))

    tiles = 2 * toks // ROW_TILE
    h, project, u, slope, wdt = enter(
        dp_size, branch_size, tok_all, row(gain), row(shift), wqkv, row(qkv_b), wup, row(up_b), down_l
    )
    found = [rotary_tables(ids[i]) for i in range(2)]
    begins = jnp.stack([t[0] for t in found])
    tables = [jnp.stack([t[1][i] for t in found]) for i in range(3)]
    queries, keys, values, o, lse_rows = attend(project, begins, tables)
    gm_own, _ = lax.optimization_barrier((gm_own, o))
    gm_other = lax.ppermute(gm_own, "dp", swap)
    half_tiles = tiles // 2

    def branch_out(first, *more):
        def later(width):
            return pl.BlockSpec((ROW_TILE, width), lambda i: (i + first, 0))

        tiled = [(o, later(cols)), (u, later(hid))] + [(x, None) for x in more]
        return row_call(branch_kernel, "branch_out", half_tiles, tiled, [wot, wdt], [(width, BF)], [])[0]

    given = lax.ppermute(branch_out(half_tiles), "dp", swap)
    xfloat = tokens.astype(F32)

    near = pl.BlockSpec((ROW_TILE, width), lambda i: (jnp.minimum(i, half_tiles - 1), 0))
    far = pl.BlockSpec((ROW_TILE, width), lambda i: (jnp.maximum(i - half_tiles, 0), 0))
    do, dz, up_sums = row_call(
        grad_kernel, "branch_grad", tiles, [(gm_own, near), (gm_other, far), (slope, None)], [wot, wdt],
        [(cols, BF), (hid, BF)], [hid],
    )
    do, given = lax.optimization_barrier((do, given))
    br = branch_out(0, given)
    do, br = lax.optimization_barrier((do, br))
    summed = lax.psum_scatter(br, "branch", scatter_dimension=0, tiled=True).astype(F32)
    dqkv = attend_back(queries, keys, values, o, do, lse_rows, begins, tables)
    three = pl.BlockSpec((3, ROW_TILE, cols), lambda i: (0, i, 0))
    dh, token_sums, q_sums = row_call(
        leave_kernel, "leave", tiles, [(tok_all, None), (dqkv, three), (dz, None)], [wqkv, wup],
        [(width, BF)], [width, 3 * cols],
    )

    part = norm_gain.shape[0]
    vectors = jnp.stack(
        [token_sums[0], token_sums[1], jnp.sum(masked_cot, axis=0, dtype=F32)]
    )
    vectors = vectors.reshape(3, dp_size, branch_size * part).transpose(1, 0, 2).reshape(dp_size, -1)
    q_sum = q_sums[0].reshape(3, heads, dp_size, -1).transpose(2, 0, 1, 3).reshape(dp_size, -1)
    u_sum = up_sums[0].reshape(b_up.shape[0] // 2, dp_size, -1).transpose(1, 0, 2)
    u_sum = u_sum.reshape(dp_size, -1)
    sums = jnp.concatenate([vectors, q_sum, u_sum], axis=1)
    ends = (vectors.shape[1], vectors.shape[1] + q_sum.shape[1], sums.shape[1])
    sums = jnp.pad(sums, ((0, 0), (0, 1024 - sums.shape[1]))).reshape(8 * dp_size, 128)

    (g_down, g_out, g_up, g_qkv), dh_mine, total = scatter_all(
        dp_size, branch_size, h, gm_own, gm_other, dqkv, dz, o, u, dh, sums
    )
    dh_mine = dh_mine.astype(F32)
    total = total.reshape(3, 1024)
    block_out = (xfloat + my_real[:, None] * (summed + bias_full)).astype(BF)
    xhat, inverse = standardized(tokens)
    scaled = dh_mine * gain
    input_grad = inverse * (
        scaled
        - jnp.mean(scaled, axis=-1, keepdims=True)
        - xhat * jnp.mean(scaled * xhat, axis=-1, keepdims=True)
    )
    tokens_grad = (cotangent.astype(F32) + input_grad).astype(BF)

    gain_g, shift_g, bias_g = lax.dynamic_slice_in_dim(
        total[2, : ends[0]].reshape(3, branch_size * part), branch * part, part, axis=1
    )
    b_q = total[:2, ends[0] : ends[1]].reshape(2, 3, heads, -1).transpose(1, 0, 2, 3).reshape(b_qkv.shape)
    b_u = total[:2, ends[1] : ends[2]].reshape(b_up.shape)
    return (block_out, tokens_grad, gain_g, shift_g, bias_g, g_qkv, b_q, g_out, g_up, b_u, g_down)


def solution(mesh):
    in_specs = (
        P(("dp", "branch"), None),
        P("dp"),
        P("dp"),
        P(("dp", "branch"), None),
        P(("dp", "branch")),
        P(("dp", "branch")),
        P(("dp", "branch")),
        P(None, "dp", "branch"),
        P(None, "branch", "dp"),
        P("branch", "dp"),
        P("dp", "branch"),
        P("branch", "dp"),
        P("branch", "dp"),
    )
    out_specs = (
        P(("dp", "branch"), None),
        P(("dp", "branch"), None),
        P(("dp", "branch")),
        P(("dp", "branch")),
        P(("dp", "branch")),
        P(None, "dp", "branch"),
        P(None, "branch", "dp"),
        P("branch", "dp"),
        P("dp", "branch"),
        P("branch", "dp"),
        P("branch", "dp"),
    )
    body = functools.partial(local, mesh.shape["dp"], mesh.shape["branch"])
    return jax.shard_map(body, mesh=mesh, in_specs=in_specs, out_specs=out_specs, check_vma=False)
```

```python
import functools
import math

import jax
import jax.numpy as jnp
import numpy as np
from jax import lax
from jax.experimental import pallas as pl
from jax.experimental.pallas import tpu as pltpu
from jax.sharding import PartitionSpec as P

HEAD_DIM = 64
ROT = 32
NORM_EPS = 1e-05
NEGATIVE = -1e30
BF = jnp.bfloat16
F32 = jnp.float32
MESH = pl.DeviceIdType.MESH
VMEM_LIMIT = 48 * 2**20
ROW_TILE = 512
ENTER_VMEM = 48 * 2**20
FIRST_HOP = 2
GATHER_VMEM = 48 * 2**20


def ring_place(group):
    row = group // 2
    return 2 * row + (group + row) % 2


def ring_group(place):
    row = place // 2
    return 2 * row + (place + row) % 2


def chunk_rows(group, half, rows):
    return pl.ds(pl.multiple_of((2 * group + half) * rows, rows), rows)


class Links:
    def __init__(self, dp_size, branch_size):
        self.groups = dp_size // 2
        self.branches = branch_size
        dp = lax.axis_index("dp")
        self.core = dp % 2
        self.other = 1 - self.core
        self.group = dp // 2
        self.place = ring_place(self.group)
        self.branch = lax.axis_index("branch")
        self.sibling = {"dp": 2 * self.group + self.other}
        right = ring_group((self.place + 1) % self.groups)
        left = ring_group((self.place + self.groups - 1) % self.groups)
        self.ring = ({"dp": 2 * right + self.core}, {"dp": 2 * left + self.core})
        self.has_up = self.branch < self.branches - 1
        self.has_down = self.branch > 0
        self.peers = [{"branch": (self.branch + k) % branch_size} for k in range(1, branch_size)]
        self.up = {"branch": self.branch + 1}
        self.down = {"branch": self.branch - 1}

    def meet(self):
        barrier = pltpu.get_barrier_semaphore()

        def greet(device):
            pl.semaphore_signal(barrier, 1, device_id=device, device_id_type=MESH)

        greet(self.sibling)
        greet(self.ring[0])
        greet(self.ring[1])
        for device in self.peers:
            greet(device)
        pl.semaphore_wait(barrier, 3 + len(self.peers))


def remote(src, dst, send, recv, device):
    return pltpu.make_async_remote_copy(
        src_ref=src, dst_ref=dst, send_sem=send, recv_sem=recv, device_id=device, device_id_type=MESH
    )


class WeightRing:
    def __init__(self, at, parts, fulls, sems):
        self.at, self.parts, self.fulls = at, parts, fulls
        self.send, self.recv, self.near_send, self.near_recv, self.local = sems

    def rows(self, w, group, half):
        return self.fulls[w].at[chunk_rows(group, half, self.parts[w].shape[1])]

    def near(self, w):
        at = self.at
        here = self.rows(w, at.group, at.core)
        return remote(self.parts[w].at[at.other], here, self.near_send.at[w], self.near_recv.at[w], at.sibling)

    def own(self, w):
        at = self.at
        return pltpu.make_async_copy(self.parts[w].at[at.core], self.rows(w, at.group, at.core), self.local.at[w])

    def hop(self, w, half, step):
        at = self.at
        shift = step if half == 0 else -step
        part = self.rows(w, ring_group((at.place - shift + at.groups) % at.groups), half)
        return remote(part, part, self.send.at[w, half, step], self.recv.at[w, half, step], at.ring[half])

    def share(self):
        for w in range(len(self.parts)):
            self.near(w).start()
            self.own(w).start()

    def shared(self):
        for w in range(len(self.parts)):
            self.own(w).wait()
            there = self.rows(w, self.at.group, self.at.other)
            remote(there, there, self.near_send.at[w], self.near_recv.at[w], self.at.sibling).wait_recv()

    def step(self, w, step):
        at = self.at
        for half in range(2):
            if step > 0:
                shift = step if half == 0 else -step
                part = self.rows(w, ring_group((at.place - shift + at.groups) % at.groups), half)
                sems = self.send.at[w, half, step - 1], self.recv.at[w, half, step - 1]
                remote(part, part, *sems, at.ring[half]).wait_recv()
            if step < at.groups - 1:
                self.hop(w, half, step).start()

    def drain(self):
        for w in range(len(self.parts)):
            self.near(w).wait_send()
            for half in range(2):
                for step in range(self.at.groups - 1):
                    self.hop(w, half, step).wait_send()


def gather_kernel(dp_size, branch_size, n_w, *refs):
    rows_ref = refs[0]
    w_refs = refs[1 : 1 + n_w]
    full_ref = refs[1 + n_w]
    wf_refs = refs[2 + n_w : 2 + 2 * n_w]
    small_out = refs[2 + 2 * n_w]
    (z_send, z_recv, s_send, s_recv, l_sem, w_send, w_recv, ws_send, ws_recv, wl_sem, p_send, p_recv, p_local) = refs[
        3 + 2 * n_w :
    ]
    at = Links(dp_size, branch_size)
    at.meet()
    rows = rows_ref.shape[0]
    waits = []

    def piece(block, branch):
        start = (block * branch_size + branch) * rows
        return full_ref.at[pl.ds(pl.multiple_of(start, rows), rows)]

    for cond, way, device in ((at.has_up, 0, at.up), (at.has_down, 1, at.down)):
        copy = remote(rows_ref, piece(0, at.branch), z_send.at[way, 0], z_recv.at[at.branch], device)
        pl.when(cond)(copy.start)
        waits.append((cond, copy.wait_send))
    copy = remote(rows_ref, piece(1, at.branch), s_send.at[at.branch], s_recv.at[at.branch], at.sibling)
    copy.start()
    waits.append((None, copy.wait_send))
    own = pltpu.make_async_copy(rows_ref, piece(0, at.branch), l_sem)
    own.start()
    waits.append((None, own.wait))
    ring = WeightRing(at, w_refs, wf_refs, (w_send, w_recv, ws_send, ws_recv, wl_sem))
    ring.share()
    ring.shared()
    for w in range(n_w):
        ring.step(w, 0)

    def line_step(step):
        for way in range(2):
            source = at.branch - step if way == 0 else at.branch + step
            inside = source >= 0 if way == 0 else source < branch_size
            onward = at.has_up if way == 0 else at.has_down
            device = at.up if way == 0 else at.down
            source = jnp.clip(source, 0, branch_size - 1)
            part = piece(0, source)
            forward = remote(part, part, z_send.at[way, step], z_recv.at[source], device)
            across = remote(part, piece(1, source), s_send.at[source], s_recv.at[source], at.sibling)

            @pl.when(inside)
            def _():
                forward.wait_recv()
                pl.when(onward)(forward.start)
                across.start()

            def both(inside=inside, onward=onward, forward=forward, across=across):
                @pl.when(inside)
                def _():
                    pl.when(onward)(forward.wait_send)
                    across.wait_send()

            waits.append((None, both))

    def spread():
        params = wf_refs[n_w - 1]
        own = pltpu.make_async_copy(params, small_out.at[at.branch], p_local)
        own.start()
        waits.append((None, own.wait))
        for k in range(1, branch_size):
            copy = remote(params, small_out.at[at.branch], p_send.at[k], p_recv.at[k], at.peers[k - 1])
            copy.start()
            waits.append((None, copy.wait_send))

    line_steps = list(range(1, branch_size))
    ring_steps = [(w, s) for s in range(1, at.groups) for w in range(n_w)]
    events = [(2.0 + 23.3 * e, 0, e) for e in line_steps]
    size = [w_refs[w].shape[1] * w_refs[w].shape[2] for w in range(n_w)]
    period = 34.0 * sum(size) / (256 * 3072)
    due = [sum(size[: w + 1]) / sum(size) for w in range(n_w)]
    due[-1] = 4.0 * size[-1] / sum(size)
    events += [(5.0 + period * (s - 1 + due[w]), 1, (w, s)) for w, s in ring_steps]
    for _, kind, event in sorted(events, key=lambda e: e[:2]):
        if kind == 0:
            line_step(event)
        else:
            ring.step(*event)
            if event == (n_w - 1, at.groups - 1):
                spread()
    for k in range(1, branch_size):
        slot = small_out.at[(at.branch - k + branch_size) % branch_size]
        remote(slot, slot, p_send.at[k], p_recv.at[k], at.peers[k - 1]).wait_recv()
    for branch in range(branch_size):
        part = piece(1, branch)
        remote(part, part, s_send.at[branch], s_recv.at[branch], at.sibling).wait_recv()
    ring.drain()
    for cond, wait in waits:
        if cond is None:
            wait()
        else:
            pl.when(cond)(wait)


def gather_all(dp_size, branch_size, array, weights):
    rows, width = array.shape
    n_w = len(weights)
    groups = dp_size // 2
    out_shape = [jax.ShapeDtypeStruct((2 * branch_size * rows, width), BF)]
    out_shape += [jax.ShapeDtypeStruct((dp_size * w.shape[1], w.shape[2]), BF) for w in weights]
    out_shape += [jax.ShapeDtypeStruct((branch_size, dp_size * weights[-1].shape[1], weights[-1].shape[2]), BF)]
    dma = pltpu.SemaphoreType.DMA
    return pl.pallas_call(
        functools.partial(gather_kernel, dp_size, branch_size, n_w),
        out_shape=out_shape,
        in_specs=[pl.BlockSpec(memory_space=pltpu.HBM)] * (1 + n_w),
        out_specs=[pl.BlockSpec(memory_space=pltpu.HBM)] * (2 + n_w),
        scratch_shapes=[
            dma((2, branch_size)),
            dma((branch_size,)),
            dma((branch_size,)),
            dma((branch_size,)),
            dma,
            dma((n_w, 2, groups)),
            dma((n_w, 2, groups)),
            dma((n_w,)),
            dma((n_w,)),
            dma((n_w,)),
            dma((branch_size,)),
            dma((branch_size,)),
            dma,
        ],
        compiler_params=pltpu.CompilerParams(
            collective_id=0, has_side_effects=True, vmem_limit_bytes=GATHER_VMEM
        ),
        cost_estimate=pl.CostEstimate(
            flops=100 * 4 * rows * width * width, bytes_accessed=2 * rows * width, transcendentals=0
        ),
        name="gather_all",
    )(array, *weights)


def scatter_kernel(dp_size, branch_size, *refs):
    n_w = 4
    (h_ref, gm_ref, other_ref, dqkv_ref, dz_ref, o_ref, u_ref, dh_ref, sums_ref) = refs[:9]
    g_refs = refs[9:13]
    tok_out, sum_out, sib_land = refs[13:16]
    slots = refs[16:20]
    got_refs = refs[20:24]
    outs = refs[24:28]
    ins = refs[28:32]
    (own_buf, sib_buf, line_slot, w_send, w_recv, ws_send, ws_recv, z_send, z_recv, s_send, s_recv,
     l_sem, left_buf, x_sem, i_sem, sum_slot, sum_first, sum_got, sum_peer, p_send, p_recv) = refs[32:]
    at = Links(dp_size, branch_size)
    at.meet()
    rows = own_buf.shape[0]
    toks = branch_size * rows
    w_rows = outs[2].shape[2]
    cols = dqkv_ref.shape[2]
    block = left_buf.shape[3]
    lefts = ((gm_ref, other_ref), (h_ref,))
    rights = (u_ref, o_ref, dz_ref, dqkv_ref)
    last = at.groups - 1
    waits = []
    sent = {}

    sib_copy = remote(dh_ref.at[pl.ds(toks, toks)], sib_land, s_send, s_recv, at.sibling)
    sib_copy.start()

    def ring_dest(half, step):
        shift = step + 1 if half == 0 else -step - 1
        return ring_group((at.place - shift + 2 * at.groups) % at.groups)

    def left_copy(a, half, step):
        dest = ring_dest(half, step)
        start = (2 * dest + half) * w_rows if block == w_rows else dest * block
        start = pl.multiple_of(start, block)
        size = left_buf.shape[2] // len(lefts[a])
        return [
            pltpu.make_async_copy(
                ref.at[:, pl.ds(start, block)], left_buf.at[a, half, pl.ds(i * size, size)], x_sem.at[a, half, i]
            )
            for i, ref in enumerate(lefts[a])
        ]

    def product(a, half, w):
        left = left_buf[a, half, :, pl.ds(half * (block - w_rows), w_rows)]

        def dot(right, flip=False):
            pair = (right, left) if flip else (left, right)
            return lax.dot_general(*pair, (((0,), (0,)), ((), ())), preferred_element_type=F32)

        if w < 3:
            return dot(rights[w][...], w < 2)
        return jnp.concatenate([dot(rights[w][c]) for c in range(3)], axis=1)

    def finish(w, values, core):
        if w < 2:
            size = values.shape[0]
            g_refs[w][pl.ds(pl.multiple_of(core * size, size), size), :] = values
        elif w == 2:
            size = values.shape[1]
            g_refs[w][:, pl.ds(pl.multiple_of(core * size, size), size)] = values
        else:
            for c in range(3):
                g_refs[w][c, :, pl.ds(pl.multiple_of(core * cols, cols), cols)] = values[:, c * cols : (c + 1) * cols]

    def ring_piece(a, half, i, step):
        w = 2 * a + i
        if i == 0:
            for load in left_copy(a, half, step):
                load.wait()
        total = product(a, half, w)
        if step > 0:
            slot = slots[w].at[half, step - 1]
            remote(
                slot, slot, w_send.at[w, half, step - 1], w_recv.at[w, half, step - 1], at.ring[half]
            ).wait_recv()
            load = pltpu.make_async_copy(slot, ins[w], i_sem)
            load.start()
            load.wait()
            total = total + ins[w][...].astype(F32)
        if step > 1:
            sent.pop((w, half, step - 2)).wait_send()
        out = outs[w].at[step % 2, half]
        if step < last:
            out[...] = total.astype(BF)
            copy = remote(
                out, slots[w].at[half, step], w_send.at[w, half, step], w_recv.at[w, half, step], at.ring[half]
            )
            copy.start()
            sent[w, half, step] = copy
        else:
            copy = remote(out, got_refs[w], ws_send.at[w], ws_recv.at[w], at.sibling)

            @pl.when(at.core == half)
            def _():
                finish(w, total, at.core)

            @pl.when(at.core != half)
            def _():
                out[...] = total.astype(BF)
                copy.start()

            waits.append(lambda copy=copy, half=half: pl.when(at.core != half)(copy.wait_send))
        if i == 1 and step < last:
            for load in left_copy(a, half, step + 1):
                load.start()

    def sum_step(step):
        for half in range(2):
            total = sums_ref[chunk_rows(ring_dest(half, step), half, 8)]
            if step > 0:
                slot = sum_slot.at[half, step - 1]
                remote(
                    slot, slot, w_send.at[n_w, half, step - 1], w_recv.at[n_w, half, step - 1], at.ring[half]
                ).wait_recv()
                total = total + slot[...]
            out = sum_first.at[step, half]
            out[...] = total
            if step < last:
                copy = remote(
                    out, sum_slot.at[half, step], w_send.at[n_w, half, step], w_recv.at[n_w, half, step], at.ring[half]
                )
                copy.start()
                waits.append(copy.wait_send)
        if step == last:
            copy = remote(sum_first.at[last, at.other], sum_got, ws_send.at[n_w], ws_recv.at[n_w], at.sibling)
            copy.start()
            copy.wait()
            mine = sum_peer.at[0]
            mine[...] = sum_first[last, at.core] + sum_got[...]
            sum_out[at.core] = sum_first[last, at.core]
            sum_out[at.other] = sum_got[...]
            for k in range(1, branch_size):
                copy = remote(mine, sum_peer.at[k], p_send.at[k], p_recv.at[k], at.peers[k - 1])
                copy.start()
                waits.append(copy.wait_send)

    def sum_end():
        total = sum_peer[0]
        for k in range(1, branch_size):
            remote(sum_peer.at[0], sum_peer.at[k], p_send.at[k], p_recv.at[k], at.peers[k - 1]).wait_recv()
            total = total + sum_peer[k]
        sum_out[2] = total

    def load_own(d):
        own = pltpu.make_async_copy(dh_ref.at[pl.ds(d * rows, rows)], own_buf, l_sem.at[0])
        sib = pltpu.make_async_copy(sib_land.at[pl.ds(d * rows, rows)], sib_buf, l_sem.at[1])
        own.start()
        sib.start()
        own.wait()
        sib.wait()

    def line_step(slot_time):
        far = branch_size - 1 - slot_time
        for way in range(2):
            d = at.branch + far if way == 0 else at.branch - far
            going = d < branch_size if way == 0 else d >= 0
            more = at.has_down if way == 0 else at.has_up
            device = at.up if way == 0 else at.down
            slot = line_slot.at[way, d - 1 + way]
            passing = remote(slot, slot, z_send.at[way, d], z_recv.at[way, d], device)

            @pl.when(going)
            def _():
                load_own(d)
                total = own_buf[...].astype(F32) + sib_buf[...].astype(F32)

                @pl.when(more)
                def _():
                    passing.wait_recv()
                    slot[...] = (total + slot[...].astype(F32)).astype(BF)

                @pl.when(jnp.logical_not(more))
                def _():
                    slot[...] = total.astype(BF)

                passing.start()

            waits.append(lambda going=going, passing=passing: pl.when(going)(passing.wait_send))

    def line_end():
        d = at.branch
        load_own(d)
        for way in range(2):
            more = at.has_down if way == 0 else at.has_up
            slot = line_slot.at[way, d - 1 + way]
            device = at.up if way == 0 else at.down

            @pl.when(more)
            def _():
                remote(slot, slot, z_send.at[way, d], z_recv.at[way, d], device).wait_recv()

        below, above = (
            jnp.where(at.has_down, line_slot[0, jnp.maximum(d - 1, 0)].astype(F32), 0.0),
            jnp.where(at.has_up, line_slot[1, jnp.minimum(d, branch_size - 2)].astype(F32), 0.0),
        )
        tok_out[...] = (own_buf[...].astype(F32) + sib_buf[...].astype(F32) + below + above).astype(BF)

    for a in range(2):
        for half in range(2):
            for load in left_copy(a, half, 0):
                load.start()
    sum_step(0)
    pieces = [(a, half, i) for a in range(2) for half in range(2) for i in range(2)]
    size = [rights[2 * a + i].shape[-1] * (1 + a * i * 2) for a, half, i in pieces]
    due = [sum(size[: i + 1]) / sum(size) for i in range(len(pieces))]
    period = 34.0
    events = [(period * (s - 1 + f) + 4.0, 1, (*p, s)) for s in range(1, at.groups) for p, f in zip(pieces, due)]
    events += [(2.0 * i, 1, (*p, 0)) for i, p in enumerate(pieces)]
    events += [(9.0 + 24.0 * k, 0, k) for k in range(branch_size)]
    events += [(10.0 + 12.0 * s, 2, s) for s in range(1, at.groups)]
    events += [(18.0 + 12.0 * at.groups, 3, 0)]
    for _, kind, event in sorted(events, key=lambda e: e[:2]):
        if kind == 0 and event == 0:
            sib_copy.wait_recv()
        if kind == 0 and event == branch_size - 1:
            line_end()
        elif kind == 0:
            line_step(event)
        elif kind == 1:
            ring_piece(*event)
        elif kind == 2:
            sum_step(event)
        else:
            sum_end()
    for w in range(n_w):
        remote(outs[w].at[0, 0], got_refs[w], ws_send.at[w], ws_recv.at[w], at.sibling).wait_recv()
        finish(w, got_refs[w][...].astype(F32), at.other)
    sib_copy.wait_send()
    for copy in sent.values():
        copy.wait_send()
    for wait in waits:
        wait()


def scatter_all(dp_size, branch_size, h, gm, gm_other, dqkv, dz, o, u, dh, sums):
    widths = [u.shape[1], o.shape[1], dz.shape[1], 3 * dqkv.shape[2]]
    width = h.shape[1]
    w_rows = width // dp_size
    groups = dp_size // 2
    toks = h.shape[0] // 2
    rows = toks // branch_size
    n_w = 4
    dma = pltpu.SemaphoreType.DMA
    vm = pl.BlockSpec(memory_space=pltpu.VMEM)
    hb = pl.BlockSpec(memory_space=pltpu.HBM)
    shapes = [(widths[0], w_rows), (widths[1], w_rows), (w_rows, widths[2]), (w_rows, widths[3])]
    out_shape = [
        jax.ShapeDtypeStruct((2 * widths[0], w_rows), F32),
        jax.ShapeDtypeStruct((2 * widths[1], w_rows), F32),
        jax.ShapeDtypeStruct((w_rows, 2 * widths[2]), F32),
        jax.ShapeDtypeStruct((3, w_rows, 2 * dqkv.shape[2]), F32),
    ]
    out_shape += [jax.ShapeDtypeStruct((rows, width), BF), jax.ShapeDtypeStruct((3, 8, 128), F32)]
    out_shape += [jax.ShapeDtypeStruct((toks, width), BF)]
    out_shape += [jax.ShapeDtypeStruct((2, groups - 1) + shape, BF) for shape in shapes]
    out = pl.pallas_call(
        functools.partial(scatter_kernel, dp_size, branch_size),
        out_shape=out_shape,
        in_specs=[hb] * 3 + [vm] * 4 + [hb, vm],
        out_specs=[vm] * 6 + [hb] * 5,
        scratch_shapes=[pltpu.VMEM(shape, BF) for shape in shapes]
        + [pltpu.VMEM((2, 2) + shape, BF) for shape in shapes]
        + [pltpu.VMEM(shape, BF) for shape in shapes]
        + [
            pltpu.VMEM((rows, width), BF),
            pltpu.VMEM((rows, width), BF),
            pltpu.VMEM((2, branch_size - 1, rows, width), BF),
            dma((n_w + 1, 2, groups)),
            dma((n_w + 1, 2, groups)),
            dma((n_w + 1,)),
            dma((n_w + 1,)),
            dma((2, branch_size)),
            dma((2, branch_size)),
            dma(()),
            dma(()),
            dma((2,)),
            pltpu.VMEM((2, 2, 2 * toks, w_rows if w_rows % 128 == 0 else 2 * w_rows), BF),
            dma((2, 2, 2)),
            dma(()),
            pltpu.VMEM((2, groups - 1, 8, 128), F32),
            pltpu.VMEM((groups, 2, 8, 128), F32),
            pltpu.VMEM((8, 128), F32),
            pltpu.VMEM((branch_size, 8, 128), F32),
            dma((branch_size,)),
            dma((branch_size,)),
        ],
        compiler_params=pltpu.CompilerParams(
            collective_id=1, has_side_effects=True, vmem_limit_bytes=VMEM_LIMIT
        ),
        cost_estimate=pl.CostEstimate(
            flops=4 * toks * width * sum(widths), bytes_accessed=2 * toks * width, transcendentals=0
        ),
        name="scatter_all",
    )(h, gm, gm_other, dqkv, dz, o, u, dh, sums)
    return out[:4], out[4], out[5]


def turn(values, tables, sign):
    fixed, from_low, from_high = tables
    half = ROT // 2
    return (
        values * fixed
        + sign * (pltpu.roll(values, half, 1) * from_low + pltpu.roll(values, 2 * HEAD_DIM - half, 1) * from_high)
    )


def score_tile(keys, queries, begins, first, q_tile):
    scores = lax.dot_general(keys, queries, (((1,), (1,)), ((), ())), preferred_element_type=F32)
    key_at = lax.broadcasted_iota(jnp.int32, scores.shape, 0)
    query_at = first + lax.broadcasted_iota(jnp.int32, scores.shape, 1)
    allowed = jnp.logical_and(key_at >= begins, key_at <= query_at)
    return jnp.where(allowed, scores, NEGATIVE)


def attend_kernel(q_tile, q_ref, k_ref, v_ref, begin_ref, fixed_ref, low_ref, high_ref, qr_ref, kr_ref, vr_ref, o_ref, lse_ref):
    tables = (fixed_ref[0], low_ref[0], high_ref[0])
    qr_ref[...] = (turn(q_ref[...], tables, 1.0) * (HEAD_DIM**-0.5)).astype(BF)
    kr_ref[...] = turn(k_ref[...], tables, 1.0).astype(BF)
    vr_ref[...] = v_ref[...].astype(BF)
    toks = q_ref.shape[0]
    for first in range(0, toks, q_tile):
        span = first + q_tile
        begins = begin_ref[0, 0:1, first:span]
        outs = []
        for head in range(2):
            lanes = slice(head * HEAD_DIM, (head + 1) * HEAD_DIM)
            scores = score_tile(kr_ref[:span, lanes], qr_ref[first:span, lanes], begins, first, q_tile)
            top = jnp.max(scores, axis=0, keepdims=True)
            weights = jnp.exp(scores - top)
            total = jnp.sum(weights, axis=0, keepdims=True)
            lse_ref[0, 0, head : head + 1, first:span] = top + jnp.log(total)
            mixed = lax.dot_general(
                vr_ref[:span, lanes], weights.astype(BF), (((0,), (0,)), ((), ())), preferred_element_type=F32
            )
            outs.append(mixed / total)
        o_ref[first:span, :] = jnp.concatenate(outs, axis=0).T.astype(BF)


def attend_back_kernel(
    q_tile, qr_ref, kr_ref, vr_ref, o_ref, do_ref, lse_ref, begin_ref, fixed_ref, low_ref, high_ref, grad_ref, k_acc, v_acc
):
    tables = (fixed_ref[0], low_ref[0], high_ref[0])
    toks = qr_ref.shape[0]
    k_acc[...] = jnp.zeros_like(k_acc)
    v_acc[...] = jnp.zeros_like(v_acc)
    for first in range(0, toks, q_tile):
        span = first + q_tile
        begins = begin_ref[0, 0:1, first:span]
        both = (do_ref[first:span, :].astype(F32) * o_ref[first:span, :].astype(F32)).T
        turned = []
        for head in range(2):
            lanes = slice(head * HEAD_DIM, (head + 1) * HEAD_DIM)
            delta = jnp.sum(both[lanes], axis=0, keepdims=True)
            queries = qr_ref[first:span, lanes]
            grads = do_ref[first:span, lanes]
            keys = kr_ref[:span, lanes]
            scores = score_tile(keys, queries, begins, first, q_tile)
            prob = jnp.exp(scores - lse_ref[0, 0, head : head + 1, first:span])
            v_acc[head, :span, :] += jnp.dot(prob.astype(BF), grads, preferred_element_type=F32)
            dprob = lax.dot_general(
                vr_ref[:span, lanes], grads, (((1,), (1,)), ((), ())), preferred_element_type=F32
            )
            ds = (prob * (dprob - delta)).astype(BF)
            k_acc[head, :span, :] += jnp.dot(ds, queries, preferred_element_type=F32)
            turned.append(
                lax.dot_general(keys, ds, (((0,), (0,)), ((), ())), preferred_element_type=F32)
            )
        dq = jnp.concatenate(turned, axis=0).T * (HEAD_DIM**-0.5)
        grad_ref[0, first:span, :] = turn(dq, tuple(t[first:span] for t in tables), -1.0).astype(BF)
    dk = jnp.concatenate([k_acc[0], k_acc[1]], axis=1)
    grad_ref[1] = turn(dk, tables, -1.0).astype(BF)
    grad_ref[2] = jnp.concatenate([v_acc[0], v_acc[1]], axis=1).astype(BF)


def attention_specs(toks, pairs):
    wide = 2 * HEAD_DIM

    def cols(shift):
        return pl.BlockSpec((toks, wide), lambda i, j: (i, j + shift * pairs))

    begin = pl.BlockSpec((1, 8, toks), lambda i, j: (i, 0, 0))
    table = pl.BlockSpec((1, toks, wide), lambda i, j: (i, 0, 0))
    lse = pl.BlockSpec((1, 1, 2, toks), lambda i, j: (i, j, 0, 0))
    return cols, begin, table, lse


def attend(project, begins, tables):
    blocks, _, toks = begins.shape
    pairs = project.shape[1] // (6 * HEAD_DIM)
    cols, begin, table, lse = attention_specs(toks, pairs)
    narrow = jax.ShapeDtypeStruct((blocks * toks, pairs * 2 * HEAD_DIM), BF)
    return pl.pallas_call(
        functools.partial(attend_kernel, min(256, toks)),
        grid=(blocks, pairs),
        in_specs=[cols(0), cols(1), cols(2), begin] + [table] * 3,
        out_specs=[cols(0)] * 4 + [lse],
        out_shape=[narrow] * 4 + [jax.ShapeDtypeStruct((blocks, pairs, 2, toks), F32)],
        compiler_params=pltpu.CompilerParams(vmem_limit_bytes=60 * 2**20),
        name="attend",
    )(project, project, project, begins, *tables)


def attend_back(queries, keys, values, o, do, lse_rows, begins, tables):
    blocks, _, toks = begins.shape
    pairs = queries.shape[1] // (2 * HEAD_DIM)
    cols, begin, table, lse = attention_specs(toks, pairs)
    acc = pltpu.VMEM((2, toks, HEAD_DIM), F32)
    return pl.pallas_call(
        functools.partial(attend_back_kernel, min(256, toks)),
        grid=(blocks, pairs),
        in_specs=[cols(0)] * 5 + [lse, begin] + [table] * 3,
        out_specs=pl.BlockSpec((3, toks, 2 * HEAD_DIM), lambda i, j: (0, i, j)),
        out_shape=jax.ShapeDtypeStruct((3,) + queries.shape, BF),
        scratch_shapes=[acc, acc],
        compiler_params=pltpu.CompilerParams(vmem_limit_bytes=60 * 2**20),
        name="attend_back",
    )(queries, keys, values, o, do, lse_rows, begins, *tables)


def rotary_tables(doc_rows):
    row_count = doc_rows.shape[0]
    row_index = jnp.arange(row_count, dtype=jnp.int32)
    same = doc_rows[:, None] == doc_rows[None, :]
    begins = jnp.min(jnp.where(same, row_index[:, None], row_count), axis=0)
    places = (row_index - begins).astype(F32)
    half = ROT // 2
    lane = np.arange(2 * HEAD_DIM) % HEAD_DIM
    turning = lane < ROT
    frequency = np.where(turning, 10000.0 ** (-2.0 * (lane % half) / ROT), 0.0).astype(np.float32)
    angles = places[:, None] * frequency[None, :]
    sine = jnp.sin(angles)
    from_low = sine * np.where(turning & (lane >= half), 1.0, 0.0).astype(np.float32)
    from_high = sine * np.where(lane < half, -1.0, 0.0).astype(np.float32)
    return jnp.broadcast_to(begins[None], (8, row_count)), (jnp.cos(angles), from_low, from_high)


def dot_nt(left, right):
    return lax.dot_general(left, right, (((1,), (1,)), ((), ())), preferred_element_type=F32)


def standardized(rows):
    xfloat = rows.astype(F32)
    removed = xfloat - jnp.mean(xfloat, axis=-1, keepdims=True)
    inverse = lax.rsqrt(jnp.mean(removed * removed, axis=-1, keepdims=True) + NORM_EPS)
    return removed * inverse, inverse


def enter_kernel(
    dp_size, branch_size, tok_ref, gain_ref, shift_ref, wq_ref, qb_ref, wu_ref, ub_ref, part_ref,
    h_ref, project_ref, u_ref, slope_ref, full_ref, *sems,
):
    tile_at, tiles = pl.program_id(0), pl.num_programs(0)
    at = Links(dp_size, branch_size)
    ring = WeightRing(at, [part_ref], [full_ref], sems)

    @pl.when(tile_at == 0)
    def _():
        at.meet()
        ring.share()
        ring.shared()
        ring.step(0, 0)

    pl.when(tile_at == FIRST_HOP)(lambda: ring.step(0, 1))

    h = (standardized(tok_ref[...])[0] * gain_ref[0:1] + shift_ref[0:1]).astype(BF)
    h_ref[...] = h
    project_ref[...] = jnp.dot(h, wq_ref[...], preferred_element_type=F32) + qb_ref[0:1]
    z = jnp.dot(h, wu_ref[...], preferred_element_type=F32) + ub_ref[0:1]
    if at.groups > 2:
        pl.when(tile_at == tiles - 1)(lambda: ring.step(0, 2))

    scale, cubic = math.sqrt(2.0 / math.pi), 0.044715
    square = z * z
    bent = jnp.tanh(scale * z * (1.0 + cubic * square))
    half = 0.5 * (1.0 + bent)
    u_ref[...] = (z * half).astype(BF)
    slope = half + 0.5 * z * (1.0 - bent * bent) * (scale * (1.0 + 3.0 * cubic * square))
    slope_ref[...] = slope.astype(BF)

    @pl.when(tile_at == tiles - 1)
    def _():
        for step in range(3, at.groups):
            ring.step(0, step)
        ring.drain()


def enter(dp_size, branch_size, tok_all, gain, shift, wqkv, qkv_b, wup, up_b, part):
    total, width = tok_all.shape
    groups = dp_size // 2
    tile = ROW_TILE
    dma = pltpu.SemaphoreType.DMA

    def spec(width):
        return pl.BlockSpec((tile, width), lambda i: (i, 0))

    whole = (gain, shift, wqkv, qkv_b, wup, up_b)
    outs = [(width, BF), (wqkv.shape[1], F32), (wup.shape[1], BF), (wup.shape[1], BF)]
    far = pl.BlockSpec(memory_space=pltpu.HBM)
    return pl.pallas_call(
        functools.partial(enter_kernel, dp_size, branch_size),
        grid=(total // tile,),
        in_specs=[spec(width)] + [pl.BlockSpec(x.shape, lambda i: (0, 0)) for x in whole] + [far],
        out_specs=[spec(w) for w, _ in outs] + [far],
        out_shape=[jax.ShapeDtypeStruct((total, w), t) for w, t in outs]
        + [jax.ShapeDtypeStruct((dp_size * part.shape[1], part.shape[2]), BF)],
        scratch_shapes=[dma((1, 2, groups)), dma((1, 2, groups)), dma((1,)), dma((1,)), dma((1,))],
        compiler_params=pltpu.CompilerParams(
            collective_id=2, has_side_effects=True, vmem_limit_bytes=ENTER_VMEM
        ),
        cost_estimate=pl.CostEstimate(
            flops=2 * total * (wqkv.size + wup.size), bytes_accessed=2 * total * width, transcendentals=0
        ),
        name="enter",
    )(tok_all, *whole, part)


def branch_kernel(o_ref, u_ref, *refs):
    more, (wo_ref, wd_ref, br_ref) = refs[:-3], refs[-3:]
    total = dot_nt(o_ref[...], wo_ref[...]) + dot_nt(u_ref[...], wd_ref[...])
    for ref in more:
        total = total + ref[...].astype(F32)
    br_ref[...] = total.astype(BF)


def grad_kernel(gm_ref, other_ref, slope_ref, wo_ref, wd_ref, do_ref, dz_ref, sum_ref):
    step = pl.program_id(0)

    @pl.when(step == 0)
    def _():
        sum_ref[...] = jnp.zeros_like(sum_ref)

    def use(rows_ref):
        gm = rows_ref[...]
        do_ref[...] = jnp.dot(gm, wo_ref[...], preferred_element_type=F32).astype(BF)
        dz = jnp.dot(gm, wd_ref[...], preferred_element_type=F32) * slope_ref[...].astype(F32)
        dz = dz.astype(BF)
        dz_ref[...] = dz
        sum_ref[0:1] += jnp.sum(dz.astype(F32), axis=0, keepdims=True)

    own = step < pl.num_programs(0) // 2
    pl.when(own)(lambda: use(gm_ref))
    pl.when(jnp.logical_not(own))(lambda: use(other_ref))


def leave_kernel(tok_ref, grad_ref, dz_ref, wq_ref, wu_ref, dh_ref, sum_ref, q_sum_ref):
    @pl.when(pl.program_id(0) == 0)
    def _():
        sum_ref[...] = jnp.zeros_like(sum_ref)
        q_sum_ref[...] = jnp.zeros_like(q_sum_ref)

    cols = grad_ref.shape[2]
    grads = jnp.concatenate([grad_ref[c] for c in range(3)], axis=1)
    dh = dot_nt(dz_ref[...], wu_ref[...]) + dot_nt(grads, wq_ref[...])
    dh_ref[...] = dh.astype(BF)
    xhat = standardized(tok_ref[...])[0]
    sum_ref[0:1] += jnp.sum(dh * xhat, axis=0, keepdims=True)
    sum_ref[1:2] += jnp.sum(dh, axis=0, keepdims=True)
    q_sum_ref[0:1] += jnp.sum(grads.astype(F32), axis=0, keepdims=True)


def row_call(kernel, name, tiles, tiled, whole, outs, sums):
    tile = ROW_TILE

    def spec(width):
        return pl.BlockSpec((tile, width), lambda i: (i, 0))

    in_specs = [s if s is not None else spec(x.shape[1]) for x, s in tiled]
    in_specs += [pl.BlockSpec(x.shape, lambda i: (0, 0)) for x in whole]
    flops = 2 * tiles * tile * sum(x.size for x in whole)
    traffic = 2 * sum(x.size for x in whole) + 2 * sum(x.size for x, _ in tiled) + 4 * tiles * tile * sum(w for w, _ in outs)
    return pl.pallas_call(
        kernel,
        grid=(tiles,),
        in_specs=in_specs,
        out_specs=[spec(w) for w, _ in outs] + [pl.BlockSpec((8, w), lambda i: (0, 0)) for w in sums],
        out_shape=[jax.ShapeDtypeStruct((tiles * tile, w), t) for w, t in outs]
        + [jax.ShapeDtypeStruct((8, w), F32) for w in sums],
        compiler_params=pltpu.CompilerParams(vmem_limit_bytes=60 * 2**20),
        cost_estimate=pl.CostEstimate(flops=flops, bytes_accessed=traffic, transcendentals=0),
        name=name,
    )(*[x for x, _ in tiled], *whole)


def local(
    dp_size, branch_size, tokens, doc_ids, real_rows, cotangent, norm_gain, norm_shift, out_bias,
    w_qkv, b_qkv, w_out, w_up, b_up, w_down,
):
    dp = lax.axis_index("dp")
    branch = lax.axis_index("branch")
    core = dp % 2
    my_rows, width = tokens.shape
    toks = doc_ids.shape[0]
    w_rows = w_qkv.shape[1]
    cols = w_qkv.shape[2] // 2
    hid = w_up.shape[1] // 2
    heads = cols // HEAD_DIM

    my_real = lax.dynamic_slice_in_dim(real_rows, branch * my_rows, my_rows).astype(F32)
    masked_cot = (cotangent.astype(F32) * my_real[:, None]).astype(BF)
    qkv_l = w_qkv.astype(BF).reshape(3, w_rows, 2, cols).transpose(2, 1, 0, 3).reshape(2, w_rows, 3 * cols)
    up_l = w_up.astype(BF).reshape(w_rows, 2, hid).transpose(1, 0, 2)
    out_l = w_out.astype(BF).T.reshape(w_rows, 2, cols).transpose(1, 0, 2)
    down_l = w_down.astype(BF).T.reshape(w_rows, 2, hid).transpose(1, 0, 2)

    small = jnp.concatenate([v.reshape(-1) for v in (norm_gain, norm_shift, out_bias, b_qkv, b_up)]).astype(BF)
    small = jnp.pad(small, (0, -small.size % 128))
    small = jnp.broadcast_to(small[None, None], (2, 16, small.size))

    tok_all, wqkv, wup, wot, _, params = gather_all(
        dp_size, branch_size, tokens, (qkv_l, up_l, out_l, small)
    )
    swap = [(i, i + 1 - 2 * (i % 2)) for i in range(dp_size)]
    late_cot, tok_all = lax.optimization_barrier((masked_cot, tok_all))
    gm_own = lax.all_gather(late_cot, "branch", axis=0, tiled=True)
    params = params.reshape(branch_size, dp_size, 16, -1)[:, :, 0].astype(F32)
    sizes = [norm_gain.size, norm_shift.size, out_bias.size, b_qkv.size, b_up.size]
    stops = [sum(sizes[: i + 1]) for i in range(5)]
    gain, shift, bias_full = (
        params[:, :, stops[i] - sizes[i] : stops[i]].transpose(1, 0, 2).reshape(width) for i in range(3)
    )
    mine = lax.dynamic_index_in_dim(params, branch, 0, keepdims=False)
    qkv_b = mine[:, stops[2] : stops[3]].reshape((dp_size,) + b_qkv.shape).transpose(1, 2, 0, 3)
    qkv_b = qkv_b.reshape(3, 2, cols)
    qkv_b = lax.dynamic_index_in_dim(qkv_b, core, 1, keepdims=False).reshape(3 * cols)
    up_b = mine[:, stops[3] : stops[4]].reshape((dp_size,) + b_up.shape).transpose(1, 0, 2).reshape(2, hid)
    up_b = lax.dynamic_index_in_dim(up_b, core, 0, keepdims=False)
    ids = jnp.stack([doc_ids, lax.ppermute(doc_ids, "dp", swap)])

    def row(values):
        return jnp.broadcast_to(values[None], (8, values.size))

    tiles = 2 * toks // ROW_TILE
    h, project, u, slope, wdt = enter(
        dp_size, branch_size, tok_all, row(gain), row(shift), wqkv, row(qkv_b), wup, row(up_b), down_l
    )
    found = [rotary_tables(ids[i]) for i in range(2)]
    begins = jnp.stack([t[0] for t in found])
    tables = [jnp.stack([t[1][i] for t in found]) for i in range(3)]
    queries, keys, values, o, lse_rows = attend(project, begins, tables)
    gm_own, _ = lax.optimization_barrier((gm_own, o))
    gm_other = lax.ppermute(gm_own, "dp", swap)
    half_tiles = tiles // 2

    def branch_out(first, *more):
        def later(width):
            return pl.BlockSpec((ROW_TILE, width), lambda i: (i + first, 0))

        tiled = [(o, later(cols)), (u, later(hid))] + [(x, None) for x in more]
        return row_call(branch_kernel, "branch_out", half_tiles, tiled, [wot, wdt], [(width, BF)], [])[0]

    given = lax.ppermute(branch_out(half_tiles), "dp", swap)
    xfloat = tokens.astype(F32)

    near = pl.BlockSpec((ROW_TILE, width), lambda i: (jnp.minimum(i, half_tiles - 1), 0))
    far = pl.BlockSpec((ROW_TILE, width), lambda i: (jnp.maximum(i - half_tiles, 0), 0))
    do, dz, up_sums = row_call(
        grad_kernel, "branch_grad", tiles, [(gm_own, near), (gm_other, far), (slope, None)], [wot, wdt],
        [(cols, BF), (hid, BF)], [hid],
    )
    do, given = lax.optimization_barrier((do, given))
    br = branch_out(0, given)
    do, br = lax.optimization_barrier((do, br))
    summed = lax.psum_scatter(br, "branch", scatter_dimension=0, tiled=True).astype(F32)
    dqkv = attend_back(queries, keys, values, o, do, lse_rows, begins, tables)
    three = pl.BlockSpec((3, ROW_TILE, cols), lambda i: (0, i, 0))
    dh, token_sums, q_sums = row_call(
        leave_kernel, "leave", tiles, [(tok_all, None), (dqkv, three), (dz, None)], [wqkv, wup],
        [(width, BF)], [width, 3 * cols],
    )

    part = norm_gain.shape[0]
    vectors = jnp.stack(
        [token_sums[0], token_sums[1], jnp.sum(masked_cot, axis=0, dtype=F32)]
    )
    vectors = vectors.reshape(3, dp_size, branch_size * part).transpose(1, 0, 2).reshape(dp_size, -1)
    q_sum = q_sums[0].reshape(3, heads, dp_size, -1).transpose(2, 0, 1, 3).reshape(dp_size, -1)
    u_sum = up_sums[0].reshape(b_up.shape[0] // 2, dp_size, -1).transpose(1, 0, 2)
    u_sum = u_sum.reshape(dp_size, -1)
    sums = jnp.concatenate([vectors, q_sum, u_sum], axis=1)
    ends = (vectors.shape[1], vectors.shape[1] + q_sum.shape[1], sums.shape[1])
    sums = jnp.pad(sums, ((0, 0), (0, 1024 - sums.shape[1]))).reshape(8 * dp_size, 128)

    (g_down, g_out, g_up, g_qkv), dh_mine, total = scatter_all(
        dp_size, branch_size, h, gm_own, gm_other, dqkv, dz, o, u, dh, sums
    )
    dh_mine = dh_mine.astype(F32)
    total = total.reshape(3, 1024)
    block_out = (xfloat + my_real[:, None] * (summed + bias_full)).astype(BF)
    xhat, inverse = standardized(tokens)
    scaled = dh_mine * gain
    input_grad = inverse * (
        scaled
        - jnp.mean(scaled, axis=-1, keepdims=True)
        - xhat * jnp.mean(scaled * xhat, axis=-1, keepdims=True)
    )
    tokens_grad = (cotangent.astype(F32) + input_grad).astype(BF)

    gain_g, shift_g, bias_g = lax.dynamic_slice_in_dim(
        total[2, : ends[0]].reshape(3, branch_size * part), branch * part, part, axis=1
    )
    b_q = total[:2, ends[0] : ends[1]].reshape(2, 3, heads, -1).transpose(1, 0, 2, 3).reshape(b_qkv.shape)
    b_u = total[:2, ends[1] : ends[2]].reshape(b_up.shape)
    return (block_out, tokens_grad, gain_g, shift_g, bias_g, g_qkv, b_q, g_out, g_up, b_u, g_down)


def solution(mesh):
    in_specs = (
        P(("dp", "branch"), None),
        P("dp"),
        P("dp"),
        P(("dp", "branch"), None),
        P(("dp", "branch")),
        P(("dp", "branch")),
        P(("dp", "branch")),
        P(None, "dp", "branch"),
        P(None, "branch", "dp"),
        P("branch", "dp"),
        P("dp", "branch"),
        P("branch", "dp"),
        P("branch", "dp"),
    )
    out_specs = (
        P(("dp", "branch"), None),
        P(("dp", "branch"), None),
        P(("dp", "branch")),
        P(("dp", "branch")),
        P(("dp", "branch")),
        P(None, "dp", "branch"),
        P(None, "branch", "dp"),
        P("branch", "dp"),
        P("dp", "branch"),
        P("branch", "dp"),
        P("branch", "dp"),
    )
    body = functools.partial(local, mesh.shape["dp"], mesh.shape["branch"])
    return jax.shard_map(body, mesh=mesh, in_specs=in_specs, out_specs=out_specs, check_vma=False)
```
